32 devices in a mesh: dp: 8 (over z, core), mp: 4 (over y, x).
Axes of the slice: x: 2, y: 2, z: 4, core: 2. Of those that a mesh axis runs over, the one named last changes fastest.
Arguments:
- tokens: bfloat16 [8192, 2048], P(('dp', 'mp')), may hold values from -6 to 6
- ln_gain: float32 [2048], replicated, may hold values from 0.1 to 1.9
- ln_bias: float32 [2048], replicated, may hold values from -4 to 4
- qkv_weight: float32 [2048, 3, 2048], P('dp', None, 'mp'), may hold values from -0.125 to 0.125
- qkv_bias: float32 [3, 2048], P(None, 'mp'), may hold values from -1.5 to 1.5
- dense_weight: float32 [2048, 2048], P('dp', 'mp'), may hold values from -1 to 1
- dense_bias: float32 [2048], replicated, may hold values from -4 to 4
- fc1_weight: float32 [2048, 8192], P('dp', 'mp'), may hold values from -0.125 to 0.125
- fc1_bias: float32 [8192], P('mp'), may hold values from -6 to 6
- fc2_weight: float32 [2048, 8192], P('dp', 'mp'), may hold values from -0.0625 to 0.0625
- fc2_bias: float32 [2048], replicated, may hold values from -4 to 4
- starts: int32 [8], P('dp'), may hold values from 0 to 768
- cotangent: bfloat16 [8192, 2048], P(('dp', 'mp')), may hold values from -18 to 18
Outputs:
- output: bfloat16 [8192, 2048], P(('dp', 'mp'))
- input_grad: bfloat16 [8192, 2048], P(('dp', 'mp'))
- ln_gain_grad: float32 [2048], replicated
- ln_bias_grad: float32 [2048], replicated
- qkv_weight_grad: float32 [2048, 3, 2048], P('dp', None, 'mp')
- qkv_bias_grad: float32 [3, 2048], P(None, 'mp')
- dense_weight_grad: float32 [2048, 2048], P('dp', 'mp')
- dense_bias_grad: float32 [2048], replicated
- fc1_weight_grad: float32 [2048, 8192], P('dp', 'mp')
- fc1_bias_grad: float32 [8192], P('mp')
- fc2_weight_grad: float32 [2048, 8192], P('dp', 'mp')
- fc2_bias_grad: float32 [2048], replicated
The draws below stay inside these ranges and needn't reach their ends.
Inputs may be any that keep to these rules, and one draw needn't show every extreme that they name: Each sequence holds one picture piece of 256 tokens that begins at its entry of starts.
All inputs are finite; a program needn't handle non-finite values.
Results may differ from the reference program's by a relative error of at most 0.012.
The reference program's roundings to bfloat16 on the way count: a program that leaves them out, or rounds other values in their place, can miss the bound.
Values may be sent and summed in bfloat16 or wider, within the bound.
A program may use at most 320 MiB of HBM per device.

```python
from functools import partial
import jax
import jax.numpy as jnp
from jax import lax

D = 2048
HEADS = 32
HEAD_DIM = 64
ROT_DIM = 32
FF = 8192
LENGTH = 1024
PIECE = 256
SEQS = 8
TOKENS = 8192


def draw_cotangent(key, part):
    rising = 1.0 + 2.0 * jnp.arange(TOKENS).astype(jnp.float32) / max(TOKENS - 1, 1)
    sample = jnp.clip(jax.random.normal(key, (TOKENS, D), jnp.float32), -6.0, 6.0)
    return (sample * rising[:, None]).astype(jnp.bfloat16)


def with_ends(drawn, own_key, least, high):
    extent = drawn.shape
    place = [jax.random.randint(jax.random.fold_in(own_key, axis), (), 0, extent[axis]) for axis in range(len(extent))]
    drawn = drawn.at[tuple(place)].set(least)
    longest = extent.index(max(extent))
    place[longest] = (place[longest] + 1) % extent[longest]
    return drawn.at[tuple(place)].set(high)


def level_of(stream_key, shape, split, least, largest):
    gain, own = 1.0, jax.random.fold_in(stream_key, 6)
    for position, blocks in split:
        heights = jnp.exp(jax.random.uniform(jax.random.fold_in(own, position), (blocks,), jnp.float32, least / len(split), largest / len(split)))
        gain = gain * jnp.repeat(heights, shape[position] // blocks).reshape([-1 if axis == position else 1 for axis in range(len(shape))])
    return gain


def scatter_about(rng, dims, deviation, bound, shards=(), kind=jnp.bfloat16):
    values = jax.random.normal(rng, dims, jnp.float32) * deviation
    if len(shards) > 0:
        values = level_of(rng, dims, shards, -0.22, 0.18) * values
    return jnp.clip(values, min=-bound, max=bound).astype(kind)


def setup_inputs(seed: int = 0) -> dict:
    keys = jax.random.split(jax.random.key(seed), 14)
    return {
        "tokens": scatter_about(keys[0], (TOKENS, D), 1.0, 6.0, ((0, 32),)),
        "ln_gain": jnp.clip(1.0 + 0.18 * jax.random.normal(keys[1], (D,), jnp.float32), 0.1, 1.9),
        "ln_bias": scatter_about(keys[2], (D,), 0.3, 4.0, (), jnp.float32),
        "qkv_weight": scatter_about(keys[3], (D, 3, D), D ** -0.5, 0.125, ((0, 8), (2, 4)), jnp.float32),
        "qkv_bias": scatter_about(keys[4], (3, D), 0.1, 1.5, ((1, 4),), jnp.float32),
        "dense_weight": scatter_about(keys[5], (D, D), (D // 64) ** -0.5, 1.0, ((0, 8), (1, 4)), jnp.float32),
        "dense_bias": scatter_about(keys[6], (D,), 0.3, 4.0, (), jnp.float32),
        "fc1_weight": scatter_about(keys[7], (D, FF), D ** -0.5, 0.125, ((0, 8), (1, 4)), jnp.float32),
        "fc1_bias": scatter_about(keys[8], (FF,), 0.5, 6.0, ((0, 4),), jnp.float32),
        "fc2_weight": scatter_about(keys[9], (D, FF), FF ** -0.5, 0.0625, ((0, 8), (1, 4)), jnp.float32),
        "fc2_bias": scatter_about(keys[10], (D,), 0.3, 4.0, (), jnp.float32),
        "starts": with_ends(jax.random.randint(keys[11], (SEQS,), 0, LENGTH - PIECE + 1), jax.random.fold_in(keys[11], 1), 0, LENGTH - PIECE).astype(jnp.int32),
        "cotangent": draw_cotangent(jax.random.fold_in(keys[13], 71), 0),
    }


EPSILON = 1e-05
NEGATIVE = -1e+30

@jax.custom_vjp
def low(v):
    return lax.optimization_barrier(v.astype(jnp.bfloat16)).astype(jnp.float32)

@jax.custom_vjp
def low_back(v):
    return v

def low_keep(v):
    return (low(v), None)

def low_pass(kept, grad):
    return (grad,)

def back_keep(v):
    return (v, None)

def back_low(kept, grad):
    return (low(grad),)
low.defvjp(low_keep, low_pass)
low_back.defvjp(back_keep, back_low)

def normalize(values, gain_vec, shift_vec):
    centre = values - lax.optimization_barrier(jnp.mean(values, axis=-1, keepdims=True))
    spread = lax.optimization_barrier(jnp.mean(centre * centre, axis=-1, keepdims=True))
    scaled = centre * lax.rsqrt(spread + EPSILON)
    return scaled * gain_vec + shift_vec

def rotary_tables(row_count):
    half_dim = ROT_DIM // 2
    places = (jnp.arange(row_count) % LENGTH).astype(jnp.float32)
    frequency = 10000.0 ** (-jnp.arange(half_dim).astype(jnp.float32) * 2.0 / ROT_DIM)
    angles = places[:, None] * frequency[None, :]
    return (jnp.cos(angles), jnp.sin(angles))

def rotate(values, cosine_table, sine_table):
    half_dim = ROT_DIM // 2
    first_part = values[..., :half_dim]
    second_part = values[..., half_dim:ROT_DIM]
    cosine_row = cosine_table[:, None, :]
    sine_row = sine_table[:, None, :]
    return jnp.concatenate([first_part * cosine_row - second_part * sine_row, second_part * cosine_row + first_part * sine_row, values[..., ROT_DIM:]], axis=-1)

def allowed_mask(piece_start):
    places = jnp.arange(LENGTH)
    inside = (places >= piece_start) & (places < piece_start + PIECE)
    return (places[None, :] <= places[:, None]) | inside[:, None] & inside[None, :]

def attend_sequence(members):
    queries, key_rows, values_in, piece_start = members
    score_scale = HEAD_DIM ** (-0.5)
    scores = low_back(jnp.einsum('qhd,khd->hqk', queries, key_rows, precision=lax.Precision.HIGHEST) * score_scale)
    masked = jnp.where(allowed_mask(piece_start)[None], scores, NEGATIVE)
    prob_values = low(jax.nn.softmax(masked, axis=-1))
    return jnp.einsum('hqk,khd->qhd', prob_values, values_in, precision=lax.Precision.HIGHEST)

def forward(tokens_f, ln_gain, ln_bias, qkv_weight, qkv_bias, dense_weight, dense_bias, fc1_weight, fc1_bias, fc2_weight, fc2_bias, starts):
    highest = lax.Precision.HIGHEST
    row_count = tokens_f.shape[0]
    normed = low(normalize(tokens_f, ln_gain, ln_bias))
    projected = low_back(jnp.dot(normed, low(qkv_weight).reshape(D, 3 * D), precision=highest) + qkv_bias.reshape(3 * D))
    cosine_table, sine_table = rotary_tables(row_count)
    queries = low(rotate(projected[:, :D].reshape(row_count, HEADS, HEAD_DIM), cosine_table, sine_table))
    key_rows = low(rotate(projected[:, D:2 * D].reshape(row_count, HEADS, HEAD_DIM), cosine_table, sine_table))
    values_in = low(projected[:, 2 * D:].reshape(row_count, HEADS, HEAD_DIM))
    shape_seq = (SEQS, LENGTH, HEADS, HEAD_DIM)
    attended = lax.map(jax.checkpoint(attend_sequence), (queries.reshape(shape_seq), key_rows.reshape(shape_seq), values_in.reshape(shape_seq), starts))
    attended = low(low_back(attended.reshape(row_count, D)))
    attn_part = jnp.dot(attended, low(dense_weight).T, precision=highest)
    hidden_pre = low_back(jnp.dot(normed, low(fc1_weight), precision=highest) + fc1_bias)
    hidden = low(jax.nn.gelu(hidden_pre, approximate=True))
    mlp_part = jnp.dot(hidden, low(fc2_weight).T, precision=highest)
    return tokens_f + attn_part + mlp_part + dense_bias + fc2_bias

def reference(tokens, ln_gain, ln_bias, qkv_weight, qkv_bias, dense_weight, dense_bias, fc1_weight, fc1_bias, fc2_weight, fc2_bias, starts, cotangent):
    tokens_f = tokens.astype(jnp.float32)
    result, pullback = jax.vjp(partial(forward, starts=starts), tokens_f, ln_gain, ln_bias, qkv_weight, qkv_bias, dense_weight, dense_bias, fc1_weight, fc1_bias, fc2_weight, fc2_bias)
    gradients = pullback(cotangent.astype(jnp.float32))
    return (result.astype(jnp.bfloat16), gradients[0].astype(jnp.bfloat16), gradients[1], gradients[2], gradients[3], gradients[4], gradients[5], gradients[6], gradients[7], gradients[8], gradients[9], gradients[10])
```

```python
from functools import partial

import jax
import jax.numpy as jnp
from jax import lax
from jax.sharding import PartitionSpec as P

HEAD_DIM = 64
ROT_DIM = 32
LENGTH = 1024
PIECE = 256


EPSILON = 1e-05
NEGATIVE = -1e30


def normalize(values, gain_vec, shift_vec):
    centre = values - jnp.mean(values, axis=-1, keepdims=True)
    spread = jnp.mean(centre * centre, axis=-1, keepdims=True)
    scaled = centre * lax.rsqrt(spread + EPSILON)
    return scaled * gain_vec + shift_vec


def rotary_tables(row_count):
    half_dim = ROT_DIM // 2
    places = (jnp.arange(row_count) % LENGTH).astype(jnp.float32)
    frequency = 10000.0 ** (-jnp.arange(half_dim).astype(jnp.float32) * 2.0 / ROT_DIM)
    angles = places[:, None] * frequency[None, :]
    return (jnp.cos(angles), jnp.sin(angles))


def rotate(values, cosine_table, sine_table):
    half_dim = ROT_DIM // 2
    first_part = values[..., :half_dim]
    second_part = values[..., half_dim:ROT_DIM]
    cosine_row = cosine_table[:, None, :]
    sine_row = sine_table[:, None, :]
    return jnp.concatenate(
        [
            first_part * cosine_row - second_part * sine_row,
            second_part * cosine_row + first_part * sine_row,
            values[..., ROT_DIM:],
        ],
        axis=-1,
    )


def unrotate(gradient, cosine_table, sine_table):
    half_dim = ROT_DIM // 2
    first_part = gradient[..., :half_dim]
    second_part = gradient[..., half_dim:ROT_DIM]
    cosine_row = cosine_table[:, None, :]
    sine_row = sine_table[:, None, :]
    return jnp.concatenate(
        [
            first_part * cosine_row + second_part * sine_row,
            second_part * cosine_row - first_part * sine_row,
            gradient[..., ROT_DIM:],
        ],
        axis=-1,
    )


def allowed_mask(piece_start):
    places = jnp.arange(LENGTH)
    inside = (places >= piece_start) & (places < piece_start + PIECE)
    return (places[None, :] <= places[:, None]) | inside[:, None] & inside[None, :]


def masked_scores(queries, key_rows, piece_start):
    scores = jnp.einsum(
        "qhd,khd->hqk", queries, key_rows, preferred_element_type=jnp.float32
    ) * HEAD_DIM ** (-0.5)
    return jnp.where(allowed_mask(piece_start)[None], scores, NEGATIVE)


def attend_forward(members):
    queries, key_rows, values_in, piece_start = members
    masked = masked_scores(queries, key_rows, piece_start)
    row_max = jnp.max(masked, axis=-1, keepdims=True)
    expo_values = jnp.exp(masked - row_max)
    row_total = jnp.sum(expo_values, axis=-1, keepdims=True)
    prob_low = (expo_values / row_total).astype(jnp.bfloat16)
    attended = jnp.einsum("hqk,khd->qhd", prob_low, values_in, preferred_element_type=jnp.float32)
    return (attended.astype(jnp.bfloat16), (row_max + jnp.log(row_total))[..., 0])


def attend_backward(members):
    queries, key_rows, values_in, piece_start, logsum, out_grad = members
    masked = masked_scores(queries, key_rows, piece_start)
    prob_values = jnp.exp(masked - logsum[..., None])
    prob_low = prob_values.astype(jnp.bfloat16)
    value_grad = jnp.einsum("hqk,qhd->khd", prob_low, out_grad, preferred_element_type=jnp.float32)
    prob_grad = jnp.einsum("qhd,khd->hqk", out_grad, values_in, preferred_element_type=jnp.float32)
    inner_sum = jnp.sum(prob_values * prob_grad, axis=-1, keepdims=True)
    score_grad = (prob_values * (prob_grad - inner_sum)).astype(jnp.bfloat16)
    query_grad = jnp.einsum(
        "hqk,khd->qhd", score_grad, key_rows, preferred_element_type=jnp.float32
    ) * HEAD_DIM ** (-0.5)
    key_grad = jnp.einsum(
        "hqk,qhd->khd", score_grad, queries, preferred_element_type=jnp.float32
    ) * HEAD_DIM ** (-0.5)
    return (query_grad, key_grad, value_grad)


def right_product(left_side, right_side):
    return lax.dot_general(
        left_side, right_side, (((1,), (1,)), ((), ())), preferred_element_type=jnp.float32
    )


def rows_product(left_side, right_side):
    return lax.dot_general(
        left_side, right_side, (((0,), (0,)), ((), ())), preferred_element_type=jnp.float32
    )


def low_scatter(partial_sums, axis):
    return lax.psum_scatter(
        partial_sums.astype(jnp.bfloat16), axis, scatter_dimension=0, tiled=True
    ).astype(jnp.float32)


def body(
    tokens,
    ln_gain,
    ln_bias,
    qkv_weight,
    qkv_bias,
    dense_weight,
    dense_bias,
    fc1_weight,
    fc1_bias,
    fc2_weight,
    fc2_bias,
    starts,
    cotangent,
):
    token_float = tokens.astype(jnp.float32)
    normed_low = normalize(token_float, ln_gain, ln_bias).astype(jnp.bfloat16)
    gathered = lax.all_gather(normed_low, "mp", axis=0, tiled=True)
    group_rows = gathered.shape[0]
    masters = (
        qkv_weight.astype(jnp.bfloat16),
        dense_weight.astype(jnp.bfloat16),
        fc1_weight.astype(jnp.bfloat16),
        fc2_weight.astype(jnp.bfloat16),
    )
    qkv_full, dense_full, up_full, down_full = (
        lax.all_gather(masters[0], "dp", axis=0, tiled=True),
        lax.all_gather(masters[1], "dp", axis=0, tiled=True),
        lax.all_gather(masters[2], "dp", axis=0, tiled=True),
        lax.all_gather(masters[3], "dp", axis=0, tiled=True),
    )
    model_width = qkv_full.shape[0]
    local_width = qkv_full.shape[2]
    heads_local = local_width // HEAD_DIM
    seq_count = group_rows // LENGTH

    def to_sequences(tensor):
        return tensor.reshape(seq_count, LENGTH, heads_local, HEAD_DIM)

    def to_heads(tensor):
        return tensor.reshape(group_rows, heads_local, HEAD_DIM)

    projected = jnp.dot(
        gathered, qkv_full.reshape(model_width, 3 * local_width), preferred_element_type=jnp.float32
    ) + qkv_bias.reshape(3 * local_width)
    cosine_table, sine_table = rotary_tables(group_rows)
    queries = rotate(to_heads(projected[:, :local_width]), cosine_table, sine_table).astype(
        jnp.bfloat16
    )
    key_rows = rotate(
        to_heads(projected[:, local_width : 2 * local_width]), cosine_table, sine_table
    ).astype(jnp.bfloat16)
    values_in = to_heads(projected[:, 2 * local_width :]).astype(jnp.bfloat16)
    attended, logsum = lax.map(
        attend_forward,
        (to_sequences(queries), to_sequences(key_rows), to_sequences(values_in), starts),
    )
    attended = attended.reshape(group_rows, local_width)
    attn_part = right_product(attended, dense_full)
    hidden_pre = jnp.dot(gathered, up_full, preferred_element_type=jnp.float32) + fc1_bias
    hidden_low = jax.nn.gelu(hidden_pre, approximate=True).astype(jnp.bfloat16)
    mlp_part = right_product(hidden_low, down_full)
    mixed_sum = low_scatter(attn_part + mlp_part, "mp")
    output = (token_float + mixed_sum + dense_bias + fc2_bias).astype(jnp.bfloat16)
    out_rows = lax.all_gather(cotangent, "mp", axis=0, tiled=True)
    qkv_full, dense_full, up_full, down_full = (
        lax.all_gather(masters[0], "dp", axis=0, tiled=True),
        lax.all_gather(masters[1], "dp", axis=0, tiled=True),
        lax.all_gather(masters[2], "dp", axis=0, tiled=True),
        lax.all_gather(masters[3], "dp", axis=0, tiled=True),
    )
    attended_grad = jnp.dot(out_rows, dense_full, preferred_element_type=jnp.float32).astype(
        jnp.bfloat16
    )
    dense_grad = rows_product(out_rows, attended)
    down_grad = rows_product(out_rows, hidden_low)
    hidden_grad = jnp.dot(out_rows, down_full, preferred_element_type=jnp.float32)
    gelu_value, gelu_back = jax.vjp(partial(jax.nn.gelu, approximate=True), hidden_pre)
    pre_grad = gelu_back(hidden_grad)[0].astype(jnp.bfloat16)
    up_grad = rows_product(gathered, pre_grad)
    up_bias_grad = jnp.sum(pre_grad.astype(jnp.float32), axis=0)
    query_grad, key_grad, value_grad = lax.map(
        attend_backward,
        (
            to_sequences(queries),
            to_sequences(key_rows),
            to_sequences(values_in),
            starts,
            logsum,
            to_sequences(attended_grad),
        ),
    )
    query_grad = unrotate(to_heads(query_grad), cosine_table, sine_table).reshape(
        group_rows, local_width
    )
    key_grad = unrotate(to_heads(key_grad), cosine_table, sine_table).reshape(
        group_rows, local_width
    )
    projected_grad = jnp.concatenate(
        [query_grad, key_grad, value_grad.reshape(group_rows, local_width)], axis=1
    ).astype(jnp.bfloat16)
    qkv_grad = rows_product(gathered, projected_grad).reshape(model_width, 3, local_width)
    qkv_bias_grad = jnp.sum(projected_grad.astype(jnp.float32), axis=0).reshape(3, local_width)
    attn_input = right_product(projected_grad, qkv_full.reshape(model_width, 3 * local_width))
    mlp_input = right_product(pre_grad, up_full)
    normed_grad = low_scatter(attn_input + mlp_input, "mp")
    norm_value, norm_back = jax.vjp(normalize, token_float, ln_gain, ln_bias)
    token_grad, gain_grad, shift_grad = norm_back(normed_grad)
    cot_float = cotangent.astype(jnp.float32)
    input_grad = (cot_float + token_grad).astype(jnp.bfloat16)
    out_bias_grad = jnp.sum(cot_float, axis=0)
    gain_total, shift_total, bias_total = lax.psum(
        (gain_grad, shift_grad, out_bias_grad), ("dp", "mp")
    )
    qkv_bias_total, up_bias_total = lax.psum((qkv_bias_grad, up_bias_grad), "dp")
    qkv_share, dense_share, up_share, down_share = (
        low_scatter(qkv_grad, "dp"),
        low_scatter(dense_grad, "dp"),
        low_scatter(up_grad, "dp"),
        low_scatter(down_grad, "dp"),
    )
    return (
        output,
        input_grad,
        gain_total,
        shift_total,
        qkv_share,
        qkv_bias_total,
        dense_share,
        bias_total,
        up_share,
        up_bias_total,
        down_share,
        bias_total,
    )


def solution(mesh):
    in_specs = (
        P(("dp", "mp"), None),
        P(),
        P(),
        P("dp", None, "mp"),
        P(None, "mp"),
        P("dp", "mp"),
        P(),
        P("dp", "mp"),
        P("mp"),
        P("dp", "mp"),
        P(),
        P("dp"),
        P(("dp", "mp"), None),
    )
    out_specs = (
        P(("dp", "mp"), None),
        P(("dp", "mp"), None),
        P(),
        P(),
        P("dp", None, "mp"),
        P(None, "mp"),
        P("dp", "mp"),
        P(),
        P("dp", "mp"),
        P("mp"),
        P("dp", "mp"),
        P(),
    )
    return jax.shard_map(body, mesh=mesh, in_specs=in_specs, out_specs=out_specs, check_vma=False)
```

```python
from functools import partial

import jax
import jax.numpy as jnp
from jax import lax
from jax.experimental import pallas as pl
from jax.experimental.pallas import tpu as pltpu
from jax.sharding import PartitionSpec as P

HEAD_DIM = 64
ROT_DIM = 32
LENGTH = 1024
PIECE = 256
EPSILON = 1e-05
NEGATIVE = -1e30
MESH = pl.DeviceIdType.MESH
BF = jnp.bfloat16
F32 = jnp.float32
ANY = pl.BlockSpec(memory_space=pl.ANY)
VM = pl.BlockSpec(memory_space=pltpu.VMEM)


def dot(a, b, ca=1, cb=0):
    return lax.dot_general(a, b, (((ca,), (cb,)), ((), ())), preferred_element_type=F32)


def remote(src, dst, send, recv, dp_index, mp_index):
    return pltpu.make_async_remote_copy(
        src_ref=src,
        dst_ref=dst,
        send_sem=send,
        recv_sem=recv,
        device_id=(dp_index, mp_index),
        device_id_type=MESH,
    )


def place():
    me = lax.axis_index("dp")
    return me, me // 2, lax.rem(me, 2), lax.axis_index("mp")


def greet(chips, mp_size):
    me, z, c, mp = place()
    bar = pltpu.get_barrier_semaphore()
    pl.semaphore_signal(bar, 1, device_id=(2 * z + 1 - c, mp), device_id_type=MESH)

    @pl.when(z > 0)
    def _():
        pl.semaphore_signal(bar, 1, device_id=(me - 2, mp), device_id_type=MESH)

    @pl.when(z < chips - 1)
    def _():
        pl.semaphore_signal(bar, 1, device_id=(me + 2, mp), device_id_type=MESH)

    for k in range(1, mp_size):
        pl.semaphore_signal(
            bar, 1, device_id=(me, lax.rem(mp + k, mp_size)), device_id_type=MESH
        )
    count = mp_size + jnp.where(z > 0, 1, 0) + jnp.where(z < chips - 1, 1, 0)
    pl.semaphore_wait(bar, count)


class RowGather:
    def __init__(self, chips, own, full, sems):
        self.chips, self.own, self.full = chips, own, full
        self.recv, self.left, self.right, self.side = sems

    def copies(self, oz):
        me, z, c, mp = place()
        b = 2 * oz + c
        dst = self.full.at[b]

        def make(src, send, target):
            return remote(src, dst, send.at[oz], self.recv.at[b], target, mp)

        return (
            lambda src: make(src, self.left, me - 2),
            lambda src: make(src, self.right, me + 2),
            lambda src: make(src, self.side, 2 * z + 1 - c),
        )

    def start(self):
        me, z, c, mp = place()
        left, right, side = self.copies(z)

        @pl.when(z > 0)
        def _():
            left(self.own).start()

        @pl.when(z < self.chips - 1)
        def _():
            right(self.own).start()

        side(self.own).start()

    def wait_block(self, b):
        me, z, c, mp = place()
        remote(self.full.at[b], self.full.at[b], self.side.at[0], self.recv.at[b], me, mp).wait_recv()

    def stage(self, k):
        me, z, c, mp = place()

        @pl.when(z + k < self.chips)
        def _():
            oz = z + k
            self.wait_block(2 * oz + c)
            left, right, side = self.copies(oz)

            @pl.when(z > 0)
            def _():
                left(self.full.at[2 * oz + c]).start()

            side(self.full.at[2 * oz + c]).start()

        @pl.when(z - k >= 0)
        def _():
            oz = z - k
            self.wait_block(2 * oz + c)
            left, right, side = self.copies(oz)

            @pl.when(z < self.chips - 1)
            def _():
                right(self.full.at[2 * oz + c]).start()

            side(self.full.at[2 * oz + c]).start()

    def drain(self):
        me, z, c, mp = place()
        for oz in range(self.chips):
            left, right, side = self.copies(oz)

            @pl.when((z > 0) & (oz >= z))
            def _():
                left(self.full.at[2 * oz + c]).wait_send()

            @pl.when((z < self.chips - 1) & (oz <= z))
            def _():
                right(self.full.at[2 * oz + c]).wait_send()

            side(self.full.at[2 * oz + c]).wait_send()


class GroupGather:
    def __init__(self, size, own, full, sems):
        self.size, self.own, self.full = size, own, full
        self.send, self.recv = sems
        self.half = full.shape[1] // 2

    def to(self, src, origin, part, slot, target):
        me, z, c, mp = place()
        rows = self.full.at[origin] if part is None else self.full.at[origin, pl.ds(part * self.half, self.half)]
        sem = self.recv.at[origin, 0 if part is None else part]
        return remote(src, rows, self.send.at[slot], sem, me, target)

    def start(self):
        me, z, c, mp = place()
        for slot, peer in self.peers():
            self.to(self.own, mp, None, slot, peer).start()

    def peers(self):
        me, z, c, mp = place()
        if self.size == 4:
            x_peer = mp + 1 - 2 * lax.rem(mp, 2)
            return ((0, x_peer), (1, lax.rem(mp + 2, 4)))
        return tuple((k - 1, lax.rem(mp + k, self.size)) for k in range(1, self.size))

    def relays(self):
        (_, x_peer), (_, y_peer) = self.peers()
        return (
            self.to(self.full.at[x_peer, pl.ds(0, self.half)], x_peer, 0, 2, y_peer),
            self.to(self.full.at[y_peer, pl.ds(self.half, self.half)], y_peer, 1, 3, x_peer),
        )

    def relay(self):
        for slot, peer in self.peers():
            self.to(self.full.at[peer], peer, None, slot, peer).wait_recv()
        if self.size == 4:
            for copy in self.relays():
                copy.start()

    def finish(self):
        me, z, c, mp = place()
        if self.size == 4:
            far = 3 - mp
            for part in (0, 1):
                rows = self.full.at[far, pl.ds(part * self.half, self.half)]
                self.to(rows, far, part, 0, mp).wait_recv()

    def drain(self):
        me, z, c, mp = place()
        for slot, peer in self.peers():
            self.to(self.own, mp, None, slot, peer).wait_send()
        if self.size == 4:
            for copy in self.relays():
                copy.wait_send()


def row_gather_sems(dp_size):
    chips = dp_size // 2
    return [pltpu.SemaphoreType.DMA((n,)) for n in (dp_size, chips, chips, chips)]


def group_gather_sems(mp_size):
    return [pltpu.SemaphoreType.DMA((max(4, mp_size - 1),)), pltpu.SemaphoreType.DMA((mp_size, 2))]


def gelu_pair(v):
    k0, k1 = 0.7978845608028654, 0.044715
    square = v * v
    t = jnp.tanh(k0 * (v + k1 * v * square))
    half = 0.5 * (1.0 + t)
    slope = half + 0.5 * v * (1.0 - t * t) * (k0 + 3.0 * k0 * k1 * square)
    return v * half, slope


def up_kernel(
    dp_size,
    mp_size,
    tokens,
    gain,
    shift,
    cot,
    up_master,
    up_bias,
    x_out,
    cot_out,
    up_out,
    hidden_out,
    slope_out,
    x_all,
    up_all,
    acc,
    hidden,
    slope,
    *sems,
):
    chips = dp_size // 2
    row_sems, x_sems, cot_sems = sems[0:4], sems[4:6], sems[6:8]
    out_sem = sems[8]
    me, z, c, mp = place()
    rows = tokens.shape[0]
    length = rows * mp_size
    depth, width = up_all.shape[1], up_all.shape[2]

    values = tokens[...].astype(F32)
    centre = values - jnp.mean(values, axis=-1, keepdims=True)
    spread = jnp.mean(centre * centre, axis=-1, keepdims=True)
    x_all[mp] = (centre * lax.rsqrt(spread + EPSILON) * gain[...] + shift[...]).astype(BF)
    up_all[me] = up_master[...].astype(BF)

    greet(chips, mp_size)
    weights = RowGather(chips, up_all.at[me], up_all, row_sems)
    x_gather = GroupGather(mp_size, x_all.at[mp], x_all, x_sems)
    cot_gather = GroupGather(mp_size, cot, cot_out, cot_sems)
    x_gather.start()
    weights.start()
    own_cot = pltpu.make_async_copy(cot, cot_out.at[mp], out_sem.at[0])
    own_cot.start()

    def product(oz, first=False):
        cols = pl.ds(pl.multiple_of(oz * (2 * depth), 2 * depth), 2 * depth)

        def tile(i, carry):
            r, n = i // (width // 512), lax.rem(i, width // 512)
            n0 = pl.ds(pl.multiple_of(n * 512, 512), 512)
            left = x_all[r, :, cols]
            right = up_all[pl.ds(2 * oz, 2), :, n0].reshape(2 * depth, 512)
            term = dot(left, right)
            if first:
                acc[r, :, n0] = term + up_bias[:, n0]
            else:
                acc[r, :, n0] += term
            return carry

        lax.fori_loop(0, mp_size * (width // 512), tile, 0)

    x_gather.relay()
    x_gather.finish()
    weights.stage(1)
    cot_gather.start()
    x_copy = pltpu.make_async_copy(x_all, x_out, out_sem.at[1])
    x_copy.start()
    weights.wait_block(2 * z + 1 - c)
    product(z, True)
    for k in range(1, chips):
        if k > 1:
            weights.stage(k)
        for oz, valid in ((z + k, z + k < chips), (z - k, z - k >= 0)):

            @pl.when(valid)
            def _():
                weights.wait_block(2 * oz + 1 - c)
                product(oz)

        if k == min(2, chips - 1):
            cot_gather.relay()
    up_copy = pltpu.make_async_copy(up_all, up_out, out_sem.at[2])
    up_copy.start()

    def finish(i, carry):
        r, n = i // (width // 512), lax.rem(i, width // 512)
        n0 = pl.ds(pl.multiple_of(n * 512, 512), 512)
        high, grad = gelu_pair(acc[r, :, n0])
        hidden[r, :, n0] = high.astype(BF)
        slope[r, :, n0] = grad.astype(BF)
        return carry

    lax.fori_loop(0, mp_size * (width // 512), finish, 0)
    hidden_copy = pltpu.make_async_copy(hidden, hidden_out, out_sem.at[3])
    slope_copy = pltpu.make_async_copy(slope, slope_out, out_sem.at[4])
    hidden_copy.start()
    slope_copy.start()
    cot_gather.finish()
    weights.drain()
    x_gather.drain()
    cot_gather.drain()
    for copy in (own_cot, x_copy, up_copy, hidden_copy, slope_copy):
        copy.wait()


def up_stage(dp_size, mp_size, tokens, gain, shift, cot, up_master, up_bias):
    rows, model = tokens.shape
    depth, width = up_master.shape
    shape = jax.ShapeDtypeStruct
    outs = (
        shape((mp_size, rows, model), BF),
        shape((mp_size, rows, model), BF),
        shape((dp_size, depth, width), BF),
        shape((mp_size, rows, width), BF),
        shape((mp_size, rows, width), BF),
    )
    return pl.pallas_call(
        partial(up_kernel, dp_size, mp_size),
        out_shape=outs,
        in_specs=[VM] * 6,
        out_specs=[ANY] * 5,
        scratch_shapes=[
            pltpu.VMEM((mp_size, rows, model), BF),
            pltpu.VMEM((dp_size, depth, width), BF),
            pltpu.VMEM((mp_size, rows, width), F32),
            pltpu.VMEM((mp_size, rows, width), BF),
            pltpu.VMEM((mp_size, rows, width), BF),
            *row_gather_sems(dp_size),
            *group_gather_sems(mp_size),
            *group_gather_sems(mp_size),
            pltpu.SemaphoreType.DMA((5,)),
        ],
        compiler_params=pltpu.CompilerParams(
            collective_id=1, has_side_effects=True, vmem_limit_bytes=58 << 20
        ),
        name="up_stage",
    )(tokens, gain.reshape(1, -1), shift.reshape(1, -1), cot, up_master, up_bias.reshape(1, -1))


def normalize(values, gain_vec, shift_vec):
    centre = values - jnp.mean(values, axis=-1, keepdims=True)
    spread = jnp.mean(centre * centre, axis=-1, keepdims=True)
    scaled = centre * lax.rsqrt(spread + EPSILON)
    return scaled * gain_vec + shift_vec


def rotary_tables(row_count):
    half_dim = ROT_DIM // 2
    places = (jnp.arange(row_count) % LENGTH).astype(jnp.float32)
    frequency = 10000.0 ** (-jnp.arange(half_dim).astype(jnp.float32) * 2.0 / ROT_DIM)
    angles = places[:, None] * frequency[None, :]
    return (jnp.cos(angles), jnp.sin(angles))


def rotate(values, cosine_table, sine_table):
    half_dim = ROT_DIM // 2
    first_part = values[..., :half_dim]
    second_part = values[..., half_dim:ROT_DIM]
    cosine_row = cosine_table[:, None, :]
    sine_row = sine_table[:, None, :]
    return jnp.concatenate(
        [
            first_part * cosine_row - second_part * sine_row,
            second_part * cosine_row + first_part * sine_row,
            values[..., ROT_DIM:],
        ],
        axis=-1,
    )


def unrotate(gradient, cosine_table, sine_table):
    half_dim = ROT_DIM // 2
    first_part = gradient[..., :half_dim]
    second_part = gradient[..., half_dim:ROT_DIM]
    cosine_row = cosine_table[:, None, :]
    sine_row = sine_table[:, None, :]
    return jnp.concatenate(
        [
            first_part * cosine_row + second_part * sine_row,
            second_part * cosine_row - first_part * sine_row,
            gradient[..., ROT_DIM:],
        ],
        axis=-1,
    )


def allowed_mask(piece_start):
    places = jnp.arange(LENGTH)
    inside = (places >= piece_start) & (places < piece_start + PIECE)
    return (places[None, :] <= places[:, None]) | inside[:, None] & inside[None, :]


def masked_scores(queries, key_rows, piece_start):
    scores = jnp.einsum(
        "qhd,khd->hqk", queries, key_rows, preferred_element_type=jnp.float32
    ) * HEAD_DIM ** (-0.5)
    return jnp.where(allowed_mask(piece_start)[None], scores, NEGATIVE)


def attend_forward(members):
    queries, key_rows, values_in, piece_start = members
    masked = masked_scores(queries, key_rows, piece_start)
    row_max = jnp.max(masked, axis=-1, keepdims=True)
    expo_values = jnp.exp(masked - row_max)
    row_total = jnp.sum(expo_values, axis=-1, keepdims=True)
    prob_low = (expo_values / row_total).astype(jnp.bfloat16)
    attended = jnp.einsum("hqk,khd->qhd", prob_low, values_in, preferred_element_type=jnp.float32)
    return (attended.astype(jnp.bfloat16), (row_max + jnp.log(row_total))[..., 0])


def attend_backward(members):
    queries, key_rows, values_in, piece_start, logsum, out_grad = members
    masked = masked_scores(queries, key_rows, piece_start)
    prob_values = jnp.exp(masked - logsum[..., None])
    prob_low = prob_values.astype(jnp.bfloat16)
    value_grad = jnp.einsum("hqk,qhd->khd", prob_low, out_grad, preferred_element_type=jnp.float32)
    prob_grad = jnp.einsum("qhd,khd->hqk", out_grad, values_in, preferred_element_type=jnp.float32)
    inner_sum = jnp.sum(prob_values * prob_grad, axis=-1, keepdims=True)
    score_grad = (prob_values * (prob_grad - inner_sum)).astype(jnp.bfloat16)
    query_grad = jnp.einsum(
        "hqk,khd->qhd", score_grad, key_rows, preferred_element_type=jnp.float32
    ) * HEAD_DIM ** (-0.5)
    key_grad = jnp.einsum(
        "hqk,qhd->khd", score_grad, queries, preferred_element_type=jnp.float32
    ) * HEAD_DIM ** (-0.5)
    return (query_grad, key_grad, value_grad)


def right_product(left_side, right_side):
    return lax.dot_general(
        left_side, right_side, (((1,), (1,)), ((), ())), preferred_element_type=jnp.float32
    )


def rows_product(left_side, right_side):
    return lax.dot_general(
        left_side, right_side, (((0,), (0,)), ((), ())), preferred_element_type=jnp.float32
    )


def low_scatter(partial_sums, axis):
    return lax.psum_scatter(
        partial_sums.astype(jnp.bfloat16), axis, scatter_dimension=0, tiled=True
    ).astype(jnp.float32)


def body(
    tokens,
    ln_gain,
    ln_bias,
    qkv_weight,
    qkv_bias,
    dense_weight,
    dense_bias,
    fc1_weight,
    fc1_bias,
    fc2_weight,
    fc2_bias,
    starts,
    cotangent,
):
    token_float = tokens.astype(jnp.float32)
    dp_size, mp_size = lax.axis_size("dp"), lax.axis_size("mp")
    x_all, cot_all, up_all, hidden_all, slope_all = up_stage(
        dp_size, mp_size, tokens, ln_gain, ln_bias, cotangent, fc1_weight, fc1_bias
    )
    gathered = x_all.reshape(-1, x_all.shape[-1])
    out_rows = cot_all.reshape(gathered.shape)
    up_full = up_all.reshape(-1, up_all.shape[-1])
    hidden_low = hidden_all.reshape(-1, up_all.shape[-1])
    slope = slope_all.reshape(hidden_low.shape)
    group_rows = gathered.shape[0]
    masters = (
        qkv_weight.astype(jnp.bfloat16),
        dense_weight.astype(jnp.bfloat16),
        fc2_weight.astype(jnp.bfloat16),
    )
    qkv_full, dense_full, down_full = (
        lax.all_gather(masters[0], "dp", axis=0, tiled=True),
        lax.all_gather(masters[1], "dp", axis=0, tiled=True),
        lax.all_gather(masters[2], "dp", axis=0, tiled=True),
    )
    model_width = qkv_full.shape[0]
    local_width = qkv_full.shape[2]
    heads_local = local_width // HEAD_DIM
    seq_count = group_rows // LENGTH

    def to_sequences(tensor):
        return tensor.reshape(seq_count, LENGTH, heads_local, HEAD_DIM)

    def to_heads(tensor):
        return tensor.reshape(group_rows, heads_local, HEAD_DIM)

    projected = jnp.dot(
        gathered, qkv_full.reshape(model_width, 3 * local_width), preferred_element_type=jnp.float32
    ) + qkv_bias.reshape(3 * local_width)
    cosine_table, sine_table = rotary_tables(group_rows)
    queries = rotate(to_heads(projected[:, :local_width]), cosine_table, sine_table).astype(
        jnp.bfloat16
    )
    key_rows = rotate(
        to_heads(projected[:, local_width : 2 * local_width]), cosine_table, sine_table
    ).astype(jnp.bfloat16)
    values_in = to_heads(projected[:, 2 * local_width :]).astype(jnp.bfloat16)
    attended, logsum = lax.map(
        attend_forward,
        (to_sequences(queries), to_sequences(key_rows), to_sequences(values_in), starts),
    )
    attended = attended.reshape(group_rows, local_width)
    attn_part = right_product(attended, dense_full)
    mlp_part = right_product(hidden_low, down_full)
    mixed_sum = low_scatter(attn_part + mlp_part, "mp")
    output = (token_float + mixed_sum + dense_bias + fc2_bias).astype(jnp.bfloat16)
    attended_grad = jnp.dot(out_rows, dense_full, preferred_element_type=jnp.float32).astype(
        jnp.bfloat16
    )
    dense_grad = rows_product(out_rows, attended)
    down_grad = rows_product(out_rows, hidden_low)
    hidden_grad = jnp.dot(out_rows, down_full, preferred_element_type=jnp.float32)
    pre_grad = (hidden_grad * slope).astype(jnp.bfloat16)
    up_grad = rows_product(gathered, pre_grad)
    up_bias_grad = jnp.sum(pre_grad.astype(jnp.float32), axis=0)
    query_grad, key_grad, value_grad = lax.map(
        attend_backward,
        (
            to_sequences(queries),
            to_sequences(key_rows),
            to_sequences(values_in),
            starts,
            logsum,
            to_sequences(attended_grad),
        ),
    )
    query_grad = unrotate(to_heads(query_grad), cosine_table, sine_table).reshape(
        group_rows, local_width
    )
    key_grad = unrotate(to_heads(key_grad), cosine_table, sine_table).reshape(
        group_rows, local_width
    )
    projected_grad = jnp.concatenate(
        [query_grad, key_grad, value_grad.reshape(group_rows, local_width)], axis=1
    ).astype(jnp.bfloat16)
    qkv_grad = rows_product(gathered, projected_grad).reshape(model_width, 3, local_width)
    qkv_bias_grad = jnp.sum(projected_grad.astype(jnp.float32), axis=0).reshape(3, local_width)
    attn_input = right_product(projected_grad, qkv_full.reshape(model_width, 3 * local_width))
    mlp_input = right_product(pre_grad, up_full)
    normed_grad = low_scatter(attn_input + mlp_input, "mp")
    norm_value, norm_back = jax.vjp(normalize, token_float, ln_gain, ln_bias)
    token_grad, gain_grad, shift_grad = norm_back(normed_grad)
    cot_float = cotangent.astype(jnp.float32)
    input_grad = (cot_float + token_grad).astype(jnp.bfloat16)
    out_bias_grad = jnp.sum(cot_float, axis=0)
    gain_total, shift_total, bias_total = lax.psum(
        (gain_grad, shift_grad, out_bias_grad), ("dp", "mp")
    )
    qkv_bias_total, up_bias_total = lax.psum((qkv_bias_grad, up_bias_grad), "dp")
    qkv_share, dense_share, up_share, down_share = (
        low_scatter(qkv_grad, "dp"),
        low_scatter(dense_grad, "dp"),
        low_scatter(up_grad, "dp"),
        low_scatter(down_grad, "dp"),
    )
    return (
        output,
        input_grad,
        gain_total,
        shift_total,
        qkv_share,
        qkv_bias_total,
        dense_share,
        bias_total,
        up_share,
        up_bias_total,
        down_share,
        bias_total,
    )


def solution(mesh):
    in_specs = (
        P(("dp", "mp"), None),
        P(),
        P(),
        P("dp", None, "mp"),
        P(None, "mp"),
        P("dp", "mp"),
        P(),
        P("dp", "mp"),
        P("mp"),
        P("dp", "mp"),
        P(),
        P("dp"),
        P(("dp", "mp"), None),
    )
    out_specs = (
        P(("dp", "mp"), None),
        P(("dp", "mp"), None),
        P(),
        P(),
        P("dp", None, "mp"),
        P(None, "mp"),
        P("dp", "mp"),
        P(),
        P("dp", "mp"),
        P("mp"),
        P("dp", "mp"),
        P(),
    )
    return jax.shard_map(body, mesh=mesh, in_specs=in_specs, out_specs=out_specs, check_vma=False)
```

```python
from functools import partial

import jax
import jax.numpy as jnp
from jax import lax
from jax.experimental import pallas as pl
from jax.experimental.pallas import tpu as pltpu
from jax.sharding import PartitionSpec as P

HEAD_DIM = 64
ROT_DIM = 32
LENGTH = 1024
PIECE = 256
EPSILON = 1e-05
NEGATIVE = -1e30
MESH = pl.DeviceIdType.MESH
BF = jnp.bfloat16
F32 = jnp.float32
ANY = pl.BlockSpec(memory_space=pl.ANY)
VM = pl.BlockSpec(memory_space=pltpu.VMEM)


def dot(a, b, ca=1, cb=0):
    return lax.dot_general(a, b, (((ca,), (cb,)), ((), ())), preferred_element_type=F32)


def remote(src, dst, send, recv, dp_index, mp_index):
    return pltpu.make_async_remote_copy(
        src_ref=src,
        dst_ref=dst,
        send_sem=send,
        recv_sem=recv,
        device_id=(dp_index, mp_index),
        device_id_type=MESH,
    )


def place():
    me = lax.axis_index("dp")
    return me, me // 2, lax.rem(me, 2), lax.axis_index("mp")


def greet(chips, mp_size):
    me, z, c, mp = place()
    bar = pltpu.get_barrier_semaphore()
    pl.semaphore_signal(bar, 1, device_id=(2 * z + 1 - c, mp), device_id_type=MESH)

    @pl.when(z > 0)
    def _():
        pl.semaphore_signal(bar, 1, device_id=(me - 2, mp), device_id_type=MESH)

    @pl.when(z < chips - 1)
    def _():
        pl.semaphore_signal(bar, 1, device_id=(me + 2, mp), device_id_type=MESH)

    for k in range(1, mp_size):
        pl.semaphore_signal(
            bar, 1, device_id=(me, lax.rem(mp + k, mp_size)), device_id_type=MESH
        )
    count = mp_size + jnp.where(z > 0, 1, 0) + jnp.where(z < chips - 1, 1, 0)
    pl.semaphore_wait(bar, count)


class RowGather:
    def __init__(self, chips, own, full, sems):
        self.chips, self.own, self.full = chips, own, full
        self.recv, self.left, self.right, self.side = sems

    def copies(self, oz):
        me, z, c, mp = place()
        b = 2 * oz + c
        dst = self.full.at[b]

        def make(src, send, target):
            return remote(src, dst, send.at[oz], self.recv.at[b], target, mp)

        return (
            lambda src: make(src, self.left, me - 2),
            lambda src: make(src, self.right, me + 2),
            lambda src: make(src, self.side, 2 * z + 1 - c),
        )

    def start(self):
        me, z, c, mp = place()
        left, right, side = self.copies(z)

        @pl.when(z > 0)
        def _():
            left(self.own).start()

        @pl.when(z < self.chips - 1)
        def _():
            right(self.own).start()

        side(self.own).start()

    def wait_block(self, b):
        me, z, c, mp = place()
        remote(self.full.at[b], self.full.at[b], self.side.at[0], self.recv.at[b], me, mp).wait_recv()

    def stage(self, k):
        me, z, c, mp = place()

        @pl.when(z + k < self.chips)
        def _():
            oz = z + k
            self.wait_block(2 * oz + c)
            left, right, side = self.copies(oz)

            @pl.when(z > 0)
            def _():
                left(self.full.at[2 * oz + c]).start()

            side(self.full.at[2 * oz + c]).start()

        @pl.when(z - k >= 0)
        def _():
            oz = z - k
            self.wait_block(2 * oz + c)
            left, right, side = self.copies(oz)

            @pl.when(z < self.chips - 1)
            def _():
                right(self.full.at[2 * oz + c]).start()

            side(self.full.at[2 * oz + c]).start()

    def drain(self):
        me, z, c, mp = place()
        for oz in range(self.chips):
            left, right, side = self.copies(oz)

            @pl.when((z > 0) & (oz >= z))
            def _():
                left(self.full.at[2 * oz + c]).wait_send()

            @pl.when((z < self.chips - 1) & (oz <= z))
            def _():
                right(self.full.at[2 * oz + c]).wait_send()

            side(self.full.at[2 * oz + c]).wait_send()


class GroupGather:
    def __init__(self, size, own, full, sems):
        self.size, self.own, self.full = size, own, full
        self.send, self.recv = sems
        self.half = full.shape[1] // 2

    def to(self, src, origin, part, slot, target):
        me, z, c, mp = place()
        rows = self.full.at[origin] if part is None else self.full.at[origin, pl.ds(part * self.half, self.half)]
        sem = self.recv.at[origin, 0 if part is None else part]
        return remote(src, rows, self.send.at[slot], sem, me, target)

    def start(self):
        me, z, c, mp = place()
        for slot, peer in self.peers():
            self.to(self.own, mp, None, slot, peer).start()

    def peers(self):
        me, z, c, mp = place()
        if self.size == 4:
            x_peer = mp + 1 - 2 * lax.rem(mp, 2)
            return ((0, x_peer), (1, lax.rem(mp + 2, 4)))
        return tuple((k - 1, lax.rem(mp + k, self.size)) for k in range(1, self.size))

    def relays(self):
        (_, x_peer), (_, y_peer) = self.peers()
        return (
            self.to(self.full.at[x_peer, pl.ds(0, self.half)], x_peer, 0, 2, y_peer),
            self.to(self.full.at[y_peer, pl.ds(self.half, self.half)], y_peer, 1, 3, x_peer),
        )

    def relay(self):
        for slot, peer in self.peers():
            self.to(self.full.at[peer], peer, None, slot, peer).wait_recv()
        if self.size == 4:
            for copy in self.relays():
                copy.start()

    def finish(self):
        me, z, c, mp = place()
        if self.size == 4:
            far = 3 - mp
            for part in (0, 1):
                rows = self.full.at[far, pl.ds(part * self.half, self.half)]
                self.to(rows, far, part, 0, mp).wait_recv()

    def drain(self):
        me, z, c, mp = place()
        for slot, peer in self.peers():
            self.to(self.own, mp, None, slot, peer).wait_send()
        if self.size == 4:
            for copy in self.relays():
                copy.wait_send()


def row_gather_sems(dp_size):
    chips = dp_size // 2
    return [pltpu.SemaphoreType.DMA((n,)) for n in (dp_size, chips, chips, chips)]


def group_gather_sems(mp_size):
    return [pltpu.SemaphoreType.DMA((max(4, mp_size - 1),)), pltpu.SemaphoreType.DMA((mp_size, 2))]


def gelu_pair(v):
    k0, k1 = 0.7978845608028654, 0.044715
    square = v * v
    t = jnp.tanh(k0 * (v + k1 * v * square))
    half = 0.5 * (1.0 + t)
    slope = half + 0.5 * v * (1.0 - t * t) * (k0 + 3.0 * k0 * k1 * square)
    return v * half, slope


def up_kernel(
    dp_size,
    mp_size,
    tokens,
    gain,
    shift,
    cot,
    up_master,
    up_bias,
    x_out,
    cot_out,
    up_out,
    hidden_out,
    slope_out,
    x_all,
    up_all,
    acc,
    hidden,
    slope,
    *sems,
):
    chips = dp_size // 2
    row_sems, x_sems, cot_sems = sems[0:4], sems[4:6], sems[6:8]
    out_sem = sems[8]
    me, z, c, mp = place()
    rows = tokens.shape[0]
    length = rows * mp_size
    depth, width = up_all.shape[1], up_all.shape[2]

    values = tokens[...].astype(F32)
    centre = values - jnp.mean(values, axis=-1, keepdims=True)
    spread = jnp.mean(centre * centre, axis=-1, keepdims=True)
    x_all[mp] = (centre * lax.rsqrt(spread + EPSILON) * gain[...] + shift[...]).astype(BF)
    up_all[me] = up_master[...].astype(BF)

    greet(chips, mp_size)
    weights = RowGather(chips, up_all.at[me], up_all, row_sems)
    x_gather = GroupGather(mp_size, x_all.at[mp], x_all, x_sems)
    cot_gather = GroupGather(mp_size, cot, cot_out, cot_sems)
    x_gather.start()
    weights.start()
    own_cot = pltpu.make_async_copy(cot, cot_out.at[mp], out_sem.at[0])
    own_cot.start()

    def product(oz, first=False):
        cols = pl.ds(pl.multiple_of(oz * (2 * depth), 2 * depth), 2 * depth)

        def tile(i, carry):
            r, n = i // (width // 512), lax.rem(i, width // 512)
            n0 = pl.ds(pl.multiple_of(n * 512, 512), 512)
            left = x_all[r, :, cols]
            right = up_all[pl.ds(2 * oz, 2), :, n0].reshape(2 * depth, 512)
            term = dot(left, right)
            if first:
                acc[r, :, n0] = term + up_bias[:, n0]
            else:
                acc[r, :, n0] += term
            return carry

        lax.fori_loop(0, mp_size * (width // 512), tile, 0)

    x_gather.relay()
    x_gather.finish()
    weights.stage(1)
    cot_gather.start()
    x_copy = pltpu.make_async_copy(x_all, x_out, out_sem.at[1])
    x_copy.start()
    weights.wait_block(2 * z + 1 - c)
    product(z, True)
    for k in range(1, chips):
        if k > 1:
            weights.stage(k)
        for oz, valid in ((z + k, z + k < chips), (z - k, z - k >= 0)):

            @pl.when(valid)
            def _():
                weights.wait_block(2 * oz + 1 - c)
                product(oz)

        if k == min(2, chips - 1):
            cot_gather.relay()
    up_copy = pltpu.make_async_copy(up_all, up_out, out_sem.at[2])
    up_copy.start()

    def finish(i, carry):
        r, n = i // (width // 512), lax.rem(i, width // 512)
        n0 = pl.ds(pl.multiple_of(n * 512, 512), 512)
        high, grad = gelu_pair(acc[r, :, n0])
        hidden[r, :, n0] = high.astype(BF)
        slope[r, :, n0] = grad.astype(BF)
        return carry

    lax.fori_loop(0, mp_size * (width // 512), finish, 0)
    hidden_copy = pltpu.make_async_copy(hidden, hidden_out, out_sem.at[3])
    slope_copy = pltpu.make_async_copy(slope, slope_out, out_sem.at[4])
    hidden_copy.start()
    slope_copy.start()
    cot_gather.finish()
    weights.drain()
    x_gather.drain()
    cot_gather.drain()
    for copy in (own_cot, x_copy, up_copy, hidden_copy, slope_copy):
        copy.wait()


def up_stage(dp_size, mp_size, tokens, gain, shift, cot, up_master, up_bias):
    rows, model = tokens.shape
    depth, width = up_master.shape
    shape = jax.ShapeDtypeStruct
    outs = (
        shape((mp_size, rows, model), BF),
        shape((mp_size, rows, model), BF),
        shape((dp_size, depth, width), BF),
        shape((mp_size, rows, width), BF),
        shape((mp_size, rows, width), BF),
    )
    return pl.pallas_call(
        partial(up_kernel, dp_size, mp_size),
        out_shape=outs,
        in_specs=[VM] * 6,
        out_specs=[ANY] * 5,
        scratch_shapes=[
            pltpu.VMEM((mp_size, rows, model), BF),
            pltpu.VMEM((dp_size, depth, width), BF),
            pltpu.VMEM((mp_size, rows, width), F32),
            pltpu.VMEM((mp_size, rows, width), BF),
            pltpu.VMEM((mp_size, rows, width), BF),
            *row_gather_sems(dp_size),
            *group_gather_sems(mp_size),
            *group_gather_sems(mp_size),
            pltpu.SemaphoreType.DMA((5,)),
        ],
        compiler_params=pltpu.CompilerParams(
            collective_id=1, has_side_effects=True, vmem_limit_bytes=58 << 20
        ),
        name="up_stage",
    )(tokens, gain.reshape(1, -1), shift.reshape(1, -1), cot, up_master, up_bias.reshape(1, -1))


def normalize(values, gain_vec, shift_vec):
    centre = values - jnp.mean(values, axis=-1, keepdims=True)
    spread = jnp.mean(centre * centre, axis=-1, keepdims=True)
    scaled = centre * lax.rsqrt(spread + EPSILON)
    return scaled * gain_vec + shift_vec


def attention_kernel(start, q_in, k_in, v_in, out_grad, rot, out, q_grad, k_grad, v_grad, q_sum, k_sum, v_sum, bias, k_acc, v_acc):
    length = q_in.shape[0]
    block = 256
    blocks = length // block

    @pl.when(pl.program_id(0) == 0)
    def _():
        first = start[0]
        for i in range(blocks):
            high = min(length, block * (i + 2)) - block * i
            keys = block * i + lax.broadcasted_iota(jnp.int32, (high, block), 0)
            places = block * i + lax.broadcasted_iota(jnp.int32, (high, block), 1)
            inside = (keys >= first) & (keys < first + PIECE) & (places >= first) & (places < first + PIECE)
            bias[i, :high] = jnp.where((keys <= places) | inside, 0.0, NEGATIVE)

    def turn(values, sign):
        return (
            values * rot[0]
            + sign * (pltpu.roll(values, 128 - ROT_DIM // 2, 1) * rot[1] + pltpu.roll(values, ROT_DIM // 2, 1) * rot[2])
        )

    scale = HEAD_DIM ** (-0.5)
    q_low = (turn(q_in[...], 1.0).astype(BF).astype(F32) * scale).astype(BF)
    k_low = turn(k_in[...], 1.0).astype(BF)
    v_low = v_in[...].astype(BF)
    grad = out_grad[...]
    k_flip, v_flip = k_low.T, v_low.T
    lane = lax.broadcasted_iota(jnp.int32, (length, 128), 1) < HEAD_DIM
    row = lax.broadcasted_iota(jnp.int32, (128, length), 0) < HEAD_DIM
    zero = jnp.zeros((), BF)
    k_acc[...] = jnp.zeros_like(k_acc)
    v_acc[...] = jnp.zeros_like(v_acc)
    heads = []
    for h in range(2):
        lanes, rows = (lane, row) if h == 0 else (~lane, ~row)
        heads.append(
            (
                jnp.where(lanes, q_low, zero),
                jnp.where(lanes, k_low, zero),
                jnp.where(lanes, v_low, zero),
                jnp.where(lanes, grad, zero),
                jnp.where(rows, k_flip, zero),
                jnp.where(rows, v_flip, zero),
            )
        )
    for i in range(blocks):
        here = slice(block * i, block * (i + 1))
        stop = min(length, block * (i + 2))
        parts = [(0, block * i)] if i else []
        parts.append((block * i, stop))
        out_flip = jnp.zeros((128, block), F32)
        q_flip = jnp.zeros((128, block), F32)
        for q_h, k_h, v_h, grad_h, kt_h, vt_h in heads:
            scores = [dot(k_h[a:b], q_low[here], 1, 1) for a, b in parts]
            scores[-1] = scores[-1] + bias[i, : stop - block * i]
            top = scores[-1].max(0, keepdims=True)
            for s in scores[:-1]:
                top = jnp.maximum(top, s.max(0, keepdims=True))
            expo = [jnp.exp(s - top) for s in scores]
            total = expo[0].sum(0, keepdims=True)
            for e in expo[1:]:
                total = total + e.sum(0, keepdims=True)
            share = 1.0 / total
            probs = [e * share for e in expo]
            grads = [dot(v_h[a:b], grad[here], 1, 1) for a, b in parts]
            inner = (probs[0] * grads[0]).sum(0, keepdims=True)
            for p, g in zip(probs[1:], grads[1:]):
                inner = inner + (p * g).sum(0, keepdims=True)
            for (a, b), p, g in zip(parts, probs, grads):
                p_low = p.astype(BF)
                s_grad = (p * (g - inner)).astype(BF)
                out_flip = out_flip + dot(vt_h[:, a:b], p_low)
                q_flip = q_flip + dot(kt_h[:, a:b], s_grad)
                v_acc[a:b] += dot(p_low, grad_h[here])
                k_acc[a:b] += dot(s_grad, q_h[here])
        out[here] = out_flip.T.astype(BF)
        q_rows = q_flip.T * scale
        q_back = (
            q_rows * rot[0, here]
            - pltpu.roll(q_rows, 128 - ROT_DIM // 2, 1) * rot[1, here]
            - pltpu.roll(q_rows, ROT_DIM // 2, 1) * rot[2, here]
        )
        q_grad[here] = q_back.astype(BF)
    k_grad[...] = turn(k_acc[...], -1.0).astype(BF)
    v_grad[...] = v_acc[...].astype(BF)
    for total_out, rows_out in ((q_sum, q_grad), (k_sum, k_grad), (v_sum, v_grad)):
        total_out[...] = jnp.sum(rows_out[...].astype(F32), axis=0, keepdims=True)


def rotary_lanes(length):
    half_dim = ROT_DIM // 2
    lane = jnp.arange(128) % HEAD_DIM
    frequency = 10000.0 ** (-jnp.arange(half_dim).astype(F32) * 2.0 / ROT_DIM)
    angles = jnp.arange(length).astype(F32)[:, None] * frequency[None, :]
    cosine = jnp.tile(jnp.cos(angles), (1, 128 // half_dim))
    sine = jnp.tile(jnp.sin(angles), (1, 128 // half_dim))
    turned = lane[None, :] < ROT_DIM
    first = lane[None, :] < half_dim
    return jnp.stack(
        [
            jnp.where(turned, cosine, 1.0),
            jnp.where(first, -sine, 0.0),
            jnp.where(turned & ~first, sine, 0.0),
        ]
    )


def attention(projected, out_grad, start):
    length, width = out_grad.shape
    pairs = width // 128
    shape = jax.ShapeDtypeStruct

    def rows(shift):
        return pl.BlockSpec((length, 128), lambda i: (0, i + shift))

    total = pl.BlockSpec((1, 128), lambda i: (0, i))
    return pl.pallas_call(
        attention_kernel,
        grid=(pairs,),
        in_specs=[
            pl.BlockSpec(memory_space=pltpu.SMEM),
            rows(0),
            rows(pairs),
            rows(2 * pairs),
            rows(0),
            pl.BlockSpec((3, length, 128), lambda i: (0, 0, 0)),
        ],
        out_specs=[rows(0)] * 4 + [total] * 3,
        out_shape=[shape((length, width), BF)] * 4 + [shape((1, width), F32)] * 3,
        scratch_shapes=[
            pltpu.VMEM((length // 256, 512, 256), F32),
            pltpu.VMEM((length, 128), F32),
            pltpu.VMEM((length, 128), F32),
        ],
        compiler_params=pltpu.CompilerParams(vmem_limit_bytes=50 << 20),
        cost_estimate=pl.CostEstimate(
            flops=16 * length * length * width, bytes_accessed=16 * length * width, transcendentals=length * length * width // 64
        ),
        name="attention",
    )(start, projected, projected, projected, out_grad, rotary_lanes(length))


def sums_kernel(dp_size, mp_size, every, group, every_out, group_out, first, second, send_1, recv_1, send_2, recv_2):
    me, z, c, mp = place()
    split = every.shape[0]
    bar = pltpu.get_barrier_semaphore()
    for k in range(1, mp_size):
        pl.semaphore_signal(bar, 1, device_id=(me, lax.rem(mp + k, mp_size)), device_id_type=MESH)
    for k in range(1, dp_size):
        pl.semaphore_signal(bar, 1, device_id=(lax.rem(me + k, dp_size), mp), device_id_type=MESH)
    pl.semaphore_wait(bar, mp_size + dp_size - 2)

    def copy_1(k):
        return remote(
            every, first.at[mp], send_1.at[k], recv_1.at[mp], me, lax.rem(mp + k, mp_size)
        )

    def copy_2(k):
        return remote(
            second.at[me], second.at[me], send_2.at[k], recv_2.at[me], lax.rem(me + k, dp_size), mp
        )

    for k in range(1, mp_size):
        copy_1(k).start()
    first[mp] = every[...]
    second[me, split:] = group[...]
    for k in range(1, mp_size):
        origin = lax.rem(mp + k, mp_size)
        remote(every, first.at[origin], send_1.at[0], recv_1.at[origin], me, origin).wait_recv()
    total = first[0]
    for k in range(1, mp_size):
        total = total + first[k]
    second[me, :split] = total
    for k in range(1, dp_size):
        copy_2(k).start()
    for k in range(1, dp_size):
        origin = lax.rem(me + k, dp_size)
        remote(second.at[origin], second.at[origin], send_2.at[0], recv_2.at[origin], origin, mp).wait_recv()
    total = second[0]
    for k in range(1, dp_size):
        total = total + second[k]
    every_out[...] = total[:split]
    group_out[...] = total[split:]
    for k in range(1, mp_size):
        copy_1(k).wait_send()
    for k in range(1, dp_size):
        copy_2(k).wait_send()


def tiled(vectors):
    flat = jnp.concatenate([v.reshape(-1) for v in vectors])
    return jnp.pad(flat, (0, -flat.shape[0] % 1024)).reshape(-1, 128)


def untiled(table, vectors):
    flat, place_at, parts = table.reshape(-1), 0, []
    for v in vectors:
        parts.append(flat[place_at : place_at + v.size].reshape(v.shape))
        place_at += v.size
    return parts


def all_sums(dp_size, mp_size, every, group):
    one, two = tiled(every), tiled(group)
    shape = jax.ShapeDtypeStruct
    totals = pl.pallas_call(
        partial(sums_kernel, dp_size, mp_size),
        out_shape=(shape(one.shape, F32), shape(two.shape, F32)),
        in_specs=[VM] * 2,
        out_specs=[VM] * 2,
        scratch_shapes=[
            pltpu.VMEM((mp_size, *one.shape), F32),
            pltpu.VMEM((dp_size, one.shape[0] + two.shape[0], 128), F32),
            *[pltpu.SemaphoreType.DMA((n,)) for n in (mp_size, mp_size, dp_size, dp_size)],
        ],
        compiler_params=pltpu.CompilerParams(collective_id=2, has_side_effects=True),
        name="all_sums",
    )(one, two)
    return untiled(totals[0], every), untiled(totals[1], group)


def right_product(left_side, right_side):
    return lax.dot_general(
        left_side, right_side, (((1,), (1,)), ((), ())), preferred_element_type=jnp.float32
    )


def rows_product(left_side, right_side):
    return lax.dot_general(
        left_side, right_side, (((0,), (0,)), ((), ())), preferred_element_type=jnp.float32
    )


def low_scatter(partial_sums, axis):
    return lax.psum_scatter(
        partial_sums.astype(jnp.bfloat16), axis, scatter_dimension=0, tiled=True
    ).astype(jnp.float32)


def body(
    tokens,
    ln_gain,
    ln_bias,
    qkv_weight,
    qkv_bias,
    dense_weight,
    dense_bias,
    fc1_weight,
    fc1_bias,
    fc2_weight,
    fc2_bias,
    starts,
    cotangent,
):
    token_float = tokens.astype(jnp.float32)
    dp_size, mp_size = lax.axis_size("dp"), lax.axis_size("mp")
    x_all, cot_all, up_all, hidden_all, slope_all = up_stage(
        dp_size, mp_size, tokens, ln_gain, ln_bias, cotangent, fc1_weight, fc1_bias
    )
    gathered = x_all.reshape(-1, x_all.shape[-1])
    out_rows = cot_all.reshape(gathered.shape)
    up_full = up_all.reshape(-1, up_all.shape[-1])
    hidden_low = hidden_all.reshape(-1, up_all.shape[-1])
    slope = slope_all.reshape(hidden_low.shape)
    masters = (
        qkv_weight.astype(jnp.bfloat16),
        dense_weight.astype(jnp.bfloat16),
        fc2_weight.astype(jnp.bfloat16),
    )
    qkv_full, dense_full, down_full = (
        lax.all_gather(masters[0], "dp", axis=0, tiled=True),
        lax.all_gather(masters[1], "dp", axis=0, tiled=True),
        lax.all_gather(masters[2], "dp", axis=0, tiled=True),
    )
    model_width = qkv_full.shape[0]
    local_width = qkv_full.shape[2]
    projected = jnp.dot(
        gathered, qkv_full.reshape(model_width, 3 * local_width), preferred_element_type=jnp.float32
    ) + qkv_bias.reshape(3 * local_width)
    attended_grad = jnp.dot(out_rows, dense_full, preferred_element_type=jnp.float32).astype(
        jnp.bfloat16
    )
    attended, query_grad, key_grad, value_grad, query_sum, key_sum, value_sum = attention(
        projected, attended_grad, starts
    )
    attn_part = right_product(attended, dense_full)
    mlp_part = right_product(hidden_low, down_full)
    mixed_sum = low_scatter(attn_part + mlp_part, "mp")
    output = (token_float + mixed_sum + dense_bias + fc2_bias).astype(jnp.bfloat16)
    dense_grad = rows_product(out_rows, attended)
    down_grad = rows_product(out_rows, hidden_low)
    hidden_grad = jnp.dot(out_rows, down_full, preferred_element_type=jnp.float32)
    pre_grad = (hidden_grad * slope).astype(jnp.bfloat16)
    up_grad = rows_product(gathered, pre_grad)
    up_bias_grad = jnp.sum(pre_grad.astype(jnp.float32), axis=0)
    projected_grad = jnp.concatenate([query_grad, key_grad, value_grad], axis=1)
    qkv_grad = rows_product(gathered, projected_grad).reshape(model_width, 3, local_width)
    qkv_bias_grad = jnp.concatenate([query_sum, key_sum, value_sum], axis=0)
    attn_input = right_product(projected_grad, qkv_full.reshape(model_width, 3 * local_width))
    mlp_input = right_product(pre_grad, up_full)
    normed_grad = low_scatter(attn_input + mlp_input, "mp")
    norm_value, norm_back = jax.vjp(normalize, token_float, ln_gain, ln_bias)
    token_grad, gain_grad, shift_grad = norm_back(normed_grad)
    cot_float = cotangent.astype(jnp.float32)
    input_grad = (cot_float + token_grad).astype(jnp.bfloat16)
    out_bias_grad = jnp.sum(cot_float, axis=0)
    (gain_total, shift_total, bias_total), (qkv_bias_total, up_bias_total) = all_sums(
        dp_size, mp_size, (gain_grad, shift_grad, out_bias_grad), (qkv_bias_grad, up_bias_grad)
    )
    qkv_share, dense_share, up_share, down_share = (
        low_scatter(qkv_grad, "dp"),
        low_scatter(dense_grad, "dp"),
        low_scatter(up_grad, "dp"),
        low_scatter(down_grad, "dp"),
    )
    return (
        output,
        input_grad,
        gain_total,
        shift_total,
        qkv_share,
        qkv_bias_total,
        dense_share,
        bias_total,
        up_share,
        up_bias_total,
        down_share,
        bias_total,
    )


def solution(mesh):
    in_specs = (
        P(("dp", "mp"), None),
        P(),
        P(),
        P("dp", None, "mp"),
        P(None, "mp"),
        P("dp", "mp"),
        P(),
        P("dp", "mp"),
        P("mp"),
        P("dp", "mp"),
        P(),
        P("dp"),
        P(("dp", "mp"), None),
    )
    out_specs = (
        P(("dp", "mp"), None),
        P(("dp", "mp"), None),
        P(),
        P(),
        P("dp", None, "mp"),
        P(None, "mp"),
        P("dp", "mp"),
        P(),
        P("dp", "mp"),
        P("mp"),
        P("dp", "mp"),
        P(),
    )
    return jax.shard_map(body, mesh=mesh, in_specs=in_specs, out_specs=out_specs, check_vma=False)
```

```python
from functools import partial

import jax
import jax.numpy as jnp
from jax import lax
from jax.experimental import pallas as pl
from jax.experimental.pallas import tpu as pltpu
from jax.sharding import PartitionSpec as P

HEAD_DIM = 64
ROT_DIM = 32
LENGTH = 1024
PIECE = 256
EPSILON = 1e-05
NEGATIVE = -1e30
MESH = pl.DeviceIdType.MESH
BF = jnp.bfloat16
F32 = jnp.float32
ANY = pl.BlockSpec(memory_space=pl.ANY)
VM = pl.BlockSpec(memory_space=pltpu.VMEM)


def dot(a, b, ca=1, cb=0):
    return lax.dot_general(a, b, (((ca,), (cb,)), ((), ())), preferred_element_type=F32)


def remote(src, dst, send, recv, dp_index, mp_index):
    return pltpu.make_async_remote_copy(
        src_ref=src,
        dst_ref=dst,
        send_sem=send,
        recv_sem=recv,
        device_id=(dp_index, mp_index),
        device_id_type=MESH,
    )


def place():
    me = lax.axis_index("dp")
    return me, me // 2, lax.rem(me, 2), lax.axis_index("mp")


def greet(chips, mp_size):
    me, z, c, mp = place()
    bar = pltpu.get_barrier_semaphore()
    pl.semaphore_signal(bar, 1, device_id=(2 * z + 1 - c, mp), device_id_type=MESH)

    @pl.when(z > 0)
    def _():
        pl.semaphore_signal(bar, 1, device_id=(me - 2, mp), device_id_type=MESH)

    @pl.when(z < chips - 1)
    def _():
        pl.semaphore_signal(bar, 1, device_id=(me + 2, mp), device_id_type=MESH)

    for k in range(1, mp_size):
        pl.semaphore_signal(
            bar, 1, device_id=(me, lax.rem(mp + k, mp_size)), device_id_type=MESH
        )
    count = mp_size + jnp.where(z > 0, 1, 0) + jnp.where(z < chips - 1, 1, 0)
    pl.semaphore_wait(bar, count)


class RowGather:
    def __init__(self, chips, own, full, sems):
        self.chips, self.own, self.full = chips, own, full
        self.recv, self.left, self.right, self.side = sems

    def copies(self, oz):
        me, z, c, mp = place()
        b = 2 * oz + c
        dst = self.full.at[b]

        def make(src, send, target):
            return remote(src, dst, send.at[oz], self.recv.at[b], target, mp)

        return (
            lambda src: make(src, self.left, me - 2),
            lambda src: make(src, self.right, me + 2),
            lambda src: make(src, self.side, 2 * z + 1 - c),
        )

    def start(self):
        me, z, c, mp = place()
        left, right, side = self.copies(z)

        @pl.when(z > 0)
        def _():
            left(self.own).start()

        @pl.when(z < self.chips - 1)
        def _():
            right(self.own).start()

        side(self.own).start()

    def wait_block(self, b):
        me, z, c, mp = place()
        remote(self.full.at[b], self.full.at[b], self.side.at[0], self.recv.at[b], me, mp).wait_recv()

    def stage(self, k):
        me, z, c, mp = place()

        @pl.when(z + k < self.chips)
        def _():
            oz = z + k
            self.wait_block(2 * oz + c)
            left, right, side = self.copies(oz)

            @pl.when(z > 0)
            def _():
                left(self.full.at[2 * oz + c]).start()

            side(self.full.at[2 * oz + c]).start()

        @pl.when(z - k >= 0)
        def _():
            oz = z - k
            self.wait_block(2 * oz + c)
            left, right, side = self.copies(oz)

            @pl.when(z < self.chips - 1)
            def _():
                right(self.full.at[2 * oz + c]).start()

            side(self.full.at[2 * oz + c]).start()

    def drain(self):
        me, z, c, mp = place()
        for oz in range(self.chips):
            left, right, side = self.copies(oz)

            @pl.when((z > 0) & (oz >= z))
            def _():
                left(self.full.at[2 * oz + c]).wait_send()

            @pl.when((z < self.chips - 1) & (oz <= z))
            def _():
                right(self.full.at[2 * oz + c]).wait_send()

            side(self.full.at[2 * oz + c]).wait_send()


class GroupGather:
    def __init__(self, size, own, full, sems):
        self.size, self.own, self.full = size, own, full
        self.send, self.recv = sems
        self.half = full.shape[1] // 2

    def to(self, src, origin, part, slot, target):
        me, z, c, mp = place()
        rows = self.full.at[origin] if part is None else self.full.at[origin, pl.ds(part * self.half, self.half)]
        sem = self.recv.at[origin, 0 if part is None else part]
        return remote(src, rows, self.send.at[slot], sem, me, target)

    def start(self):
        me, z, c, mp = place()
        for slot, peer in self.peers():
            self.to(self.own, mp, None, slot, peer).start()

    def peers(self):
        me, z, c, mp = place()
        if self.size == 4:
            x_peer = mp + 1 - 2 * lax.rem(mp, 2)
            return ((0, x_peer), (1, lax.rem(mp + 2, 4)))
        return tuple((k - 1, lax.rem(mp + k, self.size)) for k in range(1, self.size))

    def relays(self):
        (_, x_peer), (_, y_peer) = self.peers()
        return (
            self.to(self.full.at[x_peer, pl.ds(0, self.half)], x_peer, 0, 2, y_peer),
            self.to(self.full.at[y_peer, pl.ds(self.half, self.half)], y_peer, 1, 3, x_peer),
        )

    def relay(self):
        for slot, peer in self.peers():
            self.to(self.full.at[peer], peer, None, slot, peer).wait_recv()
        if self.size == 4:
            for copy in self.relays():
                copy.start()

    def finish(self):
        me, z, c, mp = place()
        if self.size == 4:
            far = 3 - mp
            for part in (0, 1):
                rows = self.full.at[far, pl.ds(part * self.half, self.half)]
                self.to(rows, far, part, 0, mp).wait_recv()

    def drain(self):
        me, z, c, mp = place()
        for slot, peer in self.peers():
            self.to(self.own, mp, None, slot, peer).wait_send()
        if self.size == 4:
            for copy in self.relays():
                copy.wait_send()


def row_gather_sems(dp_size):
    chips = dp_size // 2
    return [pltpu.SemaphoreType.DMA((n,)) for n in (dp_size, chips, chips, chips)]


def group_gather_sems(mp_size):
    return [pltpu.SemaphoreType.DMA((max(4, mp_size - 1),)), pltpu.SemaphoreType.DMA((mp_size, 2))]


def gelu_pair(v):
    k0, k1 = 0.7978845608028654, 0.044715
    square = v * v
    t = jnp.tanh(k0 * (v + k1 * v * square))
    half = 0.5 * (1.0 + t)
    slope = half + 0.5 * v * (1.0 - t * t) * (k0 + 3.0 * k0 * k1 * square)
    return v * half, slope


def up_kernel(
    dp_size,
    mp_size,
    tokens,
    gain,
    shift,
    cot,
    up_master,
    up_bias,
    x_out,
    cot_out,
    up_out,
    hidden_out,
    slope_out,
    x_all,
    up_all,
    acc,
    hidden,
    slope,
    *sems,
):
    chips = dp_size // 2
    row_sems, x_sems, cot_sems = sems[0:4], sems[4:6], sems[6:8]
    out_sem = sems[8]
    me, z, c, mp = place()
    rows = tokens.shape[0]
    length = rows * mp_size
    depth, width = up_all.shape[1], up_all.shape[2]

    values = tokens[...].astype(F32)
    centre = values - jnp.mean(values, axis=-1, keepdims=True)
    spread = jnp.mean(centre * centre, axis=-1, keepdims=True)
    x_all[mp] = (centre * lax.rsqrt(spread + EPSILON) * gain[...] + shift[...]).astype(BF)
    up_all[me] = up_master[...].astype(BF)

    greet(chips, mp_size)
    weights = RowGather(chips, up_all.at[me], up_all, row_sems)
    x_gather = GroupGather(mp_size, x_all.at[mp], x_all, x_sems)
    cot_gather = GroupGather(mp_size, cot, cot_out, cot_sems)
    x_gather.start()
    weights.start()
    own_cot = pltpu.make_async_copy(cot, cot_out.at[mp], out_sem.at[0])
    own_cot.start()

    def product(oz, first=False):
        cols = pl.ds(pl.multiple_of(oz * (2 * depth), 2 * depth), 2 * depth)

        def tile(i, carry):
            r, n = i // (width // 512), lax.rem(i, width // 512)
            n0 = pl.ds(pl.multiple_of(n * 512, 512), 512)
            left = x_all[r, :, cols]
            right = up_all[pl.ds(2 * oz, 2), :, n0].reshape(2 * depth, 512)
            term = dot(left, right)
            if first:
                acc[r, :, n0] = term + up_bias[:, n0]
            else:
                acc[r, :, n0] += term
            return carry

        lax.fori_loop(0, mp_size * (width // 512), tile, 0)

    x_gather.relay()
    x_gather.finish()
    weights.stage(1)
    cot_gather.start()
    x_copy = pltpu.make_async_copy(x_all, x_out, out_sem.at[1])
    x_copy.start()
    weights.wait_block(2 * z + 1 - c)
    product(z, True)
    for k in range(1, chips):
        if k > 1:
            weights.stage(k)
        for oz, valid in ((z + k, z + k < chips), (z - k, z - k >= 0)):

            @pl.when(valid)
            def _():
                weights.wait_block(2 * oz + 1 - c)
                product(oz)

        if k == min(2, chips - 1):
            cot_gather.relay()
    up_copy = pltpu.make_async_copy(up_all, up_out, out_sem.at[2])
    up_copy.start()

    def finish(i, carry):
        r, n = i // (width // 512), lax.rem(i, width // 512)
        n0 = pl.ds(pl.multiple_of(n * 512, 512), 512)
        high, grad = gelu_pair(acc[r, :, n0])
        hidden[r, :, n0] = high.astype(BF)
        slope[r, :, n0] = grad.astype(BF)
        return carry

    lax.fori_loop(0, mp_size * (width // 512), finish, 0)
    hidden_copy = pltpu.make_async_copy(hidden, hidden_out, out_sem.at[3])
    slope_copy = pltpu.make_async_copy(slope, slope_out, out_sem.at[4])
    hidden_copy.start()
    slope_copy.start()
    cot_gather.finish()
    weights.drain()
    x_gather.drain()
    cot_gather.drain()
    for copy in (own_cot, x_copy, up_copy, hidden_copy, slope_copy):
        copy.wait()


def up_stage(dp_size, mp_size, tokens, gain, shift, cot, up_master, up_bias):
    rows, model = tokens.shape
    depth, width = up_master.shape
    shape = jax.ShapeDtypeStruct
    outs = (
        shape((mp_size, rows, model), BF),
        shape((mp_size, rows, model), BF),
        shape((dp_size, depth, width), BF),
        shape((mp_size, rows, width), BF),
        shape((mp_size, rows, width), BF),
    )
    return pl.pallas_call(
        partial(up_kernel, dp_size, mp_size),
        out_shape=outs,
        in_specs=[VM] * 6,
        out_specs=[ANY] * 5,
        scratch_shapes=[
            pltpu.VMEM((mp_size, rows, model), BF),
            pltpu.VMEM((dp_size, depth, width), BF),
            pltpu.VMEM((mp_size, rows, width), F32),
            pltpu.VMEM((mp_size, rows, width), BF),
            pltpu.VMEM((mp_size, rows, width), BF),
            *row_gather_sems(dp_size),
            *group_gather_sems(mp_size),
            *group_gather_sems(mp_size),
            pltpu.SemaphoreType.DMA((5,)),
        ],
        compiler_params=pltpu.CompilerParams(
            collective_id=1, has_side_effects=True, vmem_limit_bytes=58 << 20
        ),
        name="up_stage",
    )(tokens, gain.reshape(1, -1), shift.reshape(1, -1), cot, up_master, up_bias.reshape(1, -1))


def normalize(values, gain_vec, shift_vec):
    centre = values - jnp.mean(values, axis=-1, keepdims=True)
    spread = jnp.mean(centre * centre, axis=-1, keepdims=True)
    scaled = centre * lax.rsqrt(spread + EPSILON)
    return scaled * gain_vec + shift_vec


def attention_kernel(start, q_in, k_in, v_in, out_grad, rot, out, q_grad, k_grad, v_grad, q_sum, k_sum, v_sum, bias, k_acc, v_acc):
    length = q_in.shape[0]
    block = 256
    blocks = length // block

    @pl.when(pl.program_id(0) == 0)
    def _():
        first = start[0]
        for i in range(blocks):
            high = min(length, block * (i + 2)) - block * i
            keys = block * i + lax.broadcasted_iota(jnp.int32, (high, block), 0)
            places = block * i + lax.broadcasted_iota(jnp.int32, (high, block), 1)
            inside = (keys >= first) & (keys < first + PIECE) & (places >= first) & (places < first + PIECE)
            bias[i, :high] = jnp.where((keys <= places) | inside, 0.0, NEGATIVE)

    def turn(values, sign):
        return (
            values * rot[0]
            + sign * (pltpu.roll(values, 128 - ROT_DIM // 2, 1) * rot[1] + pltpu.roll(values, ROT_DIM // 2, 1) * rot[2])
        )

    scale = HEAD_DIM ** (-0.5)
    q_low = (turn(q_in[...], 1.0).astype(BF).astype(F32) * scale).astype(BF)
    k_low = turn(k_in[...], 1.0).astype(BF)
    v_low = v_in[...].astype(BF)
    grad = out_grad[...]
    k_flip, v_flip = k_low.T, v_low.T
    lane = lax.broadcasted_iota(jnp.int32, (length, 128), 1) < HEAD_DIM
    row = lax.broadcasted_iota(jnp.int32, (128, length), 0) < HEAD_DIM
    zero = jnp.zeros((), BF)
    k_acc[...] = jnp.zeros_like(k_acc)
    v_acc[...] = jnp.zeros_like(v_acc)
    heads = []
    for h in range(2):
        lanes, rows = (lane, row) if h == 0 else (~lane, ~row)
        heads.append(
            (
                jnp.where(lanes, q_low, zero),
                jnp.where(lanes, k_low, zero),
                jnp.where(lanes, v_low, zero),
                jnp.where(lanes, grad, zero),
                jnp.where(rows, k_flip, zero),
                jnp.where(rows, v_flip, zero),
            )
        )
    for i in range(blocks):
        here = slice(block * i, block * (i + 1))
        stop = min(length, block * (i + 2))
        parts = [(0, block * i)] if i else []
        parts.append((block * i, stop))
        out_flip = jnp.zeros((128, block), F32)
        q_flip = jnp.zeros((128, block), F32)
        for q_h, k_h, v_h, grad_h, kt_h, vt_h in heads:
            scores = [dot(k_h[a:b], q_low[here], 1, 1) for a, b in parts]
            scores[-1] = scores[-1] + bias[i, : stop - block * i]
            top = scores[-1].max(0, keepdims=True)
            for s in scores[:-1]:
                top = jnp.maximum(top, s.max(0, keepdims=True))
            expo = [jnp.exp(s - top) for s in scores]
            total = expo[0].sum(0, keepdims=True)
            for e in expo[1:]:
                total = total + e.sum(0, keepdims=True)
            share = 1.0 / total
            probs = [e * share for e in expo]
            grads = [dot(v_h[a:b], grad[here], 1, 1) for a, b in parts]
            inner = (probs[0] * grads[0]).sum(0, keepdims=True)
            for p, g in zip(probs[1:], grads[1:]):
                inner = inner + (p * g).sum(0, keepdims=True)
            for (a, b), p, g in zip(parts, probs, grads):
                p_low = p.astype(BF)
                s_grad = (p * (g - inner)).astype(BF)
                out_flip = out_flip + dot(vt_h[:, a:b], p_low)
                q_flip = q_flip + dot(kt_h[:, a:b], s_grad)
                v_acc[a:b] += dot(p_low, grad_h[here])
                k_acc[a:b] += dot(s_grad, q_h[here])
        out[here] = out_flip.T.astype(BF)
        q_rows = q_flip.T * scale
        q_back = (
            q_rows * rot[0, here]
            - pltpu.roll(q_rows, 128 - ROT_DIM // 2, 1) * rot[1, here]
            - pltpu.roll(q_rows, ROT_DIM // 2, 1) * rot[2, here]
        )
        q_grad[here] = q_back.astype(BF)
    k_grad[...] = turn(k_acc[...], -1.0).astype(BF)
    v_grad[...] = v_acc[...].astype(BF)
    for total_out, rows_out in ((q_sum, q_grad), (k_sum, k_grad), (v_sum, v_grad)):
        total_out[...] = jnp.sum(rows_out[...].astype(F32), axis=0, keepdims=True)


def rotary_lanes(length):
    half_dim = ROT_DIM // 2
    lane = jnp.arange(128) % HEAD_DIM
    frequency = 10000.0 ** (-jnp.arange(half_dim).astype(F32) * 2.0 / ROT_DIM)
    angles = jnp.arange(length).astype(F32)[:, None] * frequency[None, :]
    cosine = jnp.tile(jnp.cos(angles), (1, 128 // half_dim))
    sine = jnp.tile(jnp.sin(angles), (1, 128 // half_dim))
    turned = lane[None, :] < ROT_DIM
    first = lane[None, :] < half_dim
    return jnp.stack(
        [
            jnp.where(turned, cosine, 1.0),
            jnp.where(first, -sine, 0.0),
            jnp.where(turned & ~first, sine, 0.0),
        ]
    )


def attention(projected, out_grad, start):
    length, width = out_grad.shape
    pairs = width // 128
    shape = jax.ShapeDtypeStruct

    def rows(shift):
        return pl.BlockSpec((length, 128), lambda i: (0, i + shift))

    total = pl.BlockSpec((1, 128), lambda i: (0, i))
    return pl.pallas_call(
        attention_kernel,
        grid=(pairs,),
        in_specs=[
            pl.BlockSpec(memory_space=pltpu.SMEM),
            rows(0),
            rows(pairs),
            rows(2 * pairs),
            rows(0),
            pl.BlockSpec((3, length, 128), lambda i: (0, 0, 0)),
        ],
        out_specs=[rows(0)] * 4 + [total] * 3,
        out_shape=[shape((length, width), BF)] * 4 + [shape((1, width), F32)] * 3,
        scratch_shapes=[
            pltpu.VMEM((length // 256, 512, 256), F32),
            pltpu.VMEM((length, 128), F32),
            pltpu.VMEM((length, 128), F32),
        ],
        compiler_params=pltpu.CompilerParams(vmem_limit_bytes=50 << 20),
        cost_estimate=pl.CostEstimate(
            flops=16 * length * length * width, bytes_accessed=16 * length * width, transcendentals=length * length * width // 64
        ),
        name="attention",
    )(start, projected, projected, projected, out_grad, rotary_lanes(length))


def sums_kernel(dp_size, mp_size, every, group, every_out, group_out, first, second, send_1, recv_1, send_2, recv_2):
    me, z, c, mp = place()
    split = every.shape[0]
    bar = pltpu.get_barrier_semaphore()
    for k in range(1, mp_size):
        pl.semaphore_signal(bar, 1, device_id=(me, lax.rem(mp + k, mp_size)), device_id_type=MESH)
    for k in range(1, dp_size):
        pl.semaphore_signal(bar, 1, device_id=(lax.rem(me + k, dp_size), mp), device_id_type=MESH)
    pl.semaphore_wait(bar, mp_size + dp_size - 2)

    def copy_1(k):
        return remote(
            every, first.at[mp], send_1.at[k], recv_1.at[mp], me, lax.rem(mp + k, mp_size)
        )

    def copy_2(k):
        return remote(
            second.at[me], second.at[me], send_2.at[k], recv_2.at[me], lax.rem(me + k, dp_size), mp
        )

    for k in range(1, mp_size):
        copy_1(k).start()
    first[mp] = every[...]
    second[me, split:] = group[...]
    for k in range(1, mp_size):
        origin = lax.rem(mp + k, mp_size)
        remote(every, first.at[origin], send_1.at[0], recv_1.at[origin], me, origin).wait_recv()
    total = first[0]
    for k in range(1, mp_size):
        total = total + first[k]
    second[me, :split] = total
    for k in range(1, dp_size):
        copy_2(k).start()
    for k in range(1, dp_size):
        origin = lax.rem(me + k, dp_size)
        remote(second.at[origin], second.at[origin], send_2.at[0], recv_2.at[origin], origin, mp).wait_recv()
    total = second[0]
    for k in range(1, dp_size):
        total = total + second[k]
    every_out[...] = total[:split]
    group_out[...] = total[split:]
    for k in range(1, mp_size):
        copy_1(k).wait_send()
    for k in range(1, dp_size):
        copy_2(k).wait_send()


def tiled(vectors):
    flat = jnp.concatenate([v.reshape(-1) for v in vectors])
    return jnp.pad(flat, (0, -flat.shape[0] % 1024)).reshape(-1, 128)


def untiled(table, vectors):
    flat, place_at, parts = table.reshape(-1), 0, []
    for v in vectors:
        parts.append(flat[place_at : place_at + v.size].reshape(v.shape))
        place_at += v.size
    return parts


def all_sums(dp_size, mp_size, every, group):
    one, two = tiled(every), tiled(group)
    shape = jax.ShapeDtypeStruct
    totals = pl.pallas_call(
        partial(sums_kernel, dp_size, mp_size),
        out_shape=(shape(one.shape, F32), shape(two.shape, F32)),
        in_specs=[VM] * 2,
        out_specs=[VM] * 2,
        scratch_shapes=[
            pltpu.VMEM((mp_size, *one.shape), F32),
            pltpu.VMEM((dp_size, one.shape[0] + two.shape[0], 128), F32),
            *[pltpu.SemaphoreType.DMA((n,)) for n in (mp_size, mp_size, dp_size, dp_size)],
        ],
        compiler_params=pltpu.CompilerParams(collective_id=2, has_side_effects=True),
        name="all_sums",
    )(one, two)
    return untiled(totals[0], every), untiled(totals[1], group)


class RowScatter:
    pieces = 2

    def __init__(self, chips, left, rights, flip, give, part, land, sems):
        self.chips, self.left, self.rights, self.flip = chips, left, rights, flip
        self.give, self.part, self.land = give, part, land
        self.sib_send, self.sib_recv, self.send_l, self.send_r, self.recv = sems
        self.depth = part.shape[1]

    def target(self, p):
        me, z, c, mp = place()
        s, side = p // 2, lax.rem(p, 2)
        far = self.chips - 1
        t = jnp.where(side == 0, z + s - far, z - s + far)
        return t, (t >= 0) & (t < self.chips)

    def block(self, t, core, store):
        b = 2 * t + core
        cols = pl.ds(pl.multiple_of(b * self.depth, self.depth), self.depth)
        self.flip[...] = self.left[:, cols].T
        place_at = 0
        for right in self.rights:
            tile = min(512, right.shape[1])
            for n in range(0, right.shape[1], tile):
                store(slice(place_at + n, place_at + n + tile), dot(self.flip[...], right[:, n : n + tile]))
            place_at += right.shape[1]

    def sibling(self, t):
        me, z, c, mp = place()
        return remote(
            self.give.at[t], self.part.at[t], self.sib_send.at[t], self.sib_recv.at[t], 2 * z + 1 - c, mp
        )

    def rows(self, q):
        return pl.ds(q * (self.depth // self.pieces), self.depth // self.pieces)

    def to_left(self, t, q):
        me, z, c, mp = place()
        r = self.rows(q)
        return remote(
            self.part.at[t, r], self.land.at[t, r], self.send_l.at[t, q], self.recv.at[t, q], me - 2, mp
        )

    def to_right(self, t, q):
        me, z, c, mp = place()
        r = self.rows(q)
        slot = jnp.where(t > z + 1, t, self.chips)
        return remote(
            self.part.at[t, r], self.land.at[slot, r], self.send_r.at[t, q], self.recv.at[slot, q], me + 2, mp
        )

    def landed(self, slot, q):
        me, z, c, mp = place()
        here = self.land.at[slot, self.rows(q)]
        remote(here, here, self.send_l.at[0, 0], self.recv.at[slot, q], me, mp).wait_recv()

    def swap(self):
        me, z, c, mp = place()

        def step(p, carry):
            t, valid = self.target(p)

            @pl.when(valid)
            def _():
                def store(cols, values):
                    self.give[t, :, cols] = values.astype(BF)

                self.block(t, 1 - c, store)
                self.sibling(t).start()

            return carry

        lax.fori_loop(0, 2 * self.chips - 1, step, 0)

    def collect(self):
        me, z, c, mp = place()
        last = self.chips - 1

        def step(p, carry):
            t, valid = self.target(p)

            @pl.when(valid)
            def _():
                self.sibling(t).wait_recv()

                def store(cols, values):
                    self.part[t, :, cols] = (values + self.part[t, :, cols].astype(F32)).astype(BF)

                self.block(t, c, store)

                @pl.when((t < z) & (z == last))
                def _():
                    for q in range(self.pieces):
                        self.to_left(t, q).start()

                @pl.when((t > z) & (z == 0))
                def _():
                    for q in range(self.pieces):
                        self.to_right(t, q).start()

            return carry

        lax.fori_loop(0, 2 * self.chips - 1, step, 0)

    def add(self, t, slot, q):
        r = self.rows(q)
        self.landed(slot, q)
        self.part[t, r] = (self.part[t, r].astype(F32) + self.land[slot, r].astype(F32)).astype(BF)

    def relay(self, s):
        me, z, c, mp = place()
        last = self.chips - 1
        for q in range(self.pieces):
            t = z + s - last

            @pl.when((t >= 0) & (z < last))
            def _():
                self.add(t, t, q)
                self.to_left(t, q).start()

            u = z - s + last

            @pl.when((u <= last) & (z > 0))
            def _():
                self.add(u, u, q)
                self.to_right(u, q).start()

    def finish(self, result):
        me, z, c, mp = place()
        for q in range(self.pieces):
            r = self.rows(q)
            result[r] = self.part[z, r].astype(F32)

            @pl.when(z < self.chips - 1)
            def _():
                self.landed(z, q)
                result[r] += self.land[z, r].astype(F32)

            @pl.when(z > 0)
            def _():
                self.landed(self.chips, q)
                result[r] += self.land[self.chips, r].astype(F32)

    def drain(self):
        me, z, c, mp = place()

        def step(t, carry):
            self.sibling(t).wait_send()
            for q in range(self.pieces):

                @pl.when(t < z)
                def _():
                    self.to_left(t, q).wait_send()

                @pl.when(t > z)
                def _():
                    self.to_right(t, q).wait_send()

            return carry

        lax.fori_loop(0, self.chips, step, 0)


def row_scatter_scratch(chips, depth, width):
    return [
        pltpu.VMEM((chips, depth, width), BF),
        pltpu.VMEM((chips, depth, width), BF),
        pltpu.VMEM((chips + 1, depth, width), BF),
        pltpu.SemaphoreType.DMA((chips,)),
        pltpu.SemaphoreType.DMA((chips,)),
        pltpu.SemaphoreType.DMA((chips, RowScatter.pieces)),
        pltpu.SemaphoreType.DMA((chips, RowScatter.pieces)),
        pltpu.SemaphoreType.DMA((chips + 1, RowScatter.pieces)),
    ]


class GroupScatter:
    def __init__(self, size, parts, land, send, recv):
        self.size, self.parts, self.land, self.send, self.recv = size, parts, land, send, recv

    def copy(self, k):
        me, z, c, mp = place()
        peer = lax.rem(mp + k, self.size)
        return remote(
            self.parts.at[peer], self.land.at[mp], self.send.at[k], self.recv.at[mp], me, peer
        )

    def start(self):
        me, z, c, mp = place()
        for k in range(1, self.size):
            self.copy(k).start()

    def finish(self, result):
        me, z, c, mp = place()
        own = pltpu.make_async_copy(self.parts.at[mp], self.land.at[mp], self.send.at[0])
        own.start()
        own.wait()
        for k in range(1, self.size):
            origin = lax.rem(mp + k, self.size)
            here = self.land.at[origin]
            remote(here, here, self.send.at[0], self.recv.at[origin], me, origin).wait_recv()
        total = self.land[0].astype(F32)
        for k in range(1, self.size):
            total = total + self.land[k].astype(F32)
        result[...] = total

    def drain(self):
        for k in range(1, self.size):
            self.copy(k).wait_send()


def grad_kernel(
    dp_size,
    mp_size,
    x_all,
    query_grad,
    key_grad,
    value_grad,
    pre_grad,
    mixed,
    normed,
    qkv_share,
    up_share,
    mixed_sum,
    normed_sum,
    flip,
    *scratch,
):
    chips = dp_size // 2
    qkv_scratch, up_scratch, rest = scratch[:8], scratch[8:16], scratch[16:]
    qkv = RowScatter(chips, x_all, (query_grad, key_grad, value_grad), flip, *qkv_scratch[:3], qkv_scratch[3:])
    up = RowScatter(chips, x_all, (pre_grad,), flip, *up_scratch[:3], up_scratch[3:])
    normed_group = GroupScatter(mp_size, normed, *rest[:3])
    mixed_group = GroupScatter(mp_size, mixed, *rest[3:6])
    greet(chips, mp_size)
    normed_group.start()
    mixed_group.start()
    qkv.swap()
    qkv.collect()
    up.swap()
    if chips > 2:
        qkv.relay(1)
    up.collect()
    for s in range(2, chips - 1):
        qkv.relay(s)
    qkv.finish(qkv_share)
    for s in range(1, chips - 1):
        up.relay(s)
    normed_group.finish(normed_sum)
    mixed_group.finish(mixed_sum)
    up.finish(up_share)
    for stream in (qkv, up, normed_group, mixed_group):
        stream.drain()


def grad_stage(dp_size, mp_size, x_all, query_grad, key_grad, value_grad, pre_grad, mixed, normed):
    length, model = x_all.shape
    rows = length // mp_size
    depth, chips = model // dp_size, dp_size // 2
    width, hidden = query_grad.shape[1], pre_grad.shape[1]
    shape = jax.ShapeDtypeStruct
    group = [
        pltpu.VMEM((mp_size, rows, model), BF),
        pltpu.SemaphoreType.DMA((mp_size,)),
        pltpu.SemaphoreType.DMA((mp_size,)),
    ]
    return pl.pallas_call(
        partial(grad_kernel, dp_size, mp_size),
        out_shape=(
            shape((depth, 3 * width), F32),
            shape((depth, hidden), F32),
            shape((rows, model), F32),
            shape((rows, model), F32),
        ),
        in_specs=[VM] * 5 + [ANY] * 2,
        out_specs=[VM] * 4,
        scratch_shapes=[
            pltpu.VMEM((depth, length), BF),
            *row_scatter_scratch(chips, depth, 3 * width),
            *row_scatter_scratch(chips, depth, hidden),
            *group,
            *group,
        ],
        compiler_params=pltpu.CompilerParams(
            collective_id=3, has_side_effects=True, vmem_limit_bytes=60 << 20
        ),
        name="grad_stage",
    )(
        x_all,
        query_grad,
        key_grad,
        value_grad,
        pre_grad,
        mixed.astype(BF).reshape(mp_size, rows, model),
        normed.astype(BF).reshape(mp_size, rows, model),
    )


def right_product(left_side, right_side):
    return lax.dot_general(
        left_side, right_side, (((1,), (1,)), ((), ())), preferred_element_type=jnp.float32
    )


def rows_product(left_side, right_side):
    return lax.dot_general(
        left_side, right_side, (((0,), (0,)), ((), ())), preferred_element_type=jnp.float32
    )


def low_scatter(partial_sums, axis):
    return lax.psum_scatter(
        partial_sums.astype(jnp.bfloat16), axis, scatter_dimension=0, tiled=True
    ).astype(jnp.float32)


def body(
    tokens,
    ln_gain,
    ln_bias,
    qkv_weight,
    qkv_bias,
    dense_weight,
    dense_bias,
    fc1_weight,
    fc1_bias,
    fc2_weight,
    fc2_bias,
    starts,
    cotangent,
):
    token_float = tokens.astype(jnp.float32)
    dp_size, mp_size = lax.axis_size("dp"), lax.axis_size("mp")
    x_all, cot_all, up_all, hidden_all, slope_all = up_stage(
        dp_size, mp_size, tokens, ln_gain, ln_bias, cotangent, fc1_weight, fc1_bias
    )
    gathered = x_all.reshape(-1, x_all.shape[-1])
    out_rows = cot_all.reshape(gathered.shape)
    up_full = up_all.reshape(-1, up_all.shape[-1])
    hidden_low = hidden_all.reshape(-1, up_all.shape[-1])
    slope = slope_all.reshape(hidden_low.shape)
    masters = (
        qkv_weight.astype(jnp.bfloat16),
        dense_weight.astype(jnp.bfloat16),
        fc2_weight.astype(jnp.bfloat16),
    )
    qkv_full, dense_full, down_full = (
        lax.all_gather(masters[0], "dp", axis=0, tiled=True),
        lax.all_gather(masters[1], "dp", axis=0, tiled=True),
        lax.all_gather(masters[2], "dp", axis=0, tiled=True),
    )
    model_width = qkv_full.shape[0]
    local_width = qkv_full.shape[2]
    projected = jnp.dot(
        gathered, qkv_full.reshape(model_width, 3 * local_width), preferred_element_type=jnp.float32
    ) + qkv_bias.reshape(3 * local_width)
    attended_grad = jnp.dot(out_rows, dense_full, preferred_element_type=jnp.float32).astype(
        jnp.bfloat16
    )
    attended, query_grad, key_grad, value_grad, query_sum, key_sum, value_sum = attention(
        projected, attended_grad, starts
    )
    attn_part = right_product(attended, dense_full)
    mlp_part = right_product(hidden_low, down_full)
    dense_grad = rows_product(out_rows, attended)
    down_grad = rows_product(out_rows, hidden_low)
    hidden_grad = jnp.dot(out_rows, down_full, preferred_element_type=jnp.float32)
    pre_grad = (hidden_grad * slope).astype(jnp.bfloat16)
    up_bias_grad = jnp.sum(pre_grad.astype(jnp.float32), axis=0)
    projected_grad = jnp.concatenate([query_grad, key_grad, value_grad], axis=1)
    qkv_bias_grad = jnp.concatenate([query_sum, key_sum, value_sum], axis=0)
    attn_input = right_product(projected_grad, qkv_full.reshape(model_width, 3 * local_width))
    mlp_input = right_product(pre_grad, up_full)
    qkv_share, up_share, mixed_sum, normed_grad = grad_stage(
        dp_size,
        mp_size,
        gathered,
        query_grad,
        key_grad,
        value_grad,
        pre_grad,
        attn_part + mlp_part,
        attn_input + mlp_input,
    )
    qkv_share = qkv_share.reshape(-1, 3, local_width)
    output = (token_float + mixed_sum + dense_bias + fc2_bias).astype(jnp.bfloat16)
    norm_value, norm_back = jax.vjp(normalize, token_float, ln_gain, ln_bias)
    token_grad, gain_grad, shift_grad = norm_back(normed_grad)
    cot_float = cotangent.astype(jnp.float32)
    input_grad = (cot_float + token_grad).astype(jnp.bfloat16)
    out_bias_grad = jnp.sum(cot_float, axis=0)
    (gain_total, shift_total, bias_total), (qkv_bias_total, up_bias_total) = all_sums(
        dp_size, mp_size, (gain_grad, shift_grad, out_bias_grad), (qkv_bias_grad, up_bias_grad)
    )
    dense_share = low_scatter(dense_grad, "dp")
    down_share = low_scatter(down_grad, "dp")
    return (
        output,
        input_grad,
        gain_total,
        shift_total,
        qkv_share,
        qkv_bias_total,
        dense_share,
        bias_total,
        up_share,
        up_bias_total,
        down_share,
        bias_total,
    )


def solution(mesh):
    in_specs = (
        P(("dp", "mp"), None),
        P(),
        P(),
        P("dp", None, "mp"),
        P(None, "mp"),
        P("dp", "mp"),
        P(),
        P("dp", "mp"),
        P("mp"),
        P("dp", "mp"),
        P(),
        P("dp"),
        P(("dp", "mp"), None),
    )
    out_specs = (
        P(("dp", "mp"), None),
        P(("dp", "mp"), None),
        P(),
        P(),
        P("dp", None, "mp"),
        P(None, "mp"),
        P("dp", "mp"),
        P(),
        P("dp", "mp"),
        P("mp"),
        P("dp", "mp"),
        P(),
    )
    return jax.shard_map(body, mesh=mesh, in_specs=in_specs, out_specs=out_specs, check_vma=False)
```

```python
from functools import partial

import jax
import jax.numpy as jnp
from jax import lax
from jax.experimental import pallas as pl
from jax.experimental.pallas import tpu as pltpu
from jax.sharding import PartitionSpec as P

HEAD_DIM = 64
ROT_DIM = 32
LENGTH = 1024
PIECE = 256
EPSILON = 1e-05
NEGATIVE = -1e30
MESH = pl.DeviceIdType.MESH
BF = jnp.bfloat16
F32 = jnp.float32
ANY = pl.BlockSpec(memory_space=pl.ANY)
VM = pl.BlockSpec(memory_space=pltpu.VMEM)


def dot(a, b, ca=1, cb=0):
    return lax.dot_general(a, b, (((ca,), (cb,)), ((), ())), preferred_element_type=F32)


def remote(src, dst, send, recv, dp_index, mp_index):
    return pltpu.make_async_remote_copy(
        src_ref=src,
        dst_ref=dst,
        send_sem=send,
        recv_sem=recv,
        device_id=(dp_index, mp_index),
        device_id_type=MESH,
    )


def place():
    me = lax.axis_index("dp")
    return me, me // 2, lax.rem(me, 2), lax.axis_index("mp")


def greet(chips, mp_size):
    me, z, c, mp = place()
    bar = pltpu.get_barrier_semaphore()
    pl.semaphore_signal(bar, 1, device_id=(2 * z + 1 - c, mp), device_id_type=MESH)

    @pl.when(z > 0)
    def _():
        pl.semaphore_signal(bar, 1, device_id=(me - 2, mp), device_id_type=MESH)

    @pl.when(z < chips - 1)
    def _():
        pl.semaphore_signal(bar, 1, device_id=(me + 2, mp), device_id_type=MESH)

    for k in range(1, mp_size):
        pl.semaphore_signal(
            bar, 1, device_id=(me, lax.rem(mp + k, mp_size)), device_id_type=MESH
        )
    count = mp_size + jnp.where(z > 0, 1, 0) + jnp.where(z < chips - 1, 1, 0)
    pl.semaphore_wait(bar, count)


class RowGather:
    def __init__(self, chips, own, full, sems):
        self.chips, self.own, self.full = chips, own, full
        self.recv, self.left, self.right, self.side = sems

    def copies(self, oz):
        me, z, c, mp = place()
        b = 2 * oz + c
        dst = self.full.at[b]

        def make(src, send, target):
            return remote(src, dst, send.at[oz], self.recv.at[b], target, mp)

        return (
            lambda src: make(src, self.left, me - 2),
            lambda src: make(src, self.right, me + 2),
            lambda src: make(src, self.side, 2 * z + 1 - c),
        )

    def start(self):
        me, z, c, mp = place()
        left, right, side = self.copies(z)

        @pl.when(z > 0)
        def _():
            left(self.own).start()

        @pl.when(z < self.chips - 1)
        def _():
            right(self.own).start()

        side(self.own).start()

    def wait_block(self, b):
        me, z, c, mp = place()
        remote(self.full.at[b], self.full.at[b], self.side.at[0], self.recv.at[b], me, mp).wait_recv()

    def stage(self, k):
        me, z, c, mp = place()

        @pl.when(z + k < self.chips)
        def _():
            oz = z + k
            self.wait_block(2 * oz + c)
            left, right, side = self.copies(oz)

            @pl.when(z > 0)
            def _():
                left(self.full.at[2 * oz + c]).start()

            side(self.full.at[2 * oz + c]).start()

        @pl.when(z - k >= 0)
        def _():
            oz = z - k
            self.wait_block(2 * oz + c)
            left, right, side = self.copies(oz)

            @pl.when(z < self.chips - 1)
            def _():
                right(self.full.at[2 * oz + c]).start()

            side(self.full.at[2 * oz + c]).start()

    def drain(self):
        me, z, c, mp = place()
        for oz in range(self.chips):
            left, right, side = self.copies(oz)

            @pl.when((z > 0) & (oz >= z))
            def _():
                left(self.full.at[2 * oz + c]).wait_send()

            @pl.when((z < self.chips - 1) & (oz <= z))
            def _():
                right(self.full.at[2 * oz + c]).wait_send()

            side(self.full.at[2 * oz + c]).wait_send()


class GroupGather:
    def __init__(self, size, own, full, sems):
        self.size, self.own, self.full = size, own, full
        self.send, self.recv = sems
        self.half = full.shape[1] // 2

    def to(self, src, origin, part, slot, target):
        me, z, c, mp = place()
        rows = self.full.at[origin] if part is None else self.full.at[origin, pl.ds(part * self.half, self.half)]
        sem = self.recv.at[origin, 0 if part is None else part]
        return remote(src, rows, self.send.at[slot], sem, me, target)

    def start(self):
        me, z, c, mp = place()
        for slot, peer in self.peers():
            self.to(self.own, mp, None, slot, peer).start()

    def peers(self):
        me, z, c, mp = place()
        if self.size == 4:
            x_peer = mp + 1 - 2 * lax.rem(mp, 2)
            return ((0, x_peer), (1, lax.rem(mp + 2, 4)))
        return tuple((k - 1, lax.rem(mp + k, self.size)) for k in range(1, self.size))

    def relays(self):
        (_, x_peer), (_, y_peer) = self.peers()
        return (
            self.to(self.full.at[x_peer, pl.ds(0, self.half)], x_peer, 0, 2, y_peer),
            self.to(self.full.at[y_peer, pl.ds(self.half, self.half)], y_peer, 1, 3, x_peer),
        )

    def relay(self):
        for slot, peer in self.peers():
            self.to(self.full.at[peer], peer, None, slot, peer).wait_recv()
        if self.size == 4:
            for copy in self.relays():
                copy.start()

    def finish(self):
        me, z, c, mp = place()
        if self.size == 4:
            far = 3 - mp
            for part in (0, 1):
                rows = self.full.at[far, pl.ds(part * self.half, self.half)]
                self.to(rows, far, part, 0, mp).wait_recv()

    def drain(self):
        me, z, c, mp = place()
        for slot, peer in self.peers():
            self.to(self.own, mp, None, slot, peer).wait_send()
        if self.size == 4:
            for copy in self.relays():
                copy.wait_send()


def row_gather_sems(dp_size):
    chips = dp_size // 2
    return [pltpu.SemaphoreType.DMA((n,)) for n in (dp_size, chips, chips, chips)]


def group_gather_sems(mp_size):
    return [pltpu.SemaphoreType.DMA((max(4, mp_size - 1),)), pltpu.SemaphoreType.DMA((mp_size, 2))]


def gelu_pair(v):
    k0, k1 = 0.7978845608028654, 0.044715
    square = v * v
    t = jnp.tanh(k0 * (v + k1 * v * square))
    half = 0.5 * (1.0 + t)
    slope = half + 0.5 * v * (1.0 - t * t) * (k0 + 3.0 * k0 * k1 * square)
    return v * half, slope


def up_kernel(
    dp_size,
    mp_size,
    tokens,
    gain,
    shift,
    cot,
    up_master,
    up_bias,
    x_out,
    cot_out,
    up_out,
    hidden_out,
    slope_out,
    x_all,
    up_all,
    acc,
    hidden,
    slope,
    *sems,
):
    chips = dp_size // 2
    row_sems, x_sems, cot_sems = sems[0:4], sems[4:6], sems[6:8]
    out_sem = sems[8]
    me, z, c, mp = place()
    rows = tokens.shape[0]
    length = rows * mp_size
    depth, width = up_all.shape[1], up_all.shape[2]

    values = tokens[...].astype(F32)
    centre = values - jnp.mean(values, axis=-1, keepdims=True)
    spread = jnp.mean(centre * centre, axis=-1, keepdims=True)
    x_all[mp] = (centre * lax.rsqrt(spread + EPSILON) * gain[...] + shift[...]).astype(BF)
    up_all[me] = up_master[...].astype(BF)

    greet(chips, mp_size)
    weights = RowGather(chips, up_all.at[me], up_all, row_sems)
    x_gather = GroupGather(mp_size, x_all.at[mp], x_all, x_sems)
    cot_gather = GroupGather(mp_size, cot, cot_out, cot_sems)
    x_gather.start()
    weights.start()
    own_cot = pltpu.make_async_copy(cot, cot_out.at[mp], out_sem.at[0])
    own_cot.start()

    def product(oz, first=False):
        cols = pl.ds(pl.multiple_of(oz * (2 * depth), 2 * depth), 2 * depth)

        def tile(i, carry):
            r, n = i // (width // 512), lax.rem(i, width // 512)
            n0 = pl.ds(pl.multiple_of(n * 512, 512), 512)
            left = x_all[r, :, cols]
            right = up_all[pl.ds(2 * oz, 2), :, n0].reshape(2 * depth, 512)
            term = dot(left, right)
            if first:
                acc[r, :, n0] = term + up_bias[:, n0]
            else:
                acc[r, :, n0] += term
            return carry

        lax.fori_loop(0, mp_size * (width // 512), tile, 0)

    x_gather.relay()
    x_gather.finish()
    weights.stage(1)
    cot_gather.start()
    x_copy = pltpu.make_async_copy(x_all, x_out, out_sem.at[1])
    x_copy.start()
    weights.wait_block(2 * z + 1 - c)
    product(z, True)
    for k in range(1, chips):
        if k > 1:
            weights.stage(k)
        for oz, valid in ((z + k, z + k < chips), (z - k, z - k >= 0)):

            @pl.when(valid)
            def _():
                weights.wait_block(2 * oz + 1 - c)
                product(oz)

        if k == min(2, chips - 1):
            cot_gather.relay()
    up_copy = pltpu.make_async_copy(up_all, up_out, out_sem.at[2])
    up_copy.start()

    def finish(i, carry):
        r, n = i // (width // 512), lax.rem(i, width // 512)
        n0 = pl.ds(pl.multiple_of(n * 512, 512), 512)
        high, grad = gelu_pair(acc[r, :, n0])
        hidden[r, :, n0] = high.astype(BF)
        slope[r, :, n0] = grad.astype(BF)
        return carry

    lax.fori_loop(0, mp_size * (width // 512), finish, 0)
    hidden_copy = pltpu.make_async_copy(hidden, hidden_out, out_sem.at[3])
    slope_copy = pltpu.make_async_copy(slope, slope_out, out_sem.at[4])
    hidden_copy.start()
    slope_copy.start()
    cot_gather.finish()
    weights.drain()
    x_gather.drain()
    cot_gather.drain()
    for copy in (own_cot, x_copy, up_copy, hidden_copy, slope_copy):
        copy.wait()


def up_stage(dp_size, mp_size, tokens, gain, shift, cot, up_master, up_bias):
    rows, model = tokens.shape
    depth, width = up_master.shape
    shape = jax.ShapeDtypeStruct
    outs = (
        shape((mp_size, rows, model), BF),
        shape((mp_size, rows, model), BF),
        shape((dp_size, depth, width), BF),
        shape((mp_size, rows, width), BF),
        shape((mp_size, rows, width), BF),
    )
    return pl.pallas_call(
        partial(up_kernel, dp_size, mp_size),
        out_shape=outs,
        in_specs=[VM] * 6,
        out_specs=[ANY] * 5,
        scratch_shapes=[
            pltpu.VMEM((mp_size, rows, model), BF),
            pltpu.VMEM((dp_size, depth, width), BF),
            pltpu.VMEM((mp_size, rows, width), F32),
            pltpu.VMEM((mp_size, rows, width), BF),
            pltpu.VMEM((mp_size, rows, width), BF),
            *row_gather_sems(dp_size),
            *group_gather_sems(mp_size),
            *group_gather_sems(mp_size),
            pltpu.SemaphoreType.DMA((5,)),
        ],
        compiler_params=pltpu.CompilerParams(
            collective_id=1, has_side_effects=True, vmem_limit_bytes=58 << 20
        ),
        name="up_stage",
    )(tokens, gain.reshape(1, -1), shift.reshape(1, -1), cot, up_master, up_bias.reshape(1, -1))


def attention_kernel(start, q_in, k_in, v_in, out_grad, rot, out, q_grad, k_grad, v_grad, q_sum, k_sum, v_sum, bias, k_acc, v_acc):
    length = q_in.shape[0]
    block = 256
    blocks = length // block

    @pl.when(pl.program_id(0) == 0)
    def _():
        first = start[0]
        for i in range(blocks):
            high = min(length, block * (i + 2)) - block * i
            keys = block * i + lax.broadcasted_iota(jnp.int32, (high, block), 0)
            places = block * i + lax.broadcasted_iota(jnp.int32, (high, block), 1)
            inside = (keys >= first) & (keys < first + PIECE) & (places >= first) & (places < first + PIECE)
            bias[i, :high] = jnp.where((keys <= places) | inside, 0.0, NEGATIVE)

    def turn(values, sign):
        return (
            values * rot[0]
            + sign * (pltpu.roll(values, 128 - ROT_DIM // 2, 1) * rot[1] + pltpu.roll(values, ROT_DIM // 2, 1) * rot[2])
        )

    scale = HEAD_DIM ** (-0.5)
    q_low = (turn(q_in[...], 1.0).astype(BF).astype(F32) * scale).astype(BF)
    k_low = turn(k_in[...], 1.0).astype(BF)
    v_low = v_in[...].astype(BF)
    grad = out_grad[...]
    k_flip, v_flip = k_low.T, v_low.T
    lane = lax.broadcasted_iota(jnp.int32, (length, 128), 1) < HEAD_DIM
    row = lax.broadcasted_iota(jnp.int32, (128, length), 0) < HEAD_DIM
    zero = jnp.zeros((), BF)
    k_acc[...] = jnp.zeros_like(k_acc)
    v_acc[...] = jnp.zeros_like(v_acc)
    heads = []
    for h in range(2):
        lanes, rows = (lane, row) if h == 0 else (~lane, ~row)
        heads.append(
            (
                jnp.where(lanes, q_low, zero),
                jnp.where(lanes, k_low, zero),
                jnp.where(lanes, v_low, zero),
                jnp.where(lanes, grad, zero),
                jnp.where(rows, k_flip, zero),
                jnp.where(rows, v_flip, zero),
            )
        )
    for i in range(blocks):
        here = slice(block * i, block * (i + 1))
        stop = min(length, block * (i + 2))
        parts = [(0, block * i)] if i else []
        parts.append((block * i, stop))
        out_flip = jnp.zeros((128, block), F32)
        q_flip = jnp.zeros((128, block), F32)
        for q_h, k_h, v_h, grad_h, kt_h, vt_h in heads:
            scores = [dot(k_h[a:b], q_low[here], 1, 1) for a, b in parts]
            scores[-1] = scores[-1] + bias[i, : stop - block * i]
            top = scores[-1].max(0, keepdims=True)
            for s in scores[:-1]:
                top = jnp.maximum(top, s.max(0, keepdims=True))
            expo = [jnp.exp(s - top) for s in scores]
            total = expo[0].sum(0, keepdims=True)
            for e in expo[1:]:
                total = total + e.sum(0, keepdims=True)
            share = 1.0 / total
            probs = [e * share for e in expo]
            grads = [dot(v_h[a:b], grad[here], 1, 1) for a, b in parts]
            inner = (probs[0] * grads[0]).sum(0, keepdims=True)
            for p, g in zip(probs[1:], grads[1:]):
                inner = inner + (p * g).sum(0, keepdims=True)
            for (a, b), p, g in zip(parts, probs, grads):
                p_low = p.astype(BF)
                s_grad = (p * (g - inner)).astype(BF)
                out_flip = out_flip + dot(vt_h[:, a:b], p_low)
                q_flip = q_flip + dot(kt_h[:, a:b], s_grad)
                v_acc[a:b] += dot(p_low, grad_h[here])
                k_acc[a:b] += dot(s_grad, q_h[here])
        out[here] = out_flip.T.astype(BF)
        q_rows = q_flip.T * scale
        q_back = (
            q_rows * rot[0, here]
            - pltpu.roll(q_rows, 128 - ROT_DIM // 2, 1) * rot[1, here]
            - pltpu.roll(q_rows, ROT_DIM // 2, 1) * rot[2, here]
        )
        q_grad[here] = q_back.astype(BF)
    k_grad[...] = turn(k_acc[...], -1.0).astype(BF)
    v_grad[...] = v_acc[...].astype(BF)
    for total_out, rows_out in ((q_sum, q_grad), (k_sum, k_grad), (v_sum, v_grad)):
        total_out[...] = jnp.sum(rows_out[...].astype(F32), axis=0, keepdims=True)


def rotary_lanes(length):
    half_dim = ROT_DIM // 2
    lane = jnp.arange(128) % HEAD_DIM
    frequency = 10000.0 ** (-jnp.arange(half_dim).astype(F32) * 2.0 / ROT_DIM)
    angles = jnp.arange(length).astype(F32)[:, None] * frequency[None, :]
    cosine = jnp.tile(jnp.cos(angles), (1, 128 // half_dim))
    sine = jnp.tile(jnp.sin(angles), (1, 128 // half_dim))
    turned = lane[None, :] < ROT_DIM
    first = lane[None, :] < half_dim
    return jnp.stack(
        [
            jnp.where(turned, cosine, 1.0),
            jnp.where(first, -sine, 0.0),
            jnp.where(turned & ~first, sine, 0.0),
        ]
    )


def attention(projected, out_grad, start):
    length, width = out_grad.shape
    pairs = width // 128
    shape = jax.ShapeDtypeStruct

    def rows(shift):
        return pl.BlockSpec((length, 128), lambda i: (0, i + shift))

    total = pl.BlockSpec((1, 128), lambda i: (0, i))
    return pl.pallas_call(
        attention_kernel,
        grid=(pairs,),
        in_specs=[
            pl.BlockSpec(memory_space=pltpu.SMEM),
            rows(0),
            rows(pairs),
            rows(2 * pairs),
            rows(0),
            pl.BlockSpec((3, length, 128), lambda i: (0, 0, 0)),
        ],
        out_specs=[rows(0)] * 4 + [total] * 3,
        out_shape=[shape((length, width), BF)] * 4 + [shape((1, width), F32)] * 3,
        scratch_shapes=[
            pltpu.VMEM((length // 256, 512, 256), F32),
            pltpu.VMEM((length, 128), F32),
            pltpu.VMEM((length, 128), F32),
        ],
        compiler_params=pltpu.CompilerParams(vmem_limit_bytes=50 << 20),
        cost_estimate=pl.CostEstimate(
            flops=16 * length * length * width, bytes_accessed=16 * length * width, transcendentals=length * length * width // 64
        ),
        name="attention",
    )(start, projected, projected, projected, out_grad, rotary_lanes(length))


def flat(ref, cols):
    values = ref[..., cols]
    return values.reshape(-1, values.shape[-1])


class RowScatter:
    pieces = 2

    def __init__(self, chips, left, rights, flip, give, part, land, sems):
        self.chips, self.left, self.rights, self.flip = chips, left, rights, flip
        self.give, self.part, self.land = give, part, land
        self.sib_send, self.sib_recv, self.send_l, self.send_r, self.recv = sems
        self.depth = part.shape[1]

    def target(self, p):
        me, z, c, mp = place()
        s, side = p // 2, lax.rem(p, 2)
        far = self.chips - 1
        t = jnp.where(side == 0, z + s - far, z - s + far)
        return t, (t >= 0) & (t < self.chips)

    def block(self, t, core, store):
        b = 2 * t + core
        cols = pl.ds(pl.multiple_of(b * self.depth, self.depth), self.depth)
        self.flip[...] = flat(self.left, cols).T
        place_at = 0
        for right in self.rights:
            width = right.shape[-1]
            tile = min(512, width)
            for n in range(0, width, tile):
                product = dot(self.flip[...], flat(right, slice(n, n + tile)))
                store(slice(place_at + n, place_at + n + tile), product)
            place_at += width

    def sibling(self, t):
        me, z, c, mp = place()
        return remote(
            self.give.at[t], self.part.at[t], self.sib_send.at[t], self.sib_recv.at[t], 2 * z + 1 - c, mp
        )

    def rows(self, q):
        return pl.ds(q * (self.depth // self.pieces), self.depth // self.pieces)

    def to_left(self, t, q):
        me, z, c, mp = place()
        r = self.rows(q)
        return remote(
            self.part.at[t, r], self.land.at[t, r], self.send_l.at[t, q], self.recv.at[t, q], me - 2, mp
        )

    def to_right(self, t, q):
        me, z, c, mp = place()
        r = self.rows(q)
        slot = jnp.where(t > z + 1, t, self.chips)
        return remote(
            self.part.at[t, r], self.land.at[slot, r], self.send_r.at[t, q], self.recv.at[slot, q], me + 2, mp
        )

    def landed(self, slot, q):
        me, z, c, mp = place()
        here = self.land.at[slot, self.rows(q)]
        remote(here, here, self.send_l.at[0, 0], self.recv.at[slot, q], me, mp).wait_recv()

    def swap(self):
        me, z, c, mp = place()

        def step(p, carry):
            t, valid = self.target(p)

            @pl.when(valid)
            def _():
                def store(cols, values):
                    self.give[t, :, cols] = values.astype(BF)

                self.block(t, 1 - c, store)
                self.sibling(t).start()

            return carry

        lax.fori_loop(0, 2 * self.chips - 1, step, 0)

    def collect(self):
        me, z, c, mp = place()
        last = self.chips - 1

        def step(p, carry):
            t, valid = self.target(p)

            @pl.when(valid)
            def _():
                self.sibling(t).wait_recv()

                def store(cols, values):
                    self.part[t, :, cols] = (values + self.part[t, :, cols].astype(F32)).astype(BF)

                self.block(t, c, store)

                @pl.when((t < z) & (z == last))
                def _():
                    for q in range(self.pieces):
                        self.to_left(t, q).start()

                @pl.when((t > z) & (z == 0))
                def _():
                    for q in range(self.pieces):
                        self.to_right(t, q).start()

            return carry

        lax.fori_loop(0, 2 * self.chips - 1, step, 0)

    def add(self, t, slot, q):
        r = self.rows(q)
        self.landed(slot, q)
        self.part[t, r] = (self.part[t, r].astype(F32) + self.land[slot, r].astype(F32)).astype(BF)

    def relay(self, s):
        me, z, c, mp = place()
        last = self.chips - 1
        for q in range(self.pieces):
            t = z + s - last

            @pl.when((t >= 0) & (z < last))
            def _():
                self.add(t, t, q)
                self.to_left(t, q).start()

            u = z - s + last

            @pl.when((u <= last) & (z > 0))
            def _():
                self.add(u, u, q)
                self.to_right(u, q).start()

    def finish(self, result):
        me, z, c, mp = place()
        for q in range(self.pieces):
            r = self.rows(q)
            result[r] = self.part[z, r].astype(F32)

            @pl.when(z < self.chips - 1)
            def _():
                self.landed(z, q)
                result[r] += self.land[z, r].astype(F32)

            @pl.when(z > 0)
            def _():
                self.landed(self.chips, q)
                result[r] += self.land[self.chips, r].astype(F32)

    def drain_swap(self):
        def step(t, carry):
            self.sibling(t).wait_send()
            return carry

        lax.fori_loop(0, self.chips, step, 0)

    def drain(self):
        me, z, c, mp = place()

        def step(t, carry):
            for q in range(self.pieces):

                @pl.when(t < z)
                def _():
                    self.to_left(t, q).wait_send()

                @pl.when(t > z)
                def _():
                    self.to_right(t, q).wait_send()

            return carry

        lax.fori_loop(0, self.chips, step, 0)


def row_scatter_scratch(chips, depth, width):
    return [
        pltpu.VMEM((chips, depth, width), BF),
        pltpu.VMEM((chips + 1, depth, width), BF),
        pltpu.SemaphoreType.DMA((chips,)),
        pltpu.SemaphoreType.DMA((chips,)),
        pltpu.SemaphoreType.DMA((chips, RowScatter.pieces)),
        pltpu.SemaphoreType.DMA((chips, RowScatter.pieces)),
        pltpu.SemaphoreType.DMA((chips + 1, RowScatter.pieces)),
    ]


class GroupScatter:
    def __init__(self, size, blocks, parts, land, send, recv):
        self.size, self.blocks, self.parts, self.land, self.send, self.recv = size, blocks, parts, land, send, recv
        self.depth = parts.shape[2] // blocks

    def copy(self, k, j):
        me, z, c, mp = place()
        peer = lax.rem(mp + k, self.size)
        cols = pl.ds(pl.multiple_of(j * self.depth, self.depth), self.depth)
        return remote(
            self.parts.at[peer, :, cols],
            self.land.at[mp, :, cols],
            self.send.at[k, j],
            self.recv.at[mp, j],
            me,
            peer,
        )

    def start(self, j):
        for k in range(1, self.size):
            self.copy(k, j).start()

    def arrive(self):
        me, z, c, mp = place()

        def step(j, carry):
            cols = pl.ds(pl.multiple_of(j * self.depth, self.depth), self.depth)
            for k in range(1, self.size):
                origin = lax.rem(mp + k, self.size)
                here = self.land.at[origin, :, cols]
                remote(here, here, self.send.at[0, 0], self.recv.at[origin, j], me, origin).wait_recv()
            return carry

        lax.fori_loop(0, self.blocks, step, 0)

    def total(self, rows):
        me, z, c, mp = place()
        sums = self.parts[mp, rows].astype(F32)
        for k in range(1, self.size):
            sums = sums + self.land[lax.rem(mp + k, self.size), rows].astype(F32)
        return sums

    def drain(self):
        def step(j, carry):
            for k in range(1, self.size):
                self.copy(k, j).wait_send()
            return carry

        lax.fori_loop(0, self.blocks, step, 0)


def grad_kernel(
    dp_size,
    mp_size,
    x_all,
    pre_grad,
    attended,
    hidden_all,
    qkv_full,
    up_full,
    dense_full,
    down_full,
    query_grad,
    key_grad,
    value_grad,
    query_sum,
    key_sum,
    value_sum,
    up_sum,
    tokens,
    cot,
    gain,
    out_bias,
    qkv_share,
    up_share,
    output,
    input_grad,
    totals,
    x_buf,
    pre,
    mixed_buf,
    attended_buf,
    hidden_buf,
    wide_buf,
    thin_buf,
    flip,
    give,
    first,
    second,
    load_sem,
    stream_sem,
    *scratch,
):
    me, z, c, mp = place()
    chips = dp_size // 2
    rows, model = tokens.shape
    width, inner = query_grad.shape[1], up_sum.shape[1]
    depth = model // dp_size
    qkv_scratch, up_scratch, rest = scratch[:7], scratch[7:14], scratch[14:]
    grads = (query_grad, key_grad, value_grad)
    give_qkv = give.at[:, :, pl.ds(0, 3 * width)]
    give_up = give.at[:, :, pl.ds(0, inner)]
    qkv = RowScatter(chips, x_buf, grads, flip, give_qkv, *qkv_scratch[:2], qkv_scratch[2:])
    up = RowScatter(chips, x_buf, (pre,), flip, give_up, *up_scratch[:2], up_scratch[2:])
    normed_group = GroupScatter(mp_size, dp_size, x_buf, *rest[:3])
    mixed_group = GroupScatter(mp_size, dp_size, mixed_buf, *rest[3:6])
    send_1, recv_1, send_2, recv_2 = rest[6:]

    loads = [
        pltpu.make_async_copy(source, target, load_sem.at[n])
        for n, (source, target) in enumerate(
            ((x_all, x_buf), (pre_grad, pre), (attended, attended_buf), (hidden_all, hidden_buf))
        )
    ]
    for load in loads:
        load.start()

    def stream(wide, thin):
        def copies(j):
            slot = lax.rem(j, 2)
            r = pl.ds(pl.multiple_of(j * depth, depth), depth)
            return (
                pltpu.make_async_copy(wide.at[r], wide_buf.at[slot], stream_sem.at[0, slot]),
                pltpu.make_async_copy(
                    thin.at[r], thin_buf.at[slot, :, pl.ds(0, thin.shape[1])], stream_sem.at[1, slot]
                ),
            )

        return copies

    normed_stream = stream(up_full, qkv_full)
    mixed_stream = stream(down_full, dense_full)

    def partial_sums(copies, wide, thins, target, group_out):
        half = mp_size // 2

        def step(j, carry):
            slot = lax.rem(j, 2)
            for copy in copies(j):
                copy.wait()

            @pl.when(j + 1 < dp_size)
            def _():
                for copy in copies(j + 1):
                    copy.start()

            cols = pl.ds(pl.multiple_of(j * depth, depth), depth)
            for h in range(2):
                group = pl.ds(h * half, half)
                left = wide[group].reshape(half * rows, inner)
                sums = dot(left, wide_buf[slot], 1, 1)
                for n, thin in enumerate(thins):
                    left = thin[pl.ds(h * half * rows, half * rows), :]
                    sums = sums + dot(left, thin_buf[slot, :, n * width : (n + 1) * width], 1, 1)
                target[group, :, cols] = sums.astype(BF).reshape(half, rows, depth)
            group_out.start(j)
            return carry

        lax.fori_loop(0, dp_size, step, 0)

    for copy in mixed_stream(0):
        copy.start()
    greet_all(dp_size, mp_size)
    loads[0].wait()
    qkv.swap()
    qkv.collect()
    loads[2].wait()
    loads[3].wait()
    partial_sums(mixed_stream, hidden_buf, (attended_buf,), mixed_buf, mixed_group)
    for copy in normed_stream(0):
        copy.start()
    if chips > 2:
        qkv.relay(1)
    loads[1].wait()
    qkv.drain_swap()
    up.swap()
    up.collect()
    if chips > 3:
        qkv.relay(2)
    partial_sums(normed_stream, pre, grads, x_buf, normed_group)
    for s in range(3, chips - 1):
        qkv.relay(s)
    if chips > 2:
        up.relay(1)
    qkv.finish(qkv_share)
    for s in range(2, chips - 1):
        up.relay(s)

    normed_group.arrive()
    tile = 64
    second[me] = jnp.zeros((8, model), F32)

    def norm_back(i, carry):
        r = pl.ds(pl.multiple_of(i * tile, tile), tile)
        values = tokens[r].astype(F32)
        centre = values - jnp.mean(values, axis=-1, keepdims=True)
        spread = jnp.mean(centre * centre, axis=-1, keepdims=True)
        inverse = lax.rsqrt(spread + EPSILON)
        xhat = centre * inverse
        normed_grad = normed_group.total(r)
        e = normed_grad * gain[...]
        turned = e - jnp.mean(e, axis=-1, keepdims=True) - xhat * jnp.mean(e * xhat, axis=-1, keepdims=True)
        cot_rows = cot[r].astype(F32)
        input_grad[r] = (cot_rows + turned * inverse).astype(BF)
        second[me, 0:1] += jnp.sum(normed_grad * xhat, axis=0, keepdims=True)
        second[me, 1:2] += jnp.sum(normed_grad, axis=0, keepdims=True)
        second[me, 2:3] += jnp.sum(cot_rows, axis=0, keepdims=True)
        return carry

    lax.fori_loop(0, rows // tile, norm_back, 0)
    second[me, 3:4, :inner] = up_sum[...]
    for n, vector in enumerate((query_sum, key_sum, value_sum)):
        second[me, 4:5, n * width : (n + 1) * width] = vector[...]
    first[mp] = second[me]

    def copy_1(k):
        return remote(
            first.at[mp], first.at[mp], send_1.at[k], recv_1.at[mp], me, lax.rem(mp + k, mp_size)
        )

    def copy_2(k):
        return remote(
            second.at[me], second.at[me], send_2.at[k], recv_2.at[me], lax.rem(me + k, dp_size), mp
        )

    for k in range(1, mp_size):
        copy_1(k).start()
    mixed_group.arrive()

    def add_up(i, carry):
        r = pl.ds(pl.multiple_of(i * tile, tile), tile)
        output[r] = (tokens[r].astype(F32) + mixed_group.total(r) + out_bias[...]).astype(BF)
        return carry

    lax.fori_loop(0, rows // tile, add_up, 0)
    for k in range(1, mp_size):
        origin = lax.rem(mp + k, mp_size)
        remote(first.at[origin], first.at[origin], send_1.at[0], recv_1.at[origin], me, origin).wait_recv()
    total = first[0]
    for k in range(1, mp_size):
        total = total + first[k]
    second[me, 0:3] = total[0:3]
    for k in range(1, dp_size):
        copy_2(k).start()
    up.finish(up_share)
    for k in range(1, dp_size):
        origin = lax.rem(me + k, dp_size)
        remote(second.at[origin], second.at[origin], send_2.at[0], recv_2.at[origin], origin, mp).wait_recv()
    total = second[0]
    for k in range(1, dp_size):
        total = total + second[k]
    totals[...] = total
    for k in range(1, mp_size):
        copy_1(k).wait_send()
    for k in range(1, dp_size):
        copy_2(k).wait_send()
    up.drain_swap()
    for stream_out in (qkv, up, normed_group, mixed_group):
        stream_out.drain()


def greet_all(dp_size, mp_size):
    me, z, c, mp = place()
    bar = pltpu.get_barrier_semaphore()
    for k in range(1, mp_size):
        pl.semaphore_signal(bar, 1, device_id=(me, lax.rem(mp + k, mp_size)), device_id_type=MESH)
    for k in range(1, dp_size):
        pl.semaphore_signal(bar, 1, device_id=(lax.rem(me + k, dp_size), mp), device_id_type=MESH)
    pl.semaphore_wait(bar, mp_size + dp_size - 2)


def grad_stage(dp_size, mp_size, hbm_args, grads, sums, tokens, cot, gain, out_bias):
    x_all, pre_grad, attended, hidden_all = hbm_args[:4]
    rows, model = tokens.shape
    length = rows * mp_size
    depth, chips = model // dp_size, dp_size // 2
    width, inner = grads[0].shape[1], pre_grad.shape[2]
    wide = max(3 * width, inner)
    shape = jax.ShapeDtypeStruct
    semaphores = pltpu.SemaphoreType.DMA
    blocks = (mp_size, dp_size)
    group = [pltpu.VMEM((mp_size, rows, model), BF), semaphores(blocks), semaphores(blocks)]
    return pl.pallas_call(
        partial(grad_kernel, dp_size, mp_size),
        out_shape=(
            shape((depth, 3 * width), F32),
            shape((depth, inner), F32),
            shape((rows, model), BF),
            shape((rows, model), BF),
            shape((8, model), F32),
        ),
        in_specs=[ANY] * len(hbm_args) + [VM] * 11,
        out_specs=[VM] * 5,
        scratch_shapes=[
            pltpu.VMEM((mp_size, rows, model), BF),
            pltpu.VMEM((mp_size, rows, inner), BF),
            pltpu.VMEM((mp_size, rows, model), BF),
            pltpu.VMEM((length, width), BF),
            pltpu.VMEM((mp_size, rows, inner), BF),
            pltpu.VMEM((2, depth, inner), BF),
            pltpu.VMEM((2, depth, 3 * width), BF),
            pltpu.VMEM((depth, length), BF),
            pltpu.VMEM((chips, depth, wide), BF),
            pltpu.VMEM((mp_size, 8, model), F32),
            pltpu.VMEM((dp_size, 8, model), F32),
            semaphores((4,)),
            semaphores((2, 2)),
            *row_scatter_scratch(chips, depth, 3 * width),
            *row_scatter_scratch(chips, depth, inner),
            *group,
            *group,
            *[semaphores((n,)) for n in (mp_size, mp_size, dp_size, dp_size)],
        ],
        compiler_params=pltpu.CompilerParams(
            collective_id=3, has_side_effects=True, vmem_limit_bytes=63 << 20
        ),
        name="grad_stage",
    )(*hbm_args, *grads, *sums, tokens, cot, gain.reshape(1, -1), out_bias.reshape(1, -1))


def rows_product(left_side, right_side):
    return lax.dot_general(
        left_side, right_side, (((0,), (0,)), ((), ())), preferred_element_type=jnp.float32
    )


def low_scatter(partial_sums, axis):
    return lax.psum_scatter(
        partial_sums.astype(jnp.bfloat16), axis, scatter_dimension=0, tiled=True
    ).astype(jnp.float32)


def body(
    tokens,
    ln_gain,
    ln_bias,
    qkv_weight,
    qkv_bias,
    dense_weight,
    dense_bias,
    fc1_weight,
    fc1_bias,
    fc2_weight,
    fc2_bias,
    starts,
    cotangent,
):
    dp_size, mp_size = lax.axis_size("dp"), lax.axis_size("mp")
    x_all, cot_all, up_all, hidden_all, slope_all = up_stage(
        dp_size, mp_size, tokens, ln_gain, ln_bias, cotangent, fc1_weight, fc1_bias
    )
    gathered = x_all.reshape(-1, x_all.shape[-1])
    out_rows = cot_all.reshape(gathered.shape)
    up_full = up_all.reshape(-1, up_all.shape[-1])
    hidden_low = hidden_all.reshape(-1, up_all.shape[-1])
    slope = slope_all.reshape(hidden_low.shape)
    masters = (
        qkv_weight.astype(jnp.bfloat16).reshape(qkv_weight.shape[0], -1),
        dense_weight.astype(jnp.bfloat16),
        fc2_weight.astype(jnp.bfloat16),
    )
    qkv_full, dense_full, down_full = (
        lax.all_gather(masters[0], "dp", axis=0, tiled=True),
        lax.all_gather(masters[1], "dp", axis=0, tiled=True),
        lax.all_gather(masters[2], "dp", axis=0, tiled=True),
    )
    local_width = dense_full.shape[1]
    projected = jnp.dot(
        gathered, qkv_full, preferred_element_type=jnp.float32
    ) + qkv_bias.reshape(3 * local_width)
    attended_grad = jnp.dot(out_rows, dense_full, preferred_element_type=jnp.float32).astype(
        jnp.bfloat16
    )
    down_grad = rows_product(out_rows, hidden_low).astype(jnp.bfloat16)
    projected, down_grad = lax.optimization_barrier((projected, down_grad))
    attended, query_grad, key_grad, value_grad, query_sum, key_sum, value_sum = attention(
        projected, attended_grad, starts
    )
    dense_grad = rows_product(out_rows, attended)
    hidden_grad = jnp.dot(out_rows, down_full, preferred_element_type=jnp.float32)
    pre_grad = (hidden_grad * slope).astype(jnp.bfloat16)
    down_share = low_scatter(down_grad, "dp")
    pre_grad, dense_grad, down_share = lax.optimization_barrier(
        (pre_grad, dense_grad.astype(jnp.bfloat16), down_share)
    )
    up_bias_grad = jnp.sum(pre_grad.astype(jnp.float32), axis=0)
    qkv_share, up_share, output, input_grad, totals = grad_stage(
        dp_size,
        mp_size,
        (
            x_all,
            pre_grad.reshape(hidden_all.shape),
            attended,
            hidden_all,
            qkv_full,
            up_full,
            dense_full,
            down_full,
        ),
        (query_grad, key_grad, value_grad),
        (query_sum, key_sum, value_sum, up_bias_grad.reshape(1, -1)),
        tokens,
        cotangent,
        ln_gain,
        dense_bias + fc2_bias,
    )
    qkv_share = qkv_share.reshape(-1, 3, local_width)
    gain_total, shift_total, bias_total = totals[0], totals[1], totals[2]
    up_bias_total = totals[3, : up_full.shape[1]]
    qkv_bias_total = totals[4, : 3 * local_width].reshape(3, local_width)
    dense_share = low_scatter(dense_grad, "dp")
    return (
        output,
        input_grad,
        gain_total,
        shift_total,
        qkv_share,
        qkv_bias_total,
        dense_share,
        bias_total,
        up_share,
        up_bias_total,
        down_share,
        bias_total,
    )


def solution(mesh):
    in_specs = (
        P(("dp", "mp"), None),
        P(),
        P(),
        P("dp", None, "mp"),
        P(None, "mp"),
        P("dp", "mp"),
        P(),
        P("dp", "mp"),
        P("mp"),
        P("dp", "mp"),
        P(),
        P("dp"),
        P(("dp", "mp"), None),
    )
    out_specs = (
        P(("dp", "mp"), None),
        P(("dp", "mp"), None),
        P(),
        P(),
        P("dp", None, "mp"),
        P(None, "mp"),
        P("dp", "mp"),
        P(),
        P("dp", "mp"),
        P("mp"),
        P("dp", "mp"),
        P(),
    )
    return jax.shard_map(body, mesh=mesh, in_specs=in_specs, out_specs=out_specs, check_vma=False)
```

```python
from functools import partial

import jax
import jax.numpy as jnp
from jax import lax
from jax.experimental import pallas as pl
from jax.experimental.pallas import tpu as pltpu
from jax.sharding import PartitionSpec as P

HEAD_DIM = 64
ROT_DIM = 32
LENGTH = 1024
PIECE = 256
EPSILON = 1e-05
NEGATIVE = -1e30
MESH = pl.DeviceIdType.MESH
BF = jnp.bfloat16
F32 = jnp.float32
ANY = pl.BlockSpec(memory_space=pl.ANY)
VM = pl.BlockSpec(memory_space=pltpu.VMEM)


def dot(a, b, ca=1, cb=0):
    return lax.dot_general(a, b, (((ca,), (cb,)), ((), ())), preferred_element_type=F32)


def remote(src, dst, send, recv, dp_index, mp_index):
    return pltpu.make_async_remote_copy(
        src_ref=src,
        dst_ref=dst,
        send_sem=send,
        recv_sem=recv,
        device_id=(dp_index, mp_index),
        device_id_type=MESH,
    )


def place():
    me = lax.axis_index("dp")
    return me, me // 2, lax.rem(me, 2), lax.axis_index("mp")


def greet(chips, mp_size):
    me, z, c, mp = place()
    bar = pltpu.get_barrier_semaphore()
    pl.semaphore_signal(bar, 1, device_id=(2 * z + 1 - c, mp), device_id_type=MESH)

    @pl.when(z > 0)
    def _():
        pl.semaphore_signal(bar, 1, device_id=(me - 2, mp), device_id_type=MESH)

    @pl.when(z < chips - 1)
    def _():
        pl.semaphore_signal(bar, 1, device_id=(me + 2, mp), device_id_type=MESH)

    for k in range(1, mp_size):
        pl.semaphore_signal(
            bar, 1, device_id=(me, lax.rem(mp + k, mp_size)), device_id_type=MESH
        )
    count = mp_size + jnp.where(z > 0, 1, 0) + jnp.where(z < chips - 1, 1, 0)
    pl.semaphore_wait(bar, count)


class RowGather:
    def __init__(self, chips, own, full, sems):
        self.chips, self.own, self.full = chips, own, full
        self.recv, self.left, self.right, self.side = sems

    def copies(self, oz):
        me, z, c, mp = place()
        b = 2 * oz + c
        dst = self.full.at[b]

        def make(src, send, target):
            return remote(src, dst, send.at[oz], self.recv.at[b], target, mp)

        return (
            lambda src: make(src, self.left, me - 2),
            lambda src: make(src, self.right, me + 2),
            lambda src: make(src, self.side, 2 * z + 1 - c),
        )

    def start(self):
        me, z, c, mp = place()
        left, right, side = self.copies(z)

        @pl.when(z > 0)
        def _():
            left(self.own).start()

        @pl.when(z < self.chips - 1)
        def _():
            right(self.own).start()

        side(self.own).start()

    def wait_block(self, b):
        me, z, c, mp = place()
        remote(self.full.at[b], self.full.at[b], self.side.at[0], self.recv.at[b], me, mp).wait_recv()

    def stage(self, k):
        me, z, c, mp = place()

        @pl.when(z + k < self.chips)
        def _():
            oz = z + k
            self.wait_block(2 * oz + c)
            left, right, side = self.copies(oz)

            @pl.when(z > 0)
            def _():
                left(self.full.at[2 * oz + c]).start()

            side(self.full.at[2 * oz + c]).start()

        @pl.when(z - k >= 0)
        def _():
            oz = z - k
            self.wait_block(2 * oz + c)
            left, right, side = self.copies(oz)

            @pl.when(z < self.chips - 1)
            def _():
                right(self.full.at[2 * oz + c]).start()

            side(self.full.at[2 * oz + c]).start()

    def drain(self):
        me, z, c, mp = place()
        for oz in range(self.chips):
            left, right, side = self.copies(oz)

            @pl.when((z > 0) & (oz >= z))
            def _():
                left(self.full.at[2 * oz + c]).wait_send()

            @pl.when((z < self.chips - 1) & (oz <= z))
            def _():
                right(self.full.at[2 * oz + c]).wait_send()

            side(self.full.at[2 * oz + c]).wait_send()


class GroupGather:
    def __init__(self, size, own, full, sems):
        self.size, self.own, self.full = size, own, full
        self.send, self.recv = sems
        self.half = full.shape[1] // 2

    def to(self, src, origin, part, slot, target):
        me, z, c, mp = place()
        rows = self.full.at[origin] if part is None else self.full.at[origin, pl.ds(part * self.half, self.half)]
        sem = self.recv.at[origin, 0 if part is None else part]
        return remote(src, rows, self.send.at[slot], sem, me, target)

    def start(self):
        me, z, c, mp = place()
        for slot, peer in self.peers():
            self.to(self.own, mp, None, slot, peer).start()

    def peers(self):
        me, z, c, mp = place()
        if self.size == 4:
            x_peer = mp + 1 - 2 * lax.rem(mp, 2)
            return ((0, x_peer), (1, lax.rem(mp + 2, 4)))
        return tuple((k - 1, lax.rem(mp + k, self.size)) for k in range(1, self.size))

    def relays(self):
        (_, x_peer), (_, y_peer) = self.peers()
        return (
            self.to(self.full.at[x_peer, pl.ds(0, self.half)], x_peer, 0, 2, y_peer),
            self.to(self.full.at[y_peer, pl.ds(self.half, self.half)], y_peer, 1, 3, x_peer),
        )

    def relay(self):
        for slot, peer in self.peers():
            self.to(self.full.at[peer], peer, None, slot, peer).wait_recv()
        if self.size == 4:
            for copy in self.relays():
                copy.start()

    def finish(self):
        me, z, c, mp = place()
        if self.size == 4:
            far = 3 - mp
            for part in (0, 1):
                rows = self.full.at[far, pl.ds(part * self.half, self.half)]
                self.to(rows, far, part, 0, mp).wait_recv()

    def drain(self):
        me, z, c, mp = place()
        for slot, peer in self.peers():
            self.to(self.own, mp, None, slot, peer).wait_send()
        if self.size == 4:
            for copy in self.relays():
                copy.wait_send()


def row_gather_sems(dp_size):
    chips = dp_size // 2
    return [pltpu.SemaphoreType.DMA((n,)) for n in (dp_size, chips, chips, chips)]


def group_gather_sems(mp_size):
    return [pltpu.SemaphoreType.DMA((max(4, mp_size - 1),)), pltpu.SemaphoreType.DMA((mp_size, 2))]


def gelu_pair(v):
    k0, k1 = 0.7978845608028654, 0.044715
    square = v * v
    t = jnp.tanh(k0 * (v + k1 * v * square))
    half = 0.5 * (1.0 + t)
    slope = half + 0.5 * v * (1.0 - t * t) * (k0 + 3.0 * k0 * k1 * square)
    return v * half, slope


def up_kernel(
    dp_size,
    mp_size,
    tokens,
    gain,
    shift,
    cot,
    up_master,
    up_bias,
    x_out,
    cot_out,
    up_out,
    hidden_out,
    slope_out,
    x_all,
    up_all,
    acc,
    hidden,
    slope,
    *sems,
):
    chips = dp_size // 2
    row_sems, x_sems, cot_sems = sems[0:4], sems[4:6], sems[6:8]
    out_sem = sems[8]
    me, z, c, mp = place()
    rows = tokens.shape[0]
    length = rows * mp_size
    depth, width = up_all.shape[1], up_all.shape[2]

    values = tokens[...].astype(F32)
    centre = values - jnp.mean(values, axis=-1, keepdims=True)
    spread = jnp.mean(centre * centre, axis=-1, keepdims=True)
    x_all[mp] = (centre * lax.rsqrt(spread + EPSILON) * gain[...] + shift[...]).astype(BF)
    up_all[me] = up_master[...].astype(BF)

    greet(chips, mp_size)
    weights = RowGather(chips, up_all.at[me], up_all, row_sems)
    x_gather = GroupGather(mp_size, x_all.at[mp], x_all, x_sems)
    cot_gather = GroupGather(mp_size, cot, cot_out, cot_sems)
    x_gather.start()
    weights.start()
    own_cot = pltpu.make_async_copy(cot, cot_out.at[mp], out_sem.at[0])
    own_cot.start()

    def product(oz, first=False):
        cols = pl.ds(pl.multiple_of(oz * (2 * depth), 2 * depth), 2 * depth)

        def tile(i, carry):
            r, n = i // (width // 512), lax.rem(i, width // 512)
            n0 = pl.ds(pl.multiple_of(n * 512, 512), 512)
            left = x_all[r, :, cols]
            right = up_all[pl.ds(2 * oz, 2), :, n0].reshape(2 * depth, 512)
            term = dot(left, right)
            if first:
                acc[r, :, n0] = term + up_bias[:, n0]
            else:
                acc[r, :, n0] += term
            return carry

        lax.fori_loop(0, mp_size * (width // 512), tile, 0)

    x_gather.relay()
    x_gather.finish()
    weights.stage(1)
    cot_gather.start()
    x_copy = pltpu.make_async_copy(x_all, x_out, out_sem.at[1])
    x_copy.start()
    weights.wait_block(2 * z + 1 - c)
    product(z, True)
    for k in range(1, chips):
        if k > 1:
            weights.stage(k)
        for oz, valid in ((z + k, z + k < chips), (z - k, z - k >= 0)):

            @pl.when(valid)
            def _():
                weights.wait_block(2 * oz + 1 - c)
                product(oz)

        if k == min(2, chips - 1):
            cot_gather.relay()
    up_copy = pltpu.make_async_copy(up_all, up_out, out_sem.at[2])
    up_copy.start()

    def finish(i, carry):
        r, n = i // (width // 512), lax.rem(i, width // 512)
        n0 = pl.ds(pl.multiple_of(n * 512, 512), 512)
        high, grad = gelu_pair(acc[r, :, n0])
        hidden[r, :, n0] = high.astype(BF)
        slope[r, :, n0] = grad.astype(BF)
        return carry

    lax.fori_loop(0, mp_size * (width // 512), finish, 0)
    hidden_copy = pltpu.make_async_copy(hidden, hidden_out, out_sem.at[3])
    slope_copy = pltpu.make_async_copy(slope, slope_out, out_sem.at[4])
    hidden_copy.start()
    slope_copy.start()
    cot_gather.finish()
    weights.drain()
    x_gather.drain()
    cot_gather.drain()
    for copy in (own_cot, x_copy, up_copy, hidden_copy, slope_copy):
        copy.wait()


def up_stage(dp_size, mp_size, tokens, gain, shift, cot, up_master, up_bias):
    rows, model = tokens.shape
    depth, width = up_master.shape
    shape = jax.ShapeDtypeStruct
    outs = (
        shape((mp_size, rows, model), BF),
        shape((mp_size, rows, model), BF),
        shape((dp_size, depth, width), BF),
        shape((mp_size, rows, width), BF),
        shape((mp_size, rows, width), BF),
    )
    return pl.pallas_call(
        partial(up_kernel, dp_size, mp_size),
        out_shape=outs,
        in_specs=[VM] * 6,
        out_specs=[ANY] * 5,
        scratch_shapes=[
            pltpu.VMEM((mp_size, rows, model), BF),
            pltpu.VMEM((dp_size, depth, width), BF),
            pltpu.VMEM((mp_size, rows, width), F32),
            pltpu.VMEM((mp_size, rows, width), BF),
            pltpu.VMEM((mp_size, rows, width), BF),
            *row_gather_sems(dp_size),
            *group_gather_sems(mp_size),
            *group_gather_sems(mp_size),
            pltpu.SemaphoreType.DMA((5,)),
        ],
        compiler_params=pltpu.CompilerParams(
            collective_id=1, has_side_effects=True, vmem_limit_bytes=58 << 20
        ),
        name="up_stage",
    )(tokens, gain.reshape(1, -1), shift.reshape(1, -1), cot, up_master, up_bias.reshape(1, -1))


def attention_kernel(start, q_in, k_in, v_in, out_grad, rot, out, q_grad, k_grad, v_grad, q_sum, k_sum, v_sum, bias, k_acc, v_acc):
    length = q_in.shape[0]
    block = 256
    blocks = length // block

    @pl.when(pl.program_id(0) == 0)
    def _():
        first = start[0]
        for i in range(blocks):
            high = min(length, block * (i + 2)) - block * i
            keys = block * i + lax.broadcasted_iota(jnp.int32, (high, block), 0)
            places = block * i + lax.broadcasted_iota(jnp.int32, (high, block), 1)
            inside = (keys >= first) & (keys < first + PIECE) & (places >= first) & (places < first + PIECE)
            bias[i, :high] = jnp.where((keys <= places) | inside, 0.0, NEGATIVE)

    def turn(values, sign):
        return (
            values * rot[0]
            + sign * (pltpu.roll(values, 128 - ROT_DIM // 2, 1) * rot[1] + pltpu.roll(values, ROT_DIM // 2, 1) * rot[2])
        )

    scale = HEAD_DIM ** (-0.5)
    q_low = (turn(q_in[...], 1.0).astype(BF).astype(F32) * scale).astype(BF)
    k_low = turn(k_in[...], 1.0).astype(BF)
    v_low = v_in[...].astype(BF)
    grad = out_grad[...]
    k_flip, v_flip = k_low.T, v_low.T
    lane = lax.broadcasted_iota(jnp.int32, (length, 128), 1) < HEAD_DIM
    row = lax.broadcasted_iota(jnp.int32, (128, length), 0) < HEAD_DIM
    zero = jnp.zeros((), BF)
    k_acc[...] = jnp.zeros_like(k_acc)
    v_acc[...] = jnp.zeros_like(v_acc)
    heads = []
    for h in range(2):
        lanes, rows = (lane, row) if h == 0 else (~lane, ~row)
        heads.append(
            (
                jnp.where(lanes, q_low, zero),
                jnp.where(lanes, k_low, zero),
                jnp.where(lanes, v_low, zero),
                jnp.where(lanes, grad, zero),
                jnp.where(rows, k_flip, zero),
                jnp.where(rows, v_flip, zero),
            )
        )
    for i in range(blocks):
        here = slice(block * i, block * (i + 1))
        stop = min(length, block * (i + 2))
        parts = [(0, block * i)] if i else []
        parts.append((block * i, stop))
        out_flip = jnp.zeros((128, block), F32)
        q_flip = jnp.zeros((128, block), F32)
        for q_h, k_h, v_h, grad_h, kt_h, vt_h in heads:
            scores = [dot(k_h[a:b], q_low[here], 1, 1) for a, b in parts]
            scores[-1] = scores[-1] + bias[i, : stop - block * i]
            top = scores[-1].max(0, keepdims=True)
            for s in scores[:-1]:
                top = jnp.maximum(top, s.max(0, keepdims=True))
            expo = [jnp.exp(s - top) for s in scores]
            total = expo[0].sum(0, keepdims=True)
            for e in expo[1:]:
                total = total + e.sum(0, keepdims=True)
            share = 1.0 / total
            probs = [e * share for e in expo]
            grads = [dot(v_h[a:b], grad[here], 1, 1) for a, b in parts]
            inner = (probs[0] * grads[0]).sum(0, keepdims=True)
            for p, g in zip(probs[1:], grads[1:]):
                inner = inner + (p * g).sum(0, keepdims=True)
            for (a, b), p, g in zip(parts, probs, grads):
                p_low = p.astype(BF)
                s_grad = (p * (g - inner)).astype(BF)
                out_flip = out_flip + dot(vt_h[:, a:b], p_low)
                q_flip = q_flip + dot(kt_h[:, a:b], s_grad)
                v_acc[a:b] += dot(p_low, grad_h[here])
                k_acc[a:b] += dot(s_grad, q_h[here])
        out[here] = out_flip.T.astype(BF)
        q_rows = q_flip.T * scale
        q_back = (
            q_rows * rot[0, here]
            - pltpu.roll(q_rows, 128 - ROT_DIM // 2, 1) * rot[1, here]
            - pltpu.roll(q_rows, ROT_DIM // 2, 1) * rot[2, here]
        )
        q_grad[here] = q_back.astype(BF)
    k_grad[...] = turn(k_acc[...], -1.0).astype(BF)
    v_grad[...] = v_acc[...].astype(BF)
    for total_out, rows_out in ((q_sum, q_grad), (k_sum, k_grad), (v_sum, v_grad)):
        total_out[...] = jnp.sum(rows_out[...].astype(F32), axis=0, keepdims=True)


def rotary_lanes(length):
    half_dim = ROT_DIM // 2
    lane = jnp.arange(128) % HEAD_DIM
    frequency = 10000.0 ** (-jnp.arange(half_dim).astype(F32) * 2.0 / ROT_DIM)
    angles = jnp.arange(length).astype(F32)[:, None] * frequency[None, :]
    cosine = jnp.tile(jnp.cos(angles), (1, 128 // half_dim))
    sine = jnp.tile(jnp.sin(angles), (1, 128 // half_dim))
    turned = lane[None, :] < ROT_DIM
    first = lane[None, :] < half_dim
    return jnp.stack(
        [
            jnp.where(turned, cosine, 1.0),
            jnp.where(first, -sine, 0.0),
            jnp.where(turned & ~first, sine, 0.0),
        ]
    )


def attention(projected, out_grad, start):
    length, width = out_grad.shape
    pairs = width // 128
    shape = jax.ShapeDtypeStruct

    def rows(shift):
        return pl.BlockSpec((length, 128), lambda i: (0, i + shift))

    total = pl.BlockSpec((1, 128), lambda i: (0, i))
    return pl.pallas_call(
        attention_kernel,
        grid=(pairs,),
        in_specs=[
            pl.BlockSpec(memory_space=pltpu.SMEM),
            rows(0),
            rows(pairs),
            rows(2 * pairs),
            rows(0),
            pl.BlockSpec((3, length, 128), lambda i: (0, 0, 0)),
        ],
        out_specs=[rows(0)] * 4 + [total] * 3,
        out_shape=[shape((length, width), BF)] * 4 + [shape((1, width), F32)] * 3,
        scratch_shapes=[
            pltpu.VMEM((length // 256, 512, 256), F32),
            pltpu.VMEM((length, 128), F32),
            pltpu.VMEM((length, 128), F32),
        ],
        compiler_params=pltpu.CompilerParams(vmem_limit_bytes=62 << 20),
        cost_estimate=pl.CostEstimate(
            flops=16 * length * length * width, bytes_accessed=16 * length * width, transcendentals=length * length * width // 64
        ),
        name="attention",
    )(start, projected, projected, projected, out_grad, rotary_lanes(length))


def flat(ref, cols):
    values = ref[..., cols]
    return values.reshape(-1, values.shape[-1])


class RowScatter:
    pieces = 2

    def __init__(self, chips, left, rights, flip, give, part, land, sems):
        self.chips, self.left, self.rights, self.flip = chips, left, rights, flip
        self.give, self.part, self.land = give, part, land
        self.sib_send, self.sib_recv, self.send_l, self.send_r, self.recv = sems
        self.depth = part.shape[1]

    def target(self, p):
        me, z, c, mp = place()
        s, side = p // 2, lax.rem(p, 2)
        far = self.chips - 1
        t = jnp.where(side == 0, z + s - far, z - s + far)
        return t, (t >= 0) & (t < self.chips)

    def block(self, t, core, store):
        b = 2 * t + core
        cols = pl.ds(pl.multiple_of(b * self.depth, self.depth), self.depth)
        self.flip[...] = flat(self.left, cols).T
        place_at = 0
        for right in self.rights:
            width = right.shape[-1]
            tile = min(512, width)
            for n in range(0, width, tile):
                product = dot(self.flip[...], flat(right, slice(n, n + tile)))
                store(slice(place_at + n, place_at + n + tile), product)
            place_at += width

    def sibling(self, t):
        me, z, c, mp = place()
        return remote(
            self.give.at[t], self.part.at[t], self.sib_send.at[t], self.sib_recv.at[t], 2 * z + 1 - c, mp
        )

    def rows(self, q):
        return pl.ds(q * (self.depth // self.pieces), self.depth // self.pieces)

    def to_left(self, t, q):
        me, z, c, mp = place()
        r = self.rows(q)
        return remote(
            self.part.at[t, r], self.land.at[t, r], self.send_l.at[t, q], self.recv.at[t, q], me - 2, mp
        )

    def to_right(self, t, q):
        me, z, c, mp = place()
        r = self.rows(q)
        slot = jnp.where(t > z + 1, t, self.chips)
        return remote(
            self.part.at[t, r], self.land.at[slot, r], self.send_r.at[t, q], self.recv.at[slot, q], me + 2, mp
        )

    def landed(self, slot, q):
        me, z, c, mp = place()
        here = self.land.at[slot, self.rows(q)]
        remote(here, here, self.send_l.at[0, 0], self.recv.at[slot, q], me, mp).wait_recv()

    def swap(self):
        me, z, c, mp = place()

        def step(p, carry):
            t, valid = self.target(p)

            @pl.when(valid)
            def _():
                def store(cols, values):
                    self.give[t, :, cols] = values.astype(BF)

                self.block(t, 1 - c, store)
                self.sibling(t).start()

            return carry

        lax.fori_loop(0, 2 * self.chips - 1, step, 0)

    def collect(self):
        me, z, c, mp = place()
        last = self.chips - 1

        def step(p, carry):
            t, valid = self.target(p)

            @pl.when(valid)
            def _():
                self.sibling(t).wait_recv()

                def store(cols, values):
                    self.part[t, :, cols] = (values + self.part[t, :, cols].astype(F32)).astype(BF)

                self.block(t, c, store)

                @pl.when((t < z) & (z == last))
                def _():
                    for q in range(self.pieces):
                        self.to_left(t, q).start()

                @pl.when((t > z) & (z == 0))
                def _():
                    for q in range(self.pieces):
                        self.to_right(t, q).start()

            return carry

        lax.fori_loop(0, 2 * self.chips - 1, step, 0)

    def add(self, t, slot, q):
        r = self.rows(q)
        self.landed(slot, q)
        self.part[t, r] = (self.part[t, r].astype(F32) + self.land[slot, r].astype(F32)).astype(BF)

    def relay(self, s):
        me, z, c, mp = place()
        last = self.chips - 1
        for q in range(self.pieces):
            t = z + s - last

            @pl.when((t >= 0) & (z < last))
            def _():
                self.add(t, t, q)
                self.to_left(t, q).start()

            u = z - s + last

            @pl.when((u <= last) & (z > 0))
            def _():
                self.add(u, u, q)
                self.to_right(u, q).start()

    def finish(self, result):
        me, z, c, mp = place()
        for q in range(self.pieces):
            r = self.rows(q)
            result[r] = self.part[z, r].astype(F32)

            @pl.when(z < self.chips - 1)
            def _():
                self.landed(z, q)
                result[r] += self.land[z, r].astype(F32)

            @pl.when(z > 0)
            def _():
                self.landed(self.chips, q)
                result[r] += self.land[self.chips, r].astype(F32)

    def drain_swap(self):
        def step(t, carry):
            self.sibling(t).wait_send()
            return carry

        lax.fori_loop(0, self.chips, step, 0)

    def drain(self):
        me, z, c, mp = place()

        def step(t, carry):
            for q in range(self.pieces):

                @pl.when(t < z)
                def _():
                    self.to_left(t, q).wait_send()

                @pl.when(t > z)
                def _():
                    self.to_right(t, q).wait_send()

            return carry

        lax.fori_loop(0, self.chips, step, 0)


def row_scatter_scratch(chips, depth, width):
    return [
        pltpu.VMEM((chips, depth, width), BF),
        pltpu.VMEM((chips + 1, depth, width), BF),
        pltpu.SemaphoreType.DMA((chips,)),
        pltpu.SemaphoreType.DMA((chips,)),
        pltpu.SemaphoreType.DMA((chips, RowScatter.pieces)),
        pltpu.SemaphoreType.DMA((chips, RowScatter.pieces)),
        pltpu.SemaphoreType.DMA((chips + 1, RowScatter.pieces)),
    ]


class GroupScatter:
    def __init__(self, size, blocks, parts, land, send, recv):
        self.size, self.blocks, self.parts, self.land, self.send, self.recv = size, blocks, parts, land, send, recv
        self.depth = parts.shape[2] // blocks

    def copy(self, k, j):
        me, z, c, mp = place()
        peer = lax.rem(mp + k, self.size)
        cols = pl.ds(pl.multiple_of(j * self.depth, self.depth), self.depth)
        return remote(
            self.parts.at[peer, :, cols],
            self.land.at[mp, :, cols],
            self.send.at[k, j],
            self.recv.at[mp, j],
            me,
            peer,
        )

    def start(self, j):
        for k in range(1, self.size):
            self.copy(k, j).start()

    def arrive(self):
        me, z, c, mp = place()

        def step(j, carry):
            cols = pl.ds(pl.multiple_of(j * self.depth, self.depth), self.depth)
            for k in range(1, self.size):
                origin = lax.rem(mp + k, self.size)
                here = self.land.at[origin, :, cols]
                remote(here, here, self.send.at[0, 0], self.recv.at[origin, j], me, origin).wait_recv()
            return carry

        lax.fori_loop(0, self.blocks, step, 0)

    def total(self, rows):
        me, z, c, mp = place()
        sums = self.parts[mp, rows].astype(F32)
        for k in range(1, self.size):
            sums = sums + self.land[lax.rem(mp + k, self.size), rows].astype(F32)
        return sums

    def drain(self):
        def step(j, carry):
            for k in range(1, self.size):
                self.copy(k, j).wait_send()
            return carry

        lax.fori_loop(0, self.blocks, step, 0)


def grad_kernel(
    dp_size,
    mp_size,
    x_all,
    pre_grad,
    attended,
    hidden_all,
    cot_all,
    qkv_full,
    up_full,
    dense_full,
    down_full,
    query_grad,
    key_grad,
    value_grad,
    query_sum,
    key_sum,
    value_sum,
    up_sum,
    tokens,
    cot,
    gain,
    out_bias,
    dense_share,
    qkv_share,
    up_share,
    output,
    input_grad,
    totals,
    x_buf,
    pre,
    mixed_buf,
    attended_buf,
    hidden_buf,
    wide_buf,
    thin_buf,
    flip,
    give,
    first,
    second,
    load_sem,
    stream_sem,
    *scratch,
):
    me, z, c, mp = place()
    chips = dp_size // 2
    rows, model = tokens.shape
    width, inner = query_grad.shape[1], up_sum.shape[1]
    depth = model // dp_size
    qkv_scratch, up_scratch, dense_scratch, rest = scratch[:7], scratch[7:14], scratch[14:21], scratch[21:]
    grads = (query_grad, key_grad, value_grad)
    give_qkv = give.at[:, :, pl.ds(0, 3 * width)]
    give_up = give.at[:, :, pl.ds(0, inner)]
    give_dense = give.at[:, :, pl.ds(0, width)]
    dense = RowScatter(
        chips, mixed_buf, (attended_buf,), flip, give_dense, *dense_scratch[:2], dense_scratch[2:]
    )
    qkv = RowScatter(chips, x_buf, grads, flip, give_qkv, *qkv_scratch[:2], qkv_scratch[2:])
    up = RowScatter(chips, x_buf, (pre,), flip, give_up, *up_scratch[:2], up_scratch[2:])
    normed_group = GroupScatter(mp_size, dp_size, x_buf, *rest[:3])
    mixed_group = GroupScatter(mp_size, dp_size, mixed_buf, *rest[3:6])
    send_1, recv_1, send_2, recv_2 = rest[6:]

    loads = [
        pltpu.make_async_copy(source, target, load_sem.at[n])
        for n, (source, target) in enumerate(
            (
                (cot_all, mixed_buf),
                (attended, attended_buf),
                (x_all, x_buf),
                (pre_grad, pre),
                (hidden_all, hidden_buf),
                (tokens, rest[0].at[mp]),
                (cot, rest[3].at[mp]),
            )
        )
    ]
    for load in loads:
        load.start()

    def stream(wide, thin):
        def copies(j):
            slot = lax.rem(j, 2)
            r = pl.ds(pl.multiple_of(j * depth, depth), depth)
            return (
                pltpu.make_async_copy(wide.at[r], wide_buf.at[slot], stream_sem.at[0, slot]),
                pltpu.make_async_copy(
                    thin.at[r], thin_buf.at[slot, :, pl.ds(0, thin.shape[1])], stream_sem.at[1, slot]
                ),
            )

        return copies

    normed_stream = stream(up_full, qkv_full)
    mixed_stream = stream(down_full, dense_full)

    def partial_sums(copies, wide, thins, target, group_out):
        half = mp_size // 2

        def step(j, carry):
            slot = lax.rem(j, 2)
            for copy in copies(j):
                copy.wait()

            @pl.when(j + 1 < dp_size)
            def _():
                for copy in copies(j + 1):
                    copy.start()

            cols = pl.ds(pl.multiple_of(j * depth, depth), depth)
            for h in range(2):
                group = pl.ds(h * half, half)
                left = wide[group].reshape(half * rows, inner)
                sums = dot(left, wide_buf[slot], 1, 1)
                for n, thin in enumerate(thins):
                    left = thin[pl.ds(h * half * rows, half * rows), :]
                    sums = sums + dot(left, thin_buf[slot, :, n * width : (n + 1) * width], 1, 1)
                target[group, :, cols] = sums.astype(BF).reshape(half, rows, depth)
            group_out.start(j)
            return carry

        lax.fori_loop(0, dp_size, step, 0)

    for copy in mixed_stream(0):
        copy.start()
    greet_all(dp_size, mp_size)
    loads[0].wait()
    loads[1].wait()
    dense.swap()
    dense.collect()
    dense.drain_swap()
    loads[2].wait()
    qkv.swap()
    qkv.collect()
    if chips > 2:
        dense.relay(1)
    loads[4].wait()
    partial_sums(mixed_stream, hidden_buf, (attended_buf,), mixed_buf, mixed_group)
    for copy in normed_stream(0):
        copy.start()
    for s in range(2, chips - 1):
        dense.relay(s)
    if chips > 2:
        qkv.relay(1)
    loads[3].wait()
    qkv.drain_swap()
    up.swap()
    up.collect()
    dense.finish(dense_share)
    partial_sums(normed_stream, pre, grads, x_buf, normed_group)
    for s in range(2, chips - 1):
        qkv.relay(s)
    if chips > 2:
        up.relay(1)
    qkv.finish(qkv_share)
    for s in range(2, chips - 1):
        up.relay(s)

    normed_group.arrive()
    loads[5].wait()
    loads[6].wait()
    tile = 64
    second[me] = jnp.zeros((8, model), F32)

    def norm_back(i, carry):
        r = pl.ds(pl.multiple_of(i * tile, tile), tile)
        values = rest[0][mp, r].astype(F32)
        centre = values - jnp.mean(values, axis=-1, keepdims=True)
        spread = jnp.mean(centre * centre, axis=-1, keepdims=True)
        inverse = lax.rsqrt(spread + EPSILON)
        xhat = centre * inverse
        normed_grad = normed_group.total(r)
        e = normed_grad * gain[...]
        turned = e - jnp.mean(e, axis=-1, keepdims=True) - xhat * jnp.mean(e * xhat, axis=-1, keepdims=True)
        cot_rows = rest[3][mp, r].astype(F32)
        input_grad[r] = (cot_rows + turned * inverse).astype(BF)
        second[me, 0:1] += jnp.sum(normed_grad * xhat, axis=0, keepdims=True)
        second[me, 1:2] += jnp.sum(normed_grad, axis=0, keepdims=True)
        second[me, 2:3] += jnp.sum(cot_rows, axis=0, keepdims=True)
        return carry

    lax.fori_loop(0, rows // tile, norm_back, 0)
    second[me, 3:4, :inner] = up_sum[...]
    for n, vector in enumerate((query_sum, key_sum, value_sum)):
        second[me, 4:5, n * width : (n + 1) * width] = vector[...]
    first[mp] = second[me]

    def copy_1(k):
        return remote(
            first.at[mp], first.at[mp], send_1.at[k], recv_1.at[mp], me, lax.rem(mp + k, mp_size)
        )

    def copy_2(k):
        return remote(
            second.at[me], second.at[me], send_2.at[k], recv_2.at[me], lax.rem(me + k, dp_size), mp
        )

    for k in range(1, mp_size):
        copy_1(k).start()
    mixed_group.arrive()

    def add_up(i, carry):
        r = pl.ds(pl.multiple_of(i * tile, tile), tile)
        output[r] = (rest[0][mp, r].astype(F32) + mixed_group.total(r) + out_bias[...]).astype(BF)
        return carry

    lax.fori_loop(0, rows // tile, add_up, 0)
    for k in range(1, mp_size):
        origin = lax.rem(mp + k, mp_size)
        remote(first.at[origin], first.at[origin], send_1.at[0], recv_1.at[origin], me, origin).wait_recv()
    total = first[0]
    for k in range(1, mp_size):
        total = total + first[k]
    second[me, 0:3] = total[0:3]
    for k in range(1, dp_size):
        copy_2(k).start()
    up.finish(up_share)
    for k in range(1, dp_size):
        origin = lax.rem(me + k, dp_size)
        remote(second.at[origin], second.at[origin], send_2.at[0], recv_2.at[origin], origin, mp).wait_recv()
    total = second[0]
    for k in range(1, dp_size):
        total = total + second[k]
    totals[...] = total
    for k in range(1, mp_size):
        copy_1(k).wait_send()
    for k in range(1, dp_size):
        copy_2(k).wait_send()
    up.drain_swap()
    for stream_out in (dense, qkv, up, normed_group, mixed_group):
        stream_out.drain()


def greet_all(dp_size, mp_size):
    me, z, c, mp = place()
    bar = pltpu.get_barrier_semaphore()
    for k in range(1, mp_size):
        pl.semaphore_signal(bar, 1, device_id=(me, lax.rem(mp + k, mp_size)), device_id_type=MESH)
    for k in range(1, dp_size):
        pl.semaphore_signal(bar, 1, device_id=(lax.rem(me + k, dp_size), mp), device_id_type=MESH)
    pl.semaphore_wait(bar, mp_size + dp_size - 2)


def grad_stage(dp_size, mp_size, hbm_args, grads, sums, tokens, cot, gain, out_bias):
    pre_grad = hbm_args[1]
    rows, model = tokens.shape
    length = rows * mp_size
    depth, chips = model // dp_size, dp_size // 2
    width, inner = grads[0].shape[1], pre_grad.shape[2]
    wide = max(3 * width, inner)
    shape = jax.ShapeDtypeStruct
    semaphores = pltpu.SemaphoreType.DMA
    blocks = (mp_size, dp_size)
    group = [pltpu.VMEM((mp_size, rows, model), BF), semaphores(blocks), semaphores(blocks)]
    return pl.pallas_call(
        partial(grad_kernel, dp_size, mp_size),
        out_shape=(
            shape((depth, width), F32),
            shape((depth, 3 * width), F32),
            shape((depth, inner), F32),
            shape((rows, model), BF),
            shape((rows, model), BF),
            shape((8, model), F32),
        ),
        in_specs=[ANY] * len(hbm_args) + [VM] * 7 + [ANY] * 2 + [VM] * 2,
        out_specs=[VM] * 6,
        scratch_shapes=[
            pltpu.VMEM((mp_size, rows, model), BF),
            pltpu.VMEM((mp_size, rows, inner), BF),
            pltpu.VMEM((mp_size, rows, model), BF),
            pltpu.VMEM((length, width), BF),
            pltpu.VMEM((mp_size, rows, inner), BF),
            pltpu.VMEM((2, depth, inner), BF),
            pltpu.VMEM((2, depth, 3 * width), BF),
            pltpu.VMEM((depth, length), BF),
            pltpu.VMEM((chips, depth, wide), BF),
            pltpu.VMEM((mp_size, 8, model), F32),
            pltpu.VMEM((dp_size, 8, model), F32),
            semaphores((7,)),
            semaphores((2, 2)),
            *row_scatter_scratch(chips, depth, 3 * width),
            *row_scatter_scratch(chips, depth, inner),
            *row_scatter_scratch(chips, depth, width),
            *group,
            *group,
            *[semaphores((n,)) for n in (mp_size, mp_size, dp_size, dp_size)],
        ],
        compiler_params=pltpu.CompilerParams(
            collective_id=3, has_side_effects=True, vmem_limit_bytes=67043328
        ),
        name="grad_stage",
    )(*hbm_args, *grads, *sums, tokens, cot, gain.reshape(1, -1), out_bias.reshape(1, -1))


def rows_product(left_side, right_side):
    return lax.dot_general(
        left_side, right_side, (((0,), (0,)), ((), ())), preferred_element_type=jnp.float32
    )


def low_scatter(partial_sums, axis):
    return lax.psum_scatter(
        partial_sums.astype(jnp.bfloat16), axis, scatter_dimension=0, tiled=True
    ).astype(jnp.float32)


def body(
    tokens,
    ln_gain,
    ln_bias,
    qkv_weight,
    qkv_bias,
    dense_weight,
    dense_bias,
    fc1_weight,
    fc1_bias,
    fc2_weight,
    fc2_bias,
    starts,
    cotangent,
):
    dp_size, mp_size = lax.axis_size("dp"), lax.axis_size("mp")
    x_all, cot_all, up_all, hidden_all, slope_all = up_stage(
        dp_size, mp_size, tokens, ln_gain, ln_bias, cotangent, fc1_weight, fc1_bias
    )
    gathered = x_all.reshape(-1, x_all.shape[-1])
    out_rows = cot_all.reshape(gathered.shape)
    up_full = up_all.reshape(-1, up_all.shape[-1])
    hidden_low = hidden_all.reshape(-1, up_all.shape[-1])
    slope = slope_all.reshape(hidden_low.shape)
    masters = (
        qkv_weight.astype(jnp.bfloat16).reshape(qkv_weight.shape[0], -1),
        dense_weight.astype(jnp.bfloat16),
        fc2_weight.astype(jnp.bfloat16),
    )
    qkv_full, dense_full, down_full = (
        lax.all_gather(masters[0], "dp", axis=0, tiled=True),
        lax.all_gather(masters[1], "dp", axis=0, tiled=True),
        lax.all_gather(masters[2], "dp", axis=0, tiled=True),
    )
    local_width = dense_full.shape[1]
    projected = jnp.dot(
        gathered, qkv_full, preferred_element_type=jnp.float32
    ) + qkv_bias.reshape(3 * local_width)
    attended_grad = jnp.dot(out_rows, dense_full, preferred_element_type=jnp.float32).astype(
        jnp.bfloat16
    )
    down_grad = rows_product(out_rows, hidden_low).astype(jnp.bfloat16)
    projected, down_grad = lax.optimization_barrier((projected, down_grad))
    attended, query_grad, key_grad, value_grad, query_sum, key_sum, value_sum = attention(
        projected, attended_grad, starts
    )
    hidden_grad = jnp.dot(out_rows, down_full, preferred_element_type=jnp.float32)
    pre_grad = (hidden_grad * slope).astype(jnp.bfloat16)
    down_share = low_scatter(down_grad, "dp")
    up_bias_grad = jnp.sum(pre_grad.astype(jnp.float32), axis=0)
    dense_share, qkv_share, up_share, output, input_grad, totals = grad_stage(
        dp_size,
        mp_size,
        (
            x_all,
            pre_grad.reshape(hidden_all.shape),
            attended,
            hidden_all,
            cot_all,
            qkv_full,
            up_full,
            dense_full,
            down_full,
        ),
        (query_grad, key_grad, value_grad),
        (query_sum, key_sum, value_sum, up_bias_grad.reshape(1, -1)),
        tokens,
        cotangent,
        ln_gain,
        dense_bias + fc2_bias,
    )
    qkv_share = qkv_share.reshape(-1, 3, local_width)
    gain_total, shift_total, bias_total = totals[0], totals[1], totals[2]
    up_bias_total = totals[3, : up_full.shape[1]]
    qkv_bias_total = totals[4, : 3 * local_width].reshape(3, local_width)
    return (
        output,
        input_grad,
        gain_total,
        shift_total,
        qkv_share,
        qkv_bias_total,
        dense_share,
        bias_total,
        up_share,
        up_bias_total,
        down_share,
        bias_total,
    )


def solution(mesh):
    in_specs = (
        P(("dp", "mp"), None),
        P(),
        P(),
        P("dp", None, "mp"),
        P(None, "mp"),
        P("dp", "mp"),
        P(),
        P("dp", "mp"),
        P("mp"),
        P("dp", "mp"),
        P(),
        P("dp"),
        P(("dp", "mp"), None),
    )
    out_specs = (
        P(("dp", "mp"), None),
        P(("dp", "mp"), None),
        P(),
        P(),
        P("dp", None, "mp"),
        P(None, "mp"),
        P("dp", "mp"),
        P(),
        P("dp", "mp"),
        P("mp"),
        P("dp", "mp"),
        P(),
    )
    return jax.shard_map(body, mesh=mesh, in_specs=in_specs, out_specs=out_specs, check_vma=False)
```

```python
from functools import partial

import jax
import jax.numpy as jnp
from jax import lax
from jax.experimental import pallas as pl
from jax.experimental.pallas import tpu as pltpu
from jax.sharding import PartitionSpec as P

HEAD_DIM = 64
ROT_DIM = 32
LENGTH = 1024
PIECE = 256
EPSILON = 1e-05
NEGATIVE = -1e30
MESH = pl.DeviceIdType.MESH
BF = jnp.bfloat16
F32 = jnp.float32
ANY = pl.BlockSpec(memory_space=pl.ANY)
VM = pl.BlockSpec(memory_space=pltpu.VMEM)


def dot(a, b, ca=1, cb=0):
    return lax.dot_general(a, b, (((ca,), (cb,)), ((), ())), preferred_element_type=F32)


def remote(src, dst, send, recv, dp_index, mp_index):
    return pltpu.make_async_remote_copy(
        src_ref=src,
        dst_ref=dst,
        send_sem=send,
        recv_sem=recv,
        device_id=(dp_index, mp_index),
        device_id_type=MESH,
    )


def place():
    me = lax.axis_index("dp")
    return me, me // 2, lax.rem(me, 2), lax.axis_index("mp")


def greet(chips, mp_size):
    me, z, c, mp = place()
    bar = pltpu.get_barrier_semaphore()
    pl.semaphore_signal(bar, 1, device_id=(2 * z + 1 - c, mp), device_id_type=MESH)

    @pl.when(z > 0)
    def _():
        pl.semaphore_signal(bar, 1, device_id=(me - 2, mp), device_id_type=MESH)

    @pl.when(z < chips - 1)
    def _():
        pl.semaphore_signal(bar, 1, device_id=(me + 2, mp), device_id_type=MESH)

    for k in range(1, mp_size):
        pl.semaphore_signal(
            bar, 1, device_id=(me, lax.rem(mp + k, mp_size)), device_id_type=MESH
        )
    count = mp_size + jnp.where(z > 0, 1, 0) + jnp.where(z < chips - 1, 1, 0)
    pl.semaphore_wait(bar, count)


class RowGather:
    def __init__(self, chips, own, full, sems):
        self.chips, self.own, self.full = chips, own, full
        self.recv, self.left, self.right, self.side = sems

    def copies(self, oz):
        me, z, c, mp = place()
        b = 2 * oz + c
        dst = self.full.at[b]

        def make(src, send, target):
            return remote(src, dst, send.at[oz], self.recv.at[b], target, mp)

        return (
            lambda src: make(src, self.left, me - 2),
            lambda src: make(src, self.right, me + 2),
            lambda src: make(src, self.side, 2 * z + 1 - c),
        )

    def start(self):
        me, z, c, mp = place()
        left, right, side = self.copies(z)

        @pl.when(z > 0)
        def _():
            left(self.own).start()

        @pl.when(z < self.chips - 1)
        def _():
            right(self.own).start()

        side(self.own).start()

    def wait_block(self, b):
        me, z, c, mp = place()
        remote(self.full.at[b], self.full.at[b], self.side.at[0], self.recv.at[b], me, mp).wait_recv()

    def stage(self, k):
        me, z, c, mp = place()

        @pl.when(z + k < self.chips)
        def _():
            oz = z + k
            self.wait_block(2 * oz + c)
            left, right, side = self.copies(oz)

            @pl.when(z > 0)
            def _():
                left(self.full.at[2 * oz + c]).start()

            side(self.full.at[2 * oz + c]).start()

        @pl.when(z - k >= 0)
        def _():
            oz = z - k
            self.wait_block(2 * oz + c)
            left, right, side = self.copies(oz)

            @pl.when(z < self.chips - 1)
            def _():
                right(self.full.at[2 * oz + c]).start()

            side(self.full.at[2 * oz + c]).start()

    def drain(self):
        me, z, c, mp = place()
        for oz in range(self.chips):
            left, right, side = self.copies(oz)

            @pl.when((z > 0) & (oz >= z))
            def _():
                left(self.full.at[2 * oz + c]).wait_send()

            @pl.when((z < self.chips - 1) & (oz <= z))
            def _():
                right(self.full.at[2 * oz + c]).wait_send()

            side(self.full.at[2 * oz + c]).wait_send()


class GroupGather:
    def __init__(self, size, own, full, sems):
        self.size, self.own, self.full = size, own, full
        self.send, self.recv = sems
        self.half = full.shape[1] // 2

    def to(self, src, origin, part, slot, target):
        me, z, c, mp = place()
        rows = self.full.at[origin] if part is None else self.full.at[origin, pl.ds(part * self.half, self.half)]
        sem = self.recv.at[origin, 0 if part is None else part]
        return remote(src, rows, self.send.at[slot], sem, me, target)

    def start(self):
        me, z, c, mp = place()
        for slot, peer in self.peers():
            self.to(self.own, mp, None, slot, peer).start()

    def peers(self):
        me, z, c, mp = place()
        if self.size == 4:
            x_peer = mp + 1 - 2 * lax.rem(mp, 2)
            return ((0, x_peer), (1, lax.rem(mp + 2, 4)))
        return tuple((k - 1, lax.rem(mp + k, self.size)) for k in range(1, self.size))

    def relays(self):
        (_, x_peer), (_, y_peer) = self.peers()
        return (
            self.to(self.full.at[x_peer, pl.ds(0, self.half)], x_peer, 0, 2, y_peer),
            self.to(self.full.at[y_peer, pl.ds(self.half, self.half)], y_peer, 1, 3, x_peer),
        )

    def relay(self):
        for slot, peer in self.peers():
            self.to(self.full.at[peer], peer, None, slot, peer).wait_recv()
        if self.size == 4:
            for copy in self.relays():
                copy.start()

    def finish(self):
        me, z, c, mp = place()
        if self.size == 4:
            far = 3 - mp
            for part in (0, 1):
                rows = self.full.at[far, pl.ds(part * self.half, self.half)]
                self.to(rows, far, part, 0, mp).wait_recv()

    def drain(self):
        me, z, c, mp = place()
        for slot, peer in self.peers():
            self.to(self.own, mp, None, slot, peer).wait_send()
        if self.size == 4:
            for copy in self.relays():
                copy.wait_send()


def row_gather_sems(dp_size):
    chips = dp_size // 2
    return [pltpu.SemaphoreType.DMA((n,)) for n in (dp_size, chips, chips, chips)]


def group_gather_sems(mp_size):
    return [pltpu.SemaphoreType.DMA((max(4, mp_size - 1),)), pltpu.SemaphoreType.DMA((mp_size, 2))]


def gelu_pair(v):
    k0, k1 = 0.7978845608028654, 0.044715
    square = v * v
    t = jnp.tanh(k0 * (v + k1 * v * square))
    half = 0.5 * (1.0 + t)
    slope = half + 0.5 * v * (1.0 - t * t) * (k0 + 3.0 * k0 * k1 * square)
    return v * half, slope


def up_kernel(
    dp_size,
    mp_size,
    tokens,
    gain,
    shift,
    cot,
    up_master,
    up_bias,
    qkv_bias,
    qkv_low,
    dense_low,
    x_out,
    cot_out,
    up_out,
    hidden_out,
    slope_out,
    qkv_out,
    dense_out,
    projected_out,
    x_all,
    up_all,
    acc,
    hidden,
    slope,
    *sems,
):
    chips = dp_size // 2
    row_sems, x_sems, cot_sems = sems[0:4], sems[4:6], sems[6:8]
    out_sem = sems[8]
    qkv_gather = RowGather(chips, qkv_low, qkv_out, sems[9:13])
    dense_gather = RowGather(chips, dense_low, dense_out, sems[13:17])
    me, z, c, mp = place()
    rows = tokens.shape[0]
    length = rows * mp_size
    depth, width = up_all.shape[1], up_all.shape[2]

    values = tokens[...].astype(F32)
    centre = values - jnp.mean(values, axis=-1, keepdims=True)
    spread = jnp.mean(centre * centre, axis=-1, keepdims=True)
    x_all[mp] = (centre * lax.rsqrt(spread + EPSILON) * gain[...] + shift[...]).astype(BF)
    up_all[me] = up_master[...].astype(BF)

    greet(chips, mp_size)
    weights = RowGather(chips, up_all.at[me], up_all, row_sems)
    x_gather = GroupGather(mp_size, x_all.at[mp], x_all, x_sems)
    cot_gather = GroupGather(mp_size, cot, cot_out, cot_sems)
    x_gather.start()
    weights.start()
    own_cot = pltpu.make_async_copy(cot, cot_out.at[mp], out_sem.at[0])
    own_cot.start()
    own_blocks = [
        pltpu.make_async_copy(qkv_low, qkv_out.at[me], out_sem.at[5]),
        pltpu.make_async_copy(dense_low, dense_out.at[me], out_sem.at[6]),
    ]
    for copy in own_blocks:
        copy.start()

    def product(oz, first=False):
        cols = pl.ds(pl.multiple_of(oz * (2 * depth), 2 * depth), 2 * depth)

        def tile(i, carry):
            r, n = i // (width // 512), lax.rem(i, width // 512)
            n0 = pl.ds(pl.multiple_of(n * 512, 512), 512)
            left = x_all[r, :, cols]
            right = up_all[pl.ds(2 * oz, 2), :, n0].reshape(2 * depth, 512)
            term = dot(left, right)
            if first:
                acc[r, :, n0] = term + up_bias[:, n0]
            else:
                acc[r, :, n0] += term
            return carry

        lax.fori_loop(0, mp_size * (width // 512), tile, 0)

    x_gather.relay()
    weights.stage(1)
    x_gather.finish()
    cot_gather.start()
    x_copy = pltpu.make_async_copy(x_all, x_out, out_sem.at[1])
    x_copy.start()
    weights.wait_block(2 * z + 1 - c)
    product(z, True)
    for k in range(1, chips):
        if k > 1:
            weights.stage(k)
        if k == min(2, chips - 1):
            qkv_gather.start()
        for oz, valid in ((z + k, z + k < chips), (z - k, z - k >= 0)):

            @pl.when(valid)
            def _():
                weights.wait_block(2 * oz + 1 - c)
                product(oz)

        if k == min(2, chips - 1):
            cot_gather.relay()
    up_copy = pltpu.make_async_copy(up_all, up_out, out_sem.at[2])
    up_copy.start()
    qkv_gather.stage(1)
    dense_gather.start()

    def finish(i, carry):
        r, n = i // (width // 512), lax.rem(i, width // 512)
        n0 = pl.ds(pl.multiple_of(n * 512, 512), 512)
        high, grad = gelu_pair(acc[r, :, n0])
        hidden[r, :, n0] = high.astype(BF)
        slope[r, :, n0] = grad.astype(BF)
        return carry

    lax.fori_loop(0, mp_size * (width // 512), finish, 0)
    hidden_copy = pltpu.make_async_copy(hidden, hidden_out, out_sem.at[3])
    slope_copy = pltpu.make_async_copy(slope, slope_out, out_sem.at[4])
    hidden_copy.start()
    slope_copy.start()
    for k in range(2, chips):
        qkv_gather.stage(k)
        dense_gather.stage(k - 1)
    for oz in range(chips):
        qkv_gather.wait_block(2 * oz + 1 - c)
    weights.drain()
    up_copy.wait()
    own_blocks[0].wait()
    thirds = qkv_low.shape[1]
    qkv_load = pltpu.make_async_copy(qkv_out, up_all.at[:, :, pl.ds(0, thirds)], out_sem.at[5])
    qkv_load.start()
    qkv_load.wait()
    part = 512 if thirds % 512 == 0 else 256

    def project(i, carry):
        r, n = i // (thirds // part), lax.rem(i, thirds // part)
        n0 = pl.ds(pl.multiple_of(n * part, part), part)
        acc[r, :, n0] = dot(x_all[r], up_all[:, :, n0].reshape(dp_size * depth, part)) + qkv_bias[:, n0]
        return carry

    lax.fori_loop(0, mp_size * (thirds // part), project, 0)
    projected_copy = pltpu.make_async_copy(acc.at[:, :, pl.ds(0, thirds)], projected_out, out_sem.at[2])
    projected_copy.start()
    dense_gather.stage(chips - 1)
    for oz in range(chips):
        dense_gather.wait_block(2 * oz + 1 - c)
    qkv_gather.drain()
    dense_gather.drain()
    cot_gather.finish()
    x_gather.drain()
    cot_gather.drain()
    for copy in (own_cot, x_copy, projected_copy, hidden_copy, slope_copy, own_blocks[1]):
        copy.wait()


def up_stage(dp_size, mp_size, tokens, gain, shift, cot, up_master, up_bias, qkv_bias, qkv_low, dense_low):
    rows, model = tokens.shape
    depth, width = up_master.shape
    shape = jax.ShapeDtypeStruct
    outs = (
        shape((mp_size, rows, model), BF),
        shape((mp_size, rows, model), BF),
        shape((dp_size, depth, width), BF),
        shape((mp_size, rows, width), BF),
        shape((mp_size, rows, width), BF),
        shape((dp_size, *qkv_low.shape), BF),
        shape((dp_size, *dense_low.shape), BF),
        shape((mp_size, rows, qkv_low.shape[1]), F32),
    )
    return pl.pallas_call(
        partial(up_kernel, dp_size, mp_size),
        out_shape=outs,
        in_specs=[VM] * 7 + [ANY] * 2,
        out_specs=[ANY] * 8,
        scratch_shapes=[
            pltpu.VMEM((mp_size, rows, model), BF),
            pltpu.VMEM((dp_size, depth, width), BF),
            pltpu.VMEM((mp_size, rows, width), F32),
            pltpu.VMEM((mp_size, rows, width), BF),
            pltpu.VMEM((mp_size, rows, width), BF),
            *row_gather_sems(dp_size),
            *group_gather_sems(mp_size),
            *group_gather_sems(mp_size),
            pltpu.SemaphoreType.DMA((7,)),
            *row_gather_sems(dp_size),
            *row_gather_sems(dp_size),
        ],
        compiler_params=pltpu.CompilerParams(
            collective_id=1, has_side_effects=True, vmem_limit_bytes=58 << 20
        ),
        name="up_stage",
    )(tokens, gain.reshape(1, -1), shift.reshape(1, -1), cot, up_master, up_bias.reshape(1, -1), qkv_bias, qkv_low, dense_low)


def attention_kernel(
    dp_size,
    mp_size,
    pairs,
    bias,
    q_in,
    k_in,
    v_in,
    out_grad,
    rot,
    cot_all,
    hidden,
    down_low,
    out,
    q_grad,
    k_grad,
    v_grad,
    q_sum,
    k_sum,
    v_sum,
    down_share,
    down_full,
    k_acc,
    v_acc,
    flip,
    give,
    own_sem,
    *scratch,
):
    length = q_in.shape[0]
    block = 256
    blocks = length // block

    chips = dp_size // 2
    me, z, c, mp = place()
    down = RowScatter(chips, cot_all, (hidden,), flip, give, *scratch[:2], scratch[2:7])
    gather = RowGather(chips, down_low, down_full, scratch[7:])
    own_block = pltpu.make_async_copy(down_low, down_full.at[me], own_sem)

    @pl.when(pl.program_id(0) == 0)
    def _():
        greet(chips, mp_size)
        gather.start()
        own_block.start()
        down.swap()
        down.collect()

    def turn(values, sign):
        return (
            values * rot[0]
            + sign * (pltpu.roll(values, 128 - ROT_DIM // 2, 1) * rot[1] + pltpu.roll(values, ROT_DIM // 2, 1) * rot[2])
        )

    scale = HEAD_DIM ** (-0.5)
    q_low = (turn(q_in[...], 1.0).astype(BF).astype(F32) * scale).astype(BF)
    k_low = turn(k_in[...], 1.0).astype(BF)
    v_low = v_in[...].astype(BF)
    grad = out_grad[...]
    k_flip, v_flip = k_low.T, v_low.T
    lane = lax.broadcasted_iota(jnp.int32, (length, 128), 1) < HEAD_DIM
    row = lax.broadcasted_iota(jnp.int32, (128, length), 0) < HEAD_DIM
    zero = jnp.zeros((), BF)
    k_acc[...] = jnp.zeros_like(k_acc)
    v_acc[...] = jnp.zeros_like(v_acc)
    heads = []
    for h in range(2):
        lanes, rows = (lane, row) if h == 0 else (~lane, ~row)
        heads.append(
            (
                jnp.where(lanes, q_low, zero),
                jnp.where(lanes, k_low, zero),
                jnp.where(lanes, v_low, zero),
                jnp.where(lanes, grad, zero),
                jnp.where(rows, k_flip, zero),
                jnp.where(rows, v_flip, zero),
            )
        )
    for i in range(blocks):
        here = slice(block * i, block * (i + 1))
        stop = min(length, block * (i + 2))
        parts = [(0, block * i)] if i else []
        parts.append((block * i, stop))
        out_flip = jnp.zeros((128, block), F32)
        q_flip = jnp.zeros((128, block), F32)
        for q_h, k_h, v_h, grad_h, kt_h, vt_h in heads:
            scores = [dot(k_h[a:b], q_low[here], 1, 1) for a, b in parts]
            scores[-1] = scores[-1] + bias[i, : stop - block * i]
            top = scores[-1].max(0, keepdims=True)
            for s in scores[:-1]:
                top = jnp.maximum(top, s.max(0, keepdims=True))
            expo = [jnp.exp(s - top) for s in scores]
            total = expo[0].sum(0, keepdims=True)
            for e in expo[1:]:
                total = total + e.sum(0, keepdims=True)
            share = 1.0 / total
            probs = [e * share for e in expo]
            grads = [dot(v_h[a:b], grad[here], 1, 1) for a, b in parts]
            inner = (probs[0] * grads[0]).sum(0, keepdims=True)
            for p, g in zip(probs[1:], grads[1:]):
                inner = inner + (p * g).sum(0, keepdims=True)
            for (a, b), p, g in zip(parts, probs, grads):
                p_low = p.astype(BF)
                s_grad = (p * (g - inner)).astype(BF)
                out_flip = out_flip + dot(vt_h[:, a:b], p_low)
                q_flip = q_flip + dot(kt_h[:, a:b], s_grad)
                v_acc[a:b] += dot(p_low, grad_h[here])
                k_acc[a:b] += dot(s_grad, q_h[here])
        out[here] = out_flip.T.astype(BF)
        q_rows = q_flip.T * scale
        q_back = (
            q_rows * rot[0, here]
            - pltpu.roll(q_rows, 128 - ROT_DIM // 2, 1) * rot[1, here]
            - pltpu.roll(q_rows, ROT_DIM // 2, 1) * rot[2, here]
        )
        q_grad[here] = q_back.astype(BF)
    k_grad[...] = turn(k_acc[...], -1.0).astype(BF)
    v_grad[...] = v_acc[...].astype(BF)
    for total_out, rows_out in ((q_sum, q_grad), (k_sum, k_grad), (v_sum, v_grad)):
        total_out[...] = jnp.sum(rows_out[...].astype(F32), axis=0, keepdims=True)
    for i in range(pairs):

        @pl.when(pl.program_id(0) == i)
        def _():
            for s in range(chips - 1):
                if min(s, pairs - 1) == i:
                    gather.stage(s + 1)
                    if s > 0:
                        down.relay(s)
            if i == pairs - 1:
                down.finish(down_share)
                for oz in range(chips):
                    gather.wait_block(2 * oz + 1 - c)
                own_block.wait()
                down.drain_swap()
                down.drain()
                gather.drain()


def mask_bias(start, length):
    block = 256
    parts = []
    for i in range(length // block):
        keys = block * i + lax.broadcasted_iota(jnp.int32, (2 * block, block), 0)
        places = block * i + lax.broadcasted_iota(jnp.int32, (2 * block, block), 1)
        inside = (keys >= start) & (keys < start + PIECE) & (places >= start) & (places < start + PIECE)
        parts.append(jnp.where((keys <= places) | inside, 0.0, NEGATIVE))
    return jnp.stack(parts)


def rotary_lanes(length):
    half_dim = ROT_DIM // 2
    lane = jnp.arange(128) % HEAD_DIM
    frequency = 10000.0 ** (-jnp.arange(half_dim).astype(F32) * 2.0 / ROT_DIM)
    angles = jnp.arange(length).astype(F32)[:, None] * frequency[None, :]
    cosine = jnp.tile(jnp.cos(angles), (1, 128 // half_dim))
    sine = jnp.tile(jnp.sin(angles), (1, 128 // half_dim))
    turned = lane[None, :] < ROT_DIM
    first = lane[None, :] < half_dim
    return jnp.stack(
        [
            jnp.where(turned, cosine, 1.0),
            jnp.where(first, -sine, 0.0),
            jnp.where(turned & ~first, sine, 0.0),
        ]
    )


def attention(dp_size, mp_size, projected, out_grad, start, cot_all, hidden, down_low):
    length, width = out_grad.shape
    pairs, chips = width // 128, dp_size // 2
    depth, inner = down_low.shape
    shape = jax.ShapeDtypeStruct

    def rows(shift):
        return pl.BlockSpec((length, 128), lambda i: (0, i + shift))

    def whole(*dims):
        return pl.BlockSpec(dims, lambda i: (0,) * len(dims), pipeline_mode=pl.Buffered(1))

    total = pl.BlockSpec((1, 128), lambda i: (0, i))
    return pl.pallas_call(
        partial(attention_kernel, dp_size, mp_size, pairs),
        grid=(pairs,),
        in_specs=[
            whole(length // 256, 512, 256),
            rows(0),
            rows(pairs),
            rows(2 * pairs),
            rows(0),
            whole(3, length, 128),
            whole(*cot_all.shape),
            whole(*hidden.shape),
            ANY,
        ],
        out_specs=[rows(0)] * 4 + [total] * 3 + [pl.BlockSpec((depth, inner), lambda i: (0, 0)), ANY],
        out_shape=[shape((length, width), BF)] * 4
        + [shape((1, width), F32)] * 3
        + [shape((depth, inner), F32), shape((dp_size, depth, inner), BF)],
        scratch_shapes=[
            pltpu.VMEM((length, 128), F32),
            pltpu.VMEM((length, 128), F32),
            pltpu.VMEM((depth, length), BF),
            pltpu.VMEM((chips, depth, inner), BF),
            pltpu.SemaphoreType.DMA,
            *row_scatter_scratch(chips, depth, inner),
            *row_gather_sems(dp_size),
        ],
        compiler_params=pltpu.CompilerParams(
            collective_id=4, has_side_effects=True, vmem_limit_bytes=62 << 20
        ),
        cost_estimate=pl.CostEstimate(
            flops=16 * length * length * width + 2 * length * cot_all.shape[1] * inner,
            bytes_accessed=16 * length * width,
            transcendentals=length * length * width // 64,
        ),
        name="attention",
    )(
        mask_bias(start[0], length),
        projected,
        projected,
        projected,
        out_grad,
        rotary_lanes(length),
        cot_all,
        hidden,
        down_low,
    )


def flat(ref, cols):
    values = ref[..., cols]
    return values.reshape(-1, values.shape[-1])


class RowScatter:
    pieces = 2

    def __init__(self, chips, left, rights, flip, give, part, land, sems):
        self.chips, self.left, self.rights, self.flip = chips, left, rights, flip
        self.give, self.part, self.land = give, part, land
        self.sib_send, self.sib_recv, self.send_l, self.send_r, self.recv = sems
        self.depth = part.shape[1]

    def target(self, p):
        me, z, c, mp = place()
        s, side = p // 2, lax.rem(p, 2)
        far = self.chips - 1
        t = jnp.where(side == 0, z + s - far, z - s + far)
        return t, (t >= 0) & (t < self.chips)

    def block(self, t, core, store):
        b = 2 * t + core
        cols = pl.ds(pl.multiple_of(b * self.depth, self.depth), self.depth)
        self.flip[...] = flat(self.left, cols).T
        place_at = 0
        for right in self.rights:
            width = right.shape[-1]
            tile = min(512, width)
            for n in range(0, width, tile):
                product = dot(self.flip[...], flat(right, slice(n, n + tile)))
                store(slice(place_at + n, place_at + n + tile), product)
            place_at += width

    def sibling(self, t):
        me, z, c, mp = place()
        return remote(
            self.give.at[t], self.part.at[t], self.sib_send.at[t], self.sib_recv.at[t], 2 * z + 1 - c, mp
        )

    def rows(self, q):
        return pl.ds(q * (self.depth // self.pieces), self.depth // self.pieces)

    def to_left(self, t, q):
        me, z, c, mp = place()
        r = self.rows(q)
        return remote(
            self.part.at[t, r], self.land.at[t, r], self.send_l.at[t, q], self.recv.at[t, q], me - 2, mp
        )

    def to_right(self, t, q):
        me, z, c, mp = place()
        r = self.rows(q)
        slot = jnp.where(t > z + 1, t, self.chips)
        return remote(
            self.part.at[t, r], self.land.at[slot, r], self.send_r.at[t, q], self.recv.at[slot, q], me + 2, mp
        )

    def landed(self, slot, q):
        me, z, c, mp = place()
        here = self.land.at[slot, self.rows(q)]
        remote(here, here, self.send_l.at[0, 0], self.recv.at[slot, q], me, mp).wait_recv()

    def swap(self):
        me, z, c, mp = place()

        def step(p, carry):
            t, valid = self.target(p)

            @pl.when(valid)
            def _():
                def store(cols, values):
                    self.give[t, :, cols] = values.astype(BF)

                self.block(t, 1 - c, store)
                self.sibling(t).start()

            return carry

        lax.fori_loop(0, 2 * self.chips - 1, step, 0)

    def collect(self):
        me, z, c, mp = place()
        last = self.chips - 1

        def step(p, carry):
            t, valid = self.target(p)

            @pl.when(valid)
            def _():
                self.sibling(t).wait_recv()

                def store(cols, values):
                    self.part[t, :, cols] = (values + self.part[t, :, cols].astype(F32)).astype(BF)

                self.block(t, c, store)

                @pl.when((t < z) & (z == last))
                def _():
                    for q in range(self.pieces):
                        self.to_left(t, q).start()

                @pl.when((t > z) & (z == 0))
                def _():
                    for q in range(self.pieces):
                        self.to_right(t, q).start()

            return carry

        lax.fori_loop(0, 2 * self.chips - 1, step, 0)

    def add(self, t, slot, q):
        r = self.rows(q)
        self.landed(slot, q)
        self.part[t, r] = (self.part[t, r].astype(F32) + self.land[slot, r].astype(F32)).astype(BF)

    def relay(self, s):
        me, z, c, mp = place()
        last = self.chips - 1
        for q in range(self.pieces):
            t = z + s - last

            @pl.when((t >= 0) & (z < last))
            def _():
                self.add(t, t, q)
                self.to_left(t, q).start()

            u = z - s + last

            @pl.when((u <= last) & (z > 0))
            def _():
                self.add(u, u, q)
                self.to_right(u, q).start()

    def finish(self, result):
        me, z, c, mp = place()
        for q in range(self.pieces):
            r = self.rows(q)
            result[r] = self.part[z, r].astype(F32)

            @pl.when(z < self.chips - 1)
            def _():
                self.landed(z, q)
                result[r] += self.land[z, r].astype(F32)

            @pl.when(z > 0)
            def _():
                self.landed(self.chips, q)
                result[r] += self.land[self.chips, r].astype(F32)

    def drain_swap(self):
        def step(t, carry):
            self.sibling(t).wait_send()
            return carry

        lax.fori_loop(0, self.chips, step, 0)

    def drain(self):
        me, z, c, mp = place()

        def step(t, carry):
            for q in range(self.pieces):

                @pl.when(t < z)
                def _():
                    self.to_left(t, q).wait_send()

                @pl.when(t > z)
                def _():
                    self.to_right(t, q).wait_send()

            return carry

        lax.fori_loop(0, self.chips, step, 0)


def row_scatter_scratch(chips, depth, width):
    return [
        pltpu.VMEM((chips, depth, width), BF),
        pltpu.VMEM((chips + 1, depth, width), BF),
        pltpu.SemaphoreType.DMA((chips,)),
        pltpu.SemaphoreType.DMA((chips,)),
        pltpu.SemaphoreType.DMA((chips, RowScatter.pieces)),
        pltpu.SemaphoreType.DMA((chips, RowScatter.pieces)),
        pltpu.SemaphoreType.DMA((chips + 1, RowScatter.pieces)),
    ]


class GroupScatter:
    def __init__(self, size, blocks, parts, land, send, recv):
        self.size, self.blocks, self.parts, self.land, self.send, self.recv = size, blocks, parts, land, send, recv
        self.depth = parts.shape[2] // blocks

    def copy(self, k, j):
        me, z, c, mp = place()
        peer = lax.rem(mp + k, self.size)
        cols = pl.ds(pl.multiple_of(j * self.depth, self.depth), self.depth)
        return remote(
            self.parts.at[peer, :, cols],
            self.land.at[mp, :, cols],
            self.send.at[k, j],
            self.recv.at[mp, j],
            me,
            peer,
        )

    def start(self, j):
        for k in range(1, self.size):
            self.copy(k, j).start()

    def arrive(self):
        me, z, c, mp = place()

        def step(j, carry):
            cols = pl.ds(pl.multiple_of(j * self.depth, self.depth), self.depth)
            for k in range(1, self.size):
                origin = lax.rem(mp + k, self.size)
                here = self.land.at[origin, :, cols]
                remote(here, here, self.send.at[0, 0], self.recv.at[origin, j], me, origin).wait_recv()
            return carry

        lax.fori_loop(0, self.blocks, step, 0)

    def total(self, rows):
        me, z, c, mp = place()
        sums = self.parts[mp, rows].astype(F32)
        for k in range(1, self.size):
            sums = sums + self.land[lax.rem(mp + k, self.size), rows].astype(F32)
        return sums

    def drain(self):
        def step(j, carry):
            for k in range(1, self.size):
                self.copy(k, j).wait_send()
            return carry

        lax.fori_loop(0, self.blocks, step, 0)


def grad_kernel(
    dp_size,
    mp_size,
    x_all,
    pre_grad,
    attended,
    hidden_all,
    cot_all,
    qkv_full,
    up_full,
    dense_full,
    down_full,
    query_grad,
    key_grad,
    value_grad,
    query_sum,
    key_sum,
    value_sum,
    up_sum,
    tokens,
    cot,
    gain,
    out_bias,
    dense_share,
    qkv_share,
    up_share,
    output,
    input_grad,
    totals,
    x_buf,
    pre,
    mixed_buf,
    attended_buf,
    hidden_buf,
    wide_buf,
    thin_buf,
    flip,
    give,
    first,
    second,
    load_sem,
    stream_sem,
    *scratch,
):
    me, z, c, mp = place()
    chips = dp_size // 2
    rows, model = tokens.shape
    width, inner = query_grad.shape[1], up_sum.shape[1]
    depth = model // dp_size
    qkv_scratch, up_scratch, dense_scratch, rest = scratch[:7], scratch[7:14], scratch[14:21], scratch[21:]
    grads = (query_grad, key_grad, value_grad)
    give_qkv = give.at[:, :, pl.ds(0, 3 * width)]
    give_up = give.at[:, :, pl.ds(0, inner)]
    give_dense = give.at[:, :, pl.ds(0, width)]
    dense = RowScatter(
        chips, mixed_buf, (attended_buf,), flip, give_dense, *dense_scratch[:2], dense_scratch[2:]
    )
    qkv = RowScatter(chips, x_buf, grads, flip, give_qkv, *qkv_scratch[:2], qkv_scratch[2:])
    up = RowScatter(chips, x_buf, (pre,), flip, give_up, *up_scratch[:2], up_scratch[2:])
    normed_group = GroupScatter(mp_size, dp_size, x_buf, *rest[:3])
    mixed_group = GroupScatter(mp_size, dp_size, mixed_buf, *rest[3:6])
    send_1, recv_1, send_2, recv_2 = rest[6:]

    loads = [
        pltpu.make_async_copy(source, target, load_sem.at[n])
        for n, (source, target) in enumerate(
            (
                (cot_all, mixed_buf),
                (attended, attended_buf),
                (x_all, x_buf),
                (pre_grad, pre),
                (hidden_all, hidden_buf),
                (tokens, rest[0].at[mp]),
                (cot, rest[3].at[mp]),
            )
        )
    ]
    for load in loads:
        load.start()

    def stream(wide, thin):
        def copies(j):
            slot = lax.rem(j, 2)
            r = pl.ds(pl.multiple_of(j * depth, depth), depth)
            return (
                pltpu.make_async_copy(wide.at[r], wide_buf.at[slot], stream_sem.at[0, slot]),
                pltpu.make_async_copy(
                    thin.at[r], thin_buf.at[slot, :, pl.ds(0, thin.shape[1])], stream_sem.at[1, slot]
                ),
            )

        return copies

    normed_stream = stream(up_full, qkv_full)
    mixed_stream = stream(down_full, dense_full)

    def partial_sums(copies, wide, thins, target, group_out):
        half = mp_size // 2

        def step(j, carry):
            slot = lax.rem(j, 2)
            for copy in copies(j):
                copy.wait()

            @pl.when(j + 1 < dp_size)
            def _():
                for copy in copies(j + 1):
                    copy.start()

            cols = pl.ds(pl.multiple_of(j * depth, depth), depth)
            for h in range(2):
                group = pl.ds(h * half, half)
                left = wide[group].reshape(half * rows, inner)
                sums = dot(left, wide_buf[slot], 1, 1)
                for n, thin in enumerate(thins):
                    left = thin[pl.ds(h * half * rows, half * rows), :]
                    sums = sums + dot(left, thin_buf[slot, :, n * width : (n + 1) * width], 1, 1)
                target[group, :, cols] = sums.astype(BF).reshape(half, rows, depth)
            group_out.start(j)
            return carry

        lax.fori_loop(0, dp_size, step, 0)

    for copy in mixed_stream(0):
        copy.start()
    greet_all(dp_size, mp_size)
    loads[0].wait()
    loads[1].wait()
    dense.swap()
    dense.collect()
    dense.drain_swap()
    loads[2].wait()
    qkv.swap()
    qkv.collect()
    if chips > 2:
        dense.relay(1)
    loads[4].wait()
    partial_sums(mixed_stream, hidden_buf, (attended_buf,), mixed_buf, mixed_group)
    for copy in normed_stream(0):
        copy.start()
    for s in range(2, chips - 1):
        dense.relay(s)
    if chips > 2:
        qkv.relay(1)
    loads[3].wait()
    qkv.drain_swap()
    up.swap()
    up.collect()
    dense.finish(dense_share)
    partial_sums(normed_stream, pre, grads, x_buf, normed_group)
    for s in range(2, chips - 1):
        qkv.relay(s)
    if chips > 2:
        up.relay(1)
    qkv.finish(qkv_share)

    normed_group.arrive()
    loads[5].wait()
    loads[6].wait()
    tile = 64
    second[me] = jnp.zeros((8, model), F32)

    def norm_back(i, carry):
        r = pl.ds(pl.multiple_of(i * tile, tile), tile)
        values = rest[0][mp, r].astype(F32)
        centre = values - jnp.mean(values, axis=-1, keepdims=True)
        spread = jnp.mean(centre * centre, axis=-1, keepdims=True)
        inverse = lax.rsqrt(spread + EPSILON)
        xhat = centre * inverse
        normed_grad = normed_group.total(r)
        e = normed_grad * gain[...]
        turned = e - jnp.mean(e, axis=-1, keepdims=True) - xhat * jnp.mean(e * xhat, axis=-1, keepdims=True)
        cot_rows = rest[3][mp, r].astype(F32)
        input_grad[r] = (cot_rows + turned * inverse).astype(BF)
        second[me, 0:1] += jnp.sum(normed_grad * xhat, axis=0, keepdims=True)
        second[me, 1:2] += jnp.sum(normed_grad, axis=0, keepdims=True)
        second[me, 2:3] += jnp.sum(cot_rows, axis=0, keepdims=True)
        return carry

    lax.fori_loop(0, rows // tile, norm_back, 0)
    second[me, 3:4, :inner] = up_sum[...]
    for n, vector in enumerate((query_sum, key_sum, value_sum)):
        second[me, 4:5, n * width : (n + 1) * width] = vector[...]
    first[mp] = second[me]

    def copy_1(k):
        return remote(
            first.at[mp], first.at[mp], send_1.at[k], recv_1.at[mp], me, lax.rem(mp + k, mp_size)
        )

    def copy_2(k):
        return remote(
            second.at[me], second.at[me], send_2.at[k], recv_2.at[me], lax.rem(me + k, dp_size), mp
        )

    for k in range(1, mp_size):
        copy_1(k).start()
    for s in range(2, chips - 1):
        up.relay(s)
    mixed_group.arrive()

    def add_up(i, carry):
        r = pl.ds(pl.multiple_of(i * tile, tile), tile)
        output[r] = (rest[0][mp, r].astype(F32) + mixed_group.total(r) + out_bias[...]).astype(BF)
        return carry

    lax.fori_loop(0, rows // tile, add_up, 0)
    for k in range(1, mp_size):
        origin = lax.rem(mp + k, mp_size)
        remote(first.at[origin], first.at[origin], send_1.at[0], recv_1.at[origin], me, origin).wait_recv()
    total = first[0]
    for k in range(1, mp_size):
        total = total + first[k]
    second[me, 0:3] = total[0:3]
    for k in range(1, dp_size):
        copy_2(k).start()
    up.finish(up_share)
    for k in range(1, dp_size):
        origin = lax.rem(me + k, dp_size)
        remote(second.at[origin], second.at[origin], send_2.at[0], recv_2.at[origin], origin, mp).wait_recv()
    total = second[0]
    for k in range(1, dp_size):
        total = total + second[k]
    totals[...] = total
    for k in range(1, mp_size):
        copy_1(k).wait_send()
    for k in range(1, dp_size):
        copy_2(k).wait_send()
    up.drain_swap()
    for stream_out in (dense, qkv, up, normed_group, mixed_group):
        stream_out.drain()


def greet_all(dp_size, mp_size):
    me, z, c, mp = place()
    bar = pltpu.get_barrier_semaphore()
    for k in range(1, mp_size):
        pl.semaphore_signal(bar, 1, device_id=(me, lax.rem(mp + k, mp_size)), device_id_type=MESH)
    for k in range(1, dp_size):
        pl.semaphore_signal(bar, 1, device_id=(lax.rem(me + k, dp_size), mp), device_id_type=MESH)
    pl.semaphore_wait(bar, mp_size + dp_size - 2)


def grad_stage(dp_size, mp_size, hbm_args, grads, sums, tokens, cot, gain, out_bias):
    pre_grad = hbm_args[1]
    rows, model = tokens.shape
    length = rows * mp_size
    depth, chips = model // dp_size, dp_size // 2
    width, inner = grads[0].shape[1], pre_grad.shape[2]
    wide = max(3 * width, inner)
    shape = jax.ShapeDtypeStruct
    semaphores = pltpu.SemaphoreType.DMA
    blocks = (mp_size, dp_size)
    group = [pltpu.VMEM((mp_size, rows, model), BF), semaphores(blocks), semaphores(blocks)]
    return pl.pallas_call(
        partial(grad_kernel, dp_size, mp_size),
        out_shape=(
            shape((depth, width), F32),
            shape((depth, 3 * width), F32),
            shape((depth, inner), F32),
            shape((rows, model), BF),
            shape((rows, model), BF),
            shape((8, model), F32),
        ),
        in_specs=[ANY] * len(hbm_args) + [VM] * 7 + [ANY] * 2 + [VM] * 2,
        out_specs=[VM] * 6,
        scratch_shapes=[
            pltpu.VMEM((mp_size, rows, model), BF),
            pltpu.VMEM((mp_size, rows, inner), BF),
            pltpu.VMEM((mp_size, rows, model), BF),
            pltpu.VMEM((length, width), BF),
            pltpu.VMEM((mp_size, rows, inner), BF),
            pltpu.VMEM((2, depth, inner), BF),
            pltpu.VMEM((2, depth, 3 * width), BF),
            pltpu.VMEM((depth, length), BF),
            pltpu.VMEM((chips, depth, wide), BF),
            pltpu.VMEM((mp_size, 8, model), F32),
            pltpu.VMEM((dp_size, 8, model), F32),
            semaphores((7,)),
            semaphores((2, 2)),
            *row_scatter_scratch(chips, depth, 3 * width),
            *row_scatter_scratch(chips, depth, inner),
            *row_scatter_scratch(chips, depth, width),
            *group,
            *group,
            *[semaphores((n,)) for n in (mp_size, mp_size, dp_size, dp_size)],
        ],
        compiler_params=pltpu.CompilerParams(
            collective_id=3, has_side_effects=True, vmem_limit_bytes=67043328
        ),
        name="grad_stage",
    )(*hbm_args, *grads, *sums, tokens, cot, gain.reshape(1, -1), out_bias.reshape(1, -1))


def body(
    tokens,
    ln_gain,
    ln_bias,
    qkv_weight,
    qkv_bias,
    dense_weight,
    dense_bias,
    fc1_weight,
    fc1_bias,
    fc2_weight,
    fc2_bias,
    starts,
    cotangent,
):
    dp_size, mp_size = lax.axis_size("dp"), lax.axis_size("mp")
    x_all, cot_all, up_all, hidden_all, slope_all, qkv_all, dense_all, projected = up_stage(
        dp_size,
        mp_size,
        tokens,
        ln_gain,
        ln_bias,
        cotangent,
        fc1_weight,
        fc1_bias,
        qkv_bias.reshape(1, -1),
        qkv_weight.astype(BF).reshape(qkv_weight.shape[0], -1),
        dense_weight.astype(BF),
    )
    gathered = x_all.reshape(-1, x_all.shape[-1])
    out_rows = cot_all.reshape(gathered.shape)
    up_full = up_all.reshape(-1, up_all.shape[-1])
    hidden_low = hidden_all.reshape(-1, up_all.shape[-1])
    slope = slope_all.reshape(hidden_low.shape)
    qkv_full = qkv_all.reshape(-1, qkv_all.shape[-1])
    dense_full = dense_all.reshape(-1, dense_all.shape[-1])
    local_width = dense_full.shape[1]
    projected = projected.reshape(gathered.shape[0], -1)
    attended_grad = jnp.dot(out_rows, dense_full, preferred_element_type=jnp.float32).astype(
        jnp.bfloat16
    )
    attended, query_grad, key_grad, value_grad, query_sum, key_sum, value_sum, down_share, down_all = (
        attention(
            dp_size, mp_size, projected, attended_grad, starts, out_rows, hidden_low, fc2_weight.astype(BF)
        )
    )
    down_full = down_all.reshape(-1, down_all.shape[-1])
    hidden_grad = jnp.dot(out_rows, down_full, preferred_element_type=jnp.float32)
    pre_grad = (hidden_grad * slope).astype(jnp.bfloat16)
    up_bias_grad = jnp.sum(pre_grad.astype(jnp.float32), axis=0)
    dense_share, qkv_share, up_share, output, input_grad, totals = grad_stage(
        dp_size,
        mp_size,
        (
            x_all,
            pre_grad.reshape(hidden_all.shape),
            attended,
            hidden_all,
            cot_all,
            qkv_full,
            up_full,
            dense_full,
            down_full,
        ),
        (query_grad, key_grad, value_grad),
        (query_sum, key_sum, value_sum, up_bias_grad.reshape(1, -1)),
        tokens,
        cotangent,
        ln_gain,
        dense_bias + fc2_bias,
    )
    qkv_share = qkv_share.reshape(-1, 3, local_width)
    gain_total, shift_total, bias_total = totals[0], totals[1], totals[2]
    up_bias_total = totals[3, : up_full.shape[1]]
    qkv_bias_total = totals[4, : 3 * local_width].reshape(3, local_width)
    return (
        output,
        input_grad,
        gain_total,
        shift_total,
        qkv_share,
        qkv_bias_total,
        dense_share,
        bias_total,
        up_share,
        up_bias_total,
        down_share,
        bias_total,
    )


def solution(mesh):
    in_specs = (
        P(("dp", "mp"), None),
        P(),
        P(),
        P("dp", None, "mp"),
        P(None, "mp"),
        P("dp", "mp"),
        P(),
        P("dp", "mp"),
        P("mp"),
        P("dp", "mp"),
        P(),
        P("dp"),
        P(("dp", "mp"), None),
    )
    out_specs = (
        P(("dp", "mp"), None),
        P(("dp", "mp"), None),
        P(),
        P(),
        P("dp", None, "mp"),
        P(None, "mp"),
        P("dp", "mp"),
        P(),
        P("dp", "mp"),
        P("mp"),
        P("dp", "mp"),
        P(),
    )
    return jax.shard_map(body, mesh=mesh, in_specs=in_specs, out_specs=out_specs, check_vma=False)
```

```python
from functools import partial

import jax
import jax.numpy as jnp
from jax import lax
from jax.experimental import pallas as pl
from jax.experimental.pallas import tpu as pltpu
from jax.sharding import PartitionSpec as P

HEAD_DIM = 64
ROT_DIM = 32
LENGTH = 1024
PIECE = 256
EPSILON = 1e-05
NEGATIVE = -1e30
MESH = pl.DeviceIdType.MESH
BF = jnp.bfloat16
F32 = jnp.float32
ANY = pl.BlockSpec(memory_space=pl.ANY)
VM = pl.BlockSpec(memory_space=pltpu.VMEM)


def dot(a, b, ca=1, cb=0):
    return lax.dot_general(a, b, (((ca,), (cb,)), ((), ())), preferred_element_type=F32)


def remote(src, dst, send, recv, dp_index, mp_index):
    return pltpu.make_async_remote_copy(
        src_ref=src,
        dst_ref=dst,
        send_sem=send,
        recv_sem=recv,
        device_id=(dp_index, mp_index),
        device_id_type=MESH,
    )


def place():
    me = lax.axis_index("dp")
    return me, me // 2, lax.rem(me, 2), lax.axis_index("mp")


def greet(chips, mp_size):
    me, z, c, mp = place()
    bar = pltpu.get_barrier_semaphore()
    pl.semaphore_signal(bar, 1, device_id=(2 * z + 1 - c, mp), device_id_type=MESH)

    @pl.when(z > 0)
    def _():
        pl.semaphore_signal(bar, 1, device_id=(me - 2, mp), device_id_type=MESH)

    @pl.when(z < chips - 1)
    def _():
        pl.semaphore_signal(bar, 1, device_id=(me + 2, mp), device_id_type=MESH)

    for k in range(1, mp_size):
        pl.semaphore_signal(
            bar, 1, device_id=(me, lax.rem(mp + k, mp_size)), device_id_type=MESH
        )
    count = mp_size + jnp.where(z > 0, 1, 0) + jnp.where(z < chips - 1, 1, 0)
    pl.semaphore_wait(bar, count)


class RowGather:
    def __init__(self, chips, own, full, sems):
        self.chips, self.own, self.full = chips, own, full
        self.recv, self.left, self.right, self.side = sems

    def copies(self, oz):
        me, z, c, mp = place()
        b = 2 * oz + c
        dst = self.full.at[b]

        def make(src, send, target):
            return remote(src, dst, send.at[oz], self.recv.at[b], target, mp)

        return (
            lambda src: make(src, self.left, me - 2),
            lambda src: make(src, self.right, me + 2),
            lambda src: make(src, self.side, 2 * z + 1 - c),
        )

    def start(self):
        me, z, c, mp = place()
        left, right, side = self.copies(z)

        @pl.when(z > 0)
        def _():
            left(self.own).start()

        @pl.when(z < self.chips - 1)
        def _():
            right(self.own).start()

        side(self.own).start()

    def wait_block(self, b):
        me, z, c, mp = place()
        remote(self.full.at[b], self.full.at[b], self.side.at[0], self.recv.at[b], me, mp).wait_recv()

    def stage(self, k):
        me, z, c, mp = place()

        @pl.when(z + k < self.chips)
        def _():
            oz = z + k
            self.wait_block(2 * oz + c)
            left, right, side = self.copies(oz)

            @pl.when(z > 0)
            def _():
                left(self.full.at[2 * oz + c]).start()

            side(self.full.at[2 * oz + c]).start()

        @pl.when(z - k >= 0)
        def _():
            oz = z - k
            self.wait_block(2 * oz + c)
            left, right, side = self.copies(oz)

            @pl.when(z < self.chips - 1)
            def _():
                right(self.full.at[2 * oz + c]).start()

            side(self.full.at[2 * oz + c]).start()

    def drain(self):
        me, z, c, mp = place()
        for oz in range(self.chips):
            left, right, side = self.copies(oz)

            @pl.when((z > 0) & (oz >= z))
            def _():
                left(self.full.at[2 * oz + c]).wait_send()

            @pl.when((z < self.chips - 1) & (oz <= z))
            def _():
                right(self.full.at[2 * oz + c]).wait_send()

            side(self.full.at[2 * oz + c]).wait_send()


class GroupGather:
    def __init__(self, size, own, full, sems):
        self.size, self.own, self.full = size, own, full
        self.send, self.recv = sems
        self.half = full.shape[1] // 2

    def to(self, src, origin, part, slot, target):
        me, z, c, mp = place()
        rows = self.full.at[origin] if part is None else self.full.at[origin, pl.ds(part * self.half, self.half)]
        sem = self.recv.at[origin, 0 if part is None else part]
        return remote(src, rows, self.send.at[slot], sem, me, target)

    def start(self):
        me, z, c, mp = place()
        for slot, peer in self.peers():
            self.to(self.own, mp, None, slot, peer).start()

    def peers(self):
        me, z, c, mp = place()
        if self.size == 4:
            x_peer = mp + 1 - 2 * lax.rem(mp, 2)
            return ((0, x_peer), (1, lax.rem(mp + 2, 4)))
        return tuple((k - 1, lax.rem(mp + k, self.size)) for k in range(1, self.size))

    def relays(self):
        (_, x_peer), (_, y_peer) = self.peers()
        return (
            self.to(self.full.at[x_peer, pl.ds(0, self.half)], x_peer, 0, 2, y_peer),
            self.to(self.full.at[y_peer, pl.ds(self.half, self.half)], y_peer, 1, 3, x_peer),
        )

    def relay(self):
        for slot, peer in self.peers():
            self.to(self.full.at[peer], peer, None, slot, peer).wait_recv()
        if self.size == 4:
            for copy in self.relays():
                copy.start()

    def finish(self):
        me, z, c, mp = place()
        if self.size == 4:
            far = 3 - mp
            for part in (0, 1):
                rows = self.full.at[far, pl.ds(part * self.half, self.half)]
                self.to(rows, far, part, 0, mp).wait_recv()

    def drain(self):
        me, z, c, mp = place()
        for slot, peer in self.peers():
            self.to(self.own, mp, None, slot, peer).wait_send()
        if self.size == 4:
            for copy in self.relays():
                copy.wait_send()


def row_gather_sems(dp_size):
    chips = dp_size // 2
    return [pltpu.SemaphoreType.DMA((n,)) for n in (dp_size, chips, chips, chips)]


def group_gather_sems(mp_size):
    return [pltpu.SemaphoreType.DMA((max(4, mp_size - 1),)), pltpu.SemaphoreType.DMA((mp_size, 2))]


def gelu_pair(v):
    k0, k1 = 0.7978845608028654, 0.044715
    square = v * v
    t = jnp.tanh(k0 * (v + k1 * v * square))
    half = 0.5 * (1.0 + t)
    slope = half + 0.5 * v * (1.0 - t * t) * (k0 + 3.0 * k0 * k1 * square)
    return v * half, slope


def up_kernel(
    dp_size,
    mp_size,
    tokens,
    gain,
    shift,
    cot,
    up_master,
    up_bias,
    qkv_bias,
    qkv_low,
    dense_low,
    x_out,
    cot_out,
    up_out,
    hidden_out,
    slope_out,
    qkv_out,
    dense_out,
    projected_out,
    x_all,
    up_all,
    acc,
    hidden,
    slope,
    *sems,
):
    chips = dp_size // 2
    row_sems, x_sems, cot_sems = sems[0:4], sems[4:6], sems[6:8]
    out_sem = sems[8]
    qkv_gather = RowGather(chips, qkv_low, qkv_out, sems[9:13])
    dense_gather = RowGather(chips, dense_low, dense_out, sems[13:17])
    me, z, c, mp = place()
    rows = tokens.shape[0]
    length = rows * mp_size
    depth, width = up_all.shape[1], up_all.shape[2]

    values = tokens[...].astype(F32)
    centre = values - jnp.mean(values, axis=-1, keepdims=True)
    spread = jnp.mean(centre * centre, axis=-1, keepdims=True)
    x_all[mp] = (centre * lax.rsqrt(spread + EPSILON) * gain[...] + shift[...]).astype(BF)
    up_all[me] = up_master[...].astype(BF)

    greet(chips, mp_size)
    weights = RowGather(chips, up_all.at[me], up_all, row_sems)
    x_gather = GroupGather(mp_size, x_all.at[mp], x_all, x_sems)
    cot_gather = GroupGather(mp_size, cot, cot_out, cot_sems)
    x_gather.start()
    weights.start()
    own_cot = pltpu.make_async_copy(cot, cot_out.at[mp], out_sem.at[0])
    own_cot.start()
    own_blocks = [
        pltpu.make_async_copy(qkv_low, qkv_out.at[me], out_sem.at[5]),
        pltpu.make_async_copy(dense_low, dense_out.at[me], out_sem.at[6]),
    ]
    for copy in own_blocks:
        copy.start()

    def product(oz, first=False):
        cols = pl.ds(pl.multiple_of(oz * (2 * depth), 2 * depth), 2 * depth)

        def tile(i, carry):
            r, n = i // (width // 512), lax.rem(i, width // 512)
            n0 = pl.ds(pl.multiple_of(n * 512, 512), 512)
            left = x_all[r, :, cols]
            right = up_all[pl.ds(2 * oz, 2), :, n0].reshape(2 * depth, 512)
            term = dot(left, right)
            if first:
                acc[r, :, n0] = term + up_bias[:, n0]
            else:
                acc[r, :, n0] += term
            return carry

        lax.fori_loop(0, mp_size * (width // 512), tile, 0)

    x_gather.relay()
    weights.stage(1)
    x_gather.finish()
    cot_gather.start()
    x_copy = pltpu.make_async_copy(x_all, x_out, out_sem.at[1])
    x_copy.start()
    weights.wait_block(2 * z + 1 - c)
    product(z, True)
    for k in range(1, chips):
        if k > 1:
            weights.stage(k)
        if k == min(2, chips - 1):
            qkv_gather.start()
        for oz, valid in ((z + k, z + k < chips), (z - k, z - k >= 0)):

            @pl.when(valid)
            def _():
                weights.wait_block(2 * oz + 1 - c)
                product(oz)

        if k == min(2, chips - 1):
            cot_gather.relay()
    up_copy = pltpu.make_async_copy(up_all, up_out, out_sem.at[2])
    up_copy.start()
    qkv_gather.stage(1)
    dense_gather.start()

    def finish(i, carry):
        r, n = i // (width // 512), lax.rem(i, width // 512)
        n0 = pl.ds(pl.multiple_of(n * 512, 512), 512)
        high, grad = gelu_pair(acc[r, :, n0])
        hidden[r, :, n0] = high.astype(BF)
        slope[r, :, n0] = grad.astype(BF)
        return carry

    lax.fori_loop(0, mp_size * (width // 512), finish, 0)
    hidden_copy = pltpu.make_async_copy(hidden, hidden_out, out_sem.at[3])
    slope_copy = pltpu.make_async_copy(slope, slope_out, out_sem.at[4])
    hidden_copy.start()
    slope_copy.start()
    weights.drain()
    up_copy.wait()
    own_blocks[0].wait()
    thirds = qkv_low.shape[1]
    part = 512 if thirds % 512 == 0 else 256

    def project(oz, begins=False):
        qkv_gather.wait_block(2 * oz + 1 - c)
        pair = pl.ds(2 * oz, 2)
        load = pltpu.make_async_copy(
            qkv_out.at[pair], up_all.at[pair, :, pl.ds(0, thirds)], out_sem.at[5]
        )
        load.start()
        load.wait()
        cols = pl.ds(pl.multiple_of(oz * (2 * depth), 2 * depth), 2 * depth)

        def tile(i, carry):
            r, n = i // (thirds // part), lax.rem(i, thirds // part)
            n0 = pl.ds(pl.multiple_of(n * part, part), part)
            term = dot(x_all[r, :, cols], up_all[pair, :, n0].reshape(2 * depth, part))
            if begins:
                acc[r, :, n0] = term + qkv_bias[:, n0]
            else:
                acc[r, :, n0] += term
            return carry

        lax.fori_loop(0, mp_size * (thirds // part), tile, 0)

    project(z, True)
    for k in range(1, chips):
        if k > 1:
            qkv_gather.stage(k)
            dense_gather.stage(k - 1)
        for oz, valid in ((z + k, z + k < chips), (z - k, z - k >= 0)):

            @pl.when(valid)
            def _():
                project(oz)

    projected_copy = pltpu.make_async_copy(acc.at[:, :, pl.ds(0, thirds)], projected_out, out_sem.at[2])
    projected_copy.start()
    dense_gather.stage(chips - 1)
    for oz in range(chips):
        dense_gather.wait_block(2 * oz + 1 - c)
    qkv_gather.drain()
    dense_gather.drain()
    cot_gather.finish()
    x_gather.drain()
    cot_gather.drain()
    for copy in (own_cot, x_copy, projected_copy, hidden_copy, slope_copy, own_blocks[1]):
        copy.wait()


def up_stage(dp_size, mp_size, tokens, gain, shift, cot, up_master, up_bias, qkv_bias, qkv_low, dense_low):
    rows, model = tokens.shape
    depth, width = up_master.shape
    shape = jax.ShapeDtypeStruct
    outs = (
        shape((mp_size, rows, model), BF),
        shape((mp_size, rows, model), BF),
        shape((dp_size, depth, width), BF),
        shape((mp_size, rows, width), BF),
        shape((mp_size, rows, width), BF),
        shape((dp_size, *qkv_low.shape), BF),
        shape((dp_size, *dense_low.shape), BF),
        shape((mp_size, rows, qkv_low.shape[1]), F32),
    )
    return pl.pallas_call(
        partial(up_kernel, dp_size, mp_size),
        out_shape=outs,
        in_specs=[VM] * 7 + [ANY] * 2,
        out_specs=[ANY] * 8,
        scratch_shapes=[
            pltpu.VMEM((mp_size, rows, model), BF),
            pltpu.VMEM((dp_size, depth, width), BF),
            pltpu.VMEM((mp_size, rows, width), F32),
            pltpu.VMEM((mp_size, rows, width), BF),
            pltpu.VMEM((mp_size, rows, width), BF),
            *row_gather_sems(dp_size),
            *group_gather_sems(mp_size),
            *group_gather_sems(mp_size),
            pltpu.SemaphoreType.DMA((7,)),
            *row_gather_sems(dp_size),
            *row_gather_sems(dp_size),
        ],
        compiler_params=pltpu.CompilerParams(
            collective_id=1, has_side_effects=True, vmem_limit_bytes=58 << 20
        ),
        name="up_stage",
    )(tokens, gain.reshape(1, -1), shift.reshape(1, -1), cot, up_master, up_bias.reshape(1, -1), qkv_bias, qkv_low, dense_low)


def attention_kernel(
    dp_size,
    mp_size,
    pairs,
    bias,
    q_in,
    k_in,
    v_in,
    out_grad,
    rot,
    cot_all,
    hidden,
    down_low,
    out,
    q_grad,
    k_grad,
    v_grad,
    q_sum,
    k_sum,
    v_sum,
    down_share,
    down_full,
    k_acc,
    v_acc,
    flip,
    give,
    own_sem,
    *scratch,
):
    length = q_in.shape[0]
    block = 256
    blocks = length // block

    chips = dp_size // 2
    me, z, c, mp = place()
    down = RowScatter(chips, cot_all, (hidden,), flip, give, *scratch[:2], scratch[2:7])
    gather = RowGather(chips, down_low, down_full, scratch[7:])
    own_block = pltpu.make_async_copy(down_low, down_full.at[me], own_sem)

    @pl.when(pl.program_id(0) == 0)
    def _():
        greet(chips, mp_size)
        gather.start()
        own_block.start()
        down.swap()
        down.collect()

    def turn(values, sign):
        return (
            values * rot[0]
            + sign * (pltpu.roll(values, 128 - ROT_DIM // 2, 1) * rot[1] + pltpu.roll(values, ROT_DIM // 2, 1) * rot[2])
        )

    scale = HEAD_DIM ** (-0.5)
    q_low = (turn(q_in[...], 1.0).astype(BF).astype(F32) * scale).astype(BF)
    k_low = turn(k_in[...], 1.0).astype(BF)
    v_low = v_in[...].astype(BF)
    grad = out_grad[...]
    k_flip, v_flip = k_low.T, v_low.T
    lane = lax.broadcasted_iota(jnp.int32, (length, 128), 1) < HEAD_DIM
    row = lax.broadcasted_iota(jnp.int32, (128, length), 0) < HEAD_DIM
    zero = jnp.zeros((), BF)
    k_acc[...] = jnp.zeros_like(k_acc)
    v_acc[...] = jnp.zeros_like(v_acc)
    heads = []
    for h in range(2):
        lanes, rows = (lane, row) if h == 0 else (~lane, ~row)
        heads.append(
            (
                jnp.where(lanes, q_low, zero),
                jnp.where(lanes, k_low, zero),
                jnp.where(lanes, v_low, zero),
                jnp.where(lanes, grad, zero),
                jnp.where(rows, k_flip, zero),
                jnp.where(rows, v_flip, zero),
            )
        )
    for i in range(blocks):
        here = slice(block * i, block * (i + 1))
        stop = min(length, block * (i + 2))
        parts = [(0, block * i)] if i else []
        parts.append((block * i, stop))
        out_flip = jnp.zeros((128, block), F32)
        q_flip = jnp.zeros((128, block), F32)
        for q_h, k_h, v_h, grad_h, kt_h, vt_h in heads:
            scores = [dot(k_h[a:b], q_low[here], 1, 1) for a, b in parts]
            scores[-1] = scores[-1] + bias[i, : stop - block * i]
            top = scores[-1].max(0, keepdims=True)
            for s in scores[:-1]:
                top = jnp.maximum(top, s.max(0, keepdims=True))
            expo = [jnp.exp(s - top) for s in scores]
            total = expo[0].sum(0, keepdims=True)
            for e in expo[1:]:
                total = total + e.sum(0, keepdims=True)
            share = 1.0 / total
            probs = [e * share for e in expo]
            grads = [dot(v_h[a:b], grad[here], 1, 1) for a, b in parts]
            inner = (probs[0] * grads[0]).sum(0, keepdims=True)
            for p, g in zip(probs[1:], grads[1:]):
                inner = inner + (p * g).sum(0, keepdims=True)
            for (a, b), p, g in zip(parts, probs, grads):
                p_low = p.astype(BF)
                s_grad = (p * (g - inner)).astype(BF)
                out_flip = out_flip + dot(vt_h[:, a:b], p_low)
                q_flip = q_flip + dot(kt_h[:, a:b], s_grad)
                v_acc[a:b] += dot(p_low, grad_h[here])
                k_acc[a:b] += dot(s_grad, q_h[here])
        out[here] = out_flip.T.astype(BF)
        q_rows = q_flip.T * scale
        q_back = (
            q_rows * rot[0, here]
            - pltpu.roll(q_rows, 128 - ROT_DIM // 2, 1) * rot[1, here]
            - pltpu.roll(q_rows, ROT_DIM // 2, 1) * rot[2, here]
        )
        q_grad[here] = q_back.astype(BF)
    k_grad[...] = turn(k_acc[...], -1.0).astype(BF)
    v_grad[...] = v_acc[...].astype(BF)
    for total_out, rows_out in ((q_sum, q_grad), (k_sum, k_grad), (v_sum, v_grad)):
        total_out[...] = jnp.sum(rows_out[...].astype(F32), axis=0, keepdims=True)
    for i in range(pairs):

        @pl.when(pl.program_id(0) == i)
        def _():
            for s in range(chips - 1):
                if min(s, pairs - 1) == i:
                    gather.stage(s + 1)
                    if s > 0:
                        down.relay(s)
            if i == pairs - 1:
                down.finish(down_share)
                for oz in range(chips):
                    gather.wait_block(2 * oz + 1 - c)
                own_block.wait()
                down.drain_swap()
                down.drain()
                gather.drain()


def mask_bias(start, length):
    block = 256
    parts = []
    for i in range(length // block):
        keys = block * i + lax.broadcasted_iota(jnp.int32, (2 * block, block), 0)
        places = block * i + lax.broadcasted_iota(jnp.int32, (2 * block, block), 1)
        inside = (keys >= start) & (keys < start + PIECE) & (places >= start) & (places < start + PIECE)
        parts.append(jnp.where((keys <= places) | inside, 0.0, NEGATIVE))
    return jnp.stack(parts)


def rotary_lanes(length):
    half_dim = ROT_DIM // 2
    lane = jnp.arange(128) % HEAD_DIM
    frequency = 10000.0 ** (-jnp.arange(half_dim).astype(F32) * 2.0 / ROT_DIM)
    angles = jnp.arange(length).astype(F32)[:, None] * frequency[None, :]
    cosine = jnp.tile(jnp.cos(angles), (1, 128 // half_dim))
    sine = jnp.tile(jnp.sin(angles), (1, 128 // half_dim))
    turned = lane[None, :] < ROT_DIM
    first = lane[None, :] < half_dim
    return jnp.stack(
        [
            jnp.where(turned, cosine, 1.0),
            jnp.where(first, -sine, 0.0),
            jnp.where(turned & ~first, sine, 0.0),
        ]
    )


def attention(dp_size, mp_size, projected, out_grad, start, cot_all, hidden, down_low):
    length, width = out_grad.shape
    pairs, chips = width // 128, dp_size // 2
    depth, inner = down_low.shape
    shape = jax.ShapeDtypeStruct

    def rows(shift):
        return pl.BlockSpec((length, 128), lambda i: (0, i + shift))

    def whole(*dims):
        return pl.BlockSpec(dims, lambda i: (0,) * len(dims), pipeline_mode=pl.Buffered(1))

    total = pl.BlockSpec((1, 128), lambda i: (0, i))
    return pl.pallas_call(
        partial(attention_kernel, dp_size, mp_size, pairs),
        grid=(pairs,),
        in_specs=[
            whole(length // 256, 512, 256),
            rows(0),
            rows(pairs),
            rows(2 * pairs),
            rows(0),
            whole(3, length, 128),
            whole(*cot_all.shape),
            whole(*hidden.shape),
            ANY,
        ],
        out_specs=[rows(0)] * 4 + [total] * 3 + [pl.BlockSpec((depth, inner), lambda i: (0, 0)), ANY],
        out_shape=[shape((length, width), BF)] * 4
        + [shape((1, width), F32)] * 3
        + [shape((depth, inner), F32), shape((dp_size, depth, inner), BF)],
        scratch_shapes=[
            pltpu.VMEM((length, 128), F32),
            pltpu.VMEM((length, 128), F32),
            pltpu.VMEM((depth, length), BF),
            pltpu.VMEM((chips, depth, inner), BF),
            pltpu.SemaphoreType.DMA,
            *row_scatter_scratch(chips, depth, inner),
            *row_gather_sems(dp_size),
        ],
        compiler_params=pltpu.CompilerParams(
            collective_id=4, has_side_effects=True, vmem_limit_bytes=62 << 20
        ),
        cost_estimate=pl.CostEstimate(
            flops=16 * length * length * width + 2 * length * cot_all.shape[1] * inner,
            bytes_accessed=16 * length * width,
            transcendentals=length * length * width // 64,
        ),
        name="attention",
    )(
        mask_bias(start[0], length),
        projected,
        projected,
        projected,
        out_grad,
        rotary_lanes(length),
        cot_all,
        hidden,
        down_low,
    )


def flat(ref, cols):
    values = ref[..., cols]
    return values.reshape(-1, values.shape[-1])


class RowScatter:
    pieces = 2

    def __init__(self, chips, left, rights, flip, give, part, land, sems):
        self.chips, self.left, self.rights, self.flip = chips, left, rights, flip
        self.give, self.part, self.land = give, part, land
        self.sib_send, self.sib_recv, self.send_l, self.send_r, self.recv = sems
        self.depth = part.shape[1]

    def target(self, p):
        me, z, c, mp = place()
        s, side = p // 2, lax.rem(p, 2)
        far = self.chips - 1
        t = jnp.where(side == 0, z + s - far, z - s + far)
        return t, (t >= 0) & (t < self.chips)

    def block(self, t, core, store):
        b = 2 * t + core
        cols = pl.ds(pl.multiple_of(b * self.depth, self.depth), self.depth)
        self.flip[...] = flat(self.left, cols).T
        place_at = 0
        for right in self.rights:
            width = right.shape[-1]
            tile = min(512, width)
            for n in range(0, width, tile):
                product = dot(self.flip[...], flat(right, slice(n, n + tile)))
                store(slice(place_at + n, place_at + n + tile), product)
            place_at += width

    def sibling(self, t):
        me, z, c, mp = place()
        return remote(
            self.give.at[t], self.part.at[t], self.sib_send.at[t], self.sib_recv.at[t], 2 * z + 1 - c, mp
        )

    def rows(self, q):
        return pl.ds(q * (self.depth // self.pieces), self.depth // self.pieces)

    def to_left(self, t, q):
        me, z, c, mp = place()
        r = self.rows(q)
        return remote(
            self.part.at[t, r], self.land.at[t, r], self.send_l.at[t, q], self.recv.at[t, q], me - 2, mp
        )

    def to_right(self, t, q):
        me, z, c, mp = place()
        r = self.rows(q)
        slot = jnp.where(t > z + 1, t, self.chips)
        return remote(
            self.part.at[t, r], self.land.at[slot, r], self.send_r.at[t, q], self.recv.at[slot, q], me + 2, mp
        )

    def landed(self, slot, q):
        me, z, c, mp = place()
        here = self.land.at[slot, self.rows(q)]
        remote(here, here, self.send_l.at[0, 0], self.recv.at[slot, q], me, mp).wait_recv()

    def swap(self):
        me, z, c, mp = place()

        def step(p, carry):
            t, valid = self.target(p)

            @pl.when(valid)
            def _():
                def store(cols, values):
                    self.give[t, :, cols] = values.astype(BF)

                self.block(t, 1 - c, store)
                self.sibling(t).start()

            return carry

        lax.fori_loop(0, 2 * self.chips - 1, step, 0)

    def collect(self):
        me, z, c, mp = place()
        last = self.chips - 1

        def step(p, carry):
            t, valid = self.target(p)

            @pl.when(valid)
            def _():
                self.sibling(t).wait_recv()

                def store(cols, values):
                    self.part[t, :, cols] = (values + self.part[t, :, cols].astype(F32)).astype(BF)

                self.block(t, c, store)

                @pl.when((t < z) & (z == last))
                def _():
                    for q in range(self.pieces):
                        self.to_left(t, q).start()

                @pl.when((t > z) & (z == 0))
                def _():
                    for q in range(self.pieces):
                        self.to_right(t, q).start()

            return carry

        lax.fori_loop(0, 2 * self.chips - 1, step, 0)

    def add(self, t, slot, q):
        r = self.rows(q)
        self.landed(slot, q)
        self.part[t, r] = (self.part[t, r].astype(F32) + self.land[slot, r].astype(F32)).astype(BF)

    def relay(self, s):
        me, z, c, mp = place()
        last = self.chips - 1
        for q in range(self.pieces):
            t = z + s - last

            @pl.when((t >= 0) & (z < last))
            def _():
                self.add(t, t, q)
                self.to_left(t, q).start()

            u = z - s + last

            @pl.when((u <= last) & (z > 0))
            def _():
                self.add(u, u, q)
                self.to_right(u, q).start()

    def finish(self, result):
        me, z, c, mp = place()
        for q in range(self.pieces):
            r = self.rows(q)
            result[r] = self.part[z, r].astype(F32)

            @pl.when(z < self.chips - 1)
            def _():
                self.landed(z, q)
                result[r] += self.land[z, r].astype(F32)

            @pl.when(z > 0)
            def _():
                self.landed(self.chips, q)
                result[r] += self.land[self.chips, r].astype(F32)

    def drain_swap(self):
        def step(t, carry):
            self.sibling(t).wait_send()
            return carry

        lax.fori_loop(0, self.chips, step, 0)

    def drain(self):
        me, z, c, mp = place()

        def step(t, carry):
            for q in range(self.pieces):

                @pl.when(t < z)
                def _():
                    self.to_left(t, q).wait_send()

                @pl.when(t > z)
                def _():
                    self.to_right(t, q).wait_send()

            return carry

        lax.fori_loop(0, self.chips, step, 0)


def row_scatter_scratch(chips, depth, width):
    return [
        pltpu.VMEM((chips, depth, width), BF),
        pltpu.VMEM((chips + 1, depth, width), BF),
        pltpu.SemaphoreType.DMA((chips,)),
        pltpu.SemaphoreType.DMA((chips,)),
        pltpu.SemaphoreType.DMA((chips, RowScatter.pieces)),
        pltpu.SemaphoreType.DMA((chips, RowScatter.pieces)),
        pltpu.SemaphoreType.DMA((chips + 1, RowScatter.pieces)),
    ]


class GroupScatter:
    def __init__(self, size, blocks, parts, land, send, recv):
        self.size, self.blocks, self.parts, self.land, self.send, self.recv = size, blocks, parts, land, send, recv
        self.depth = parts.shape[2] // blocks

    def copy(self, k, j):
        me, z, c, mp = place()
        peer = lax.rem(mp + k, self.size)
        cols = pl.ds(pl.multiple_of(j * self.depth, self.depth), self.depth)
        return remote(
            self.parts.at[peer, :, cols],
            self.land.at[mp, :, cols],
            self.send.at[k, j],
            self.recv.at[mp, j],
            me,
            peer,
        )

    def start(self, j):
        for k in range(1, self.size):
            self.copy(k, j).start()

    def arrive(self):
        me, z, c, mp = place()

        def step(j, carry):
            cols = pl.ds(pl.multiple_of(j * self.depth, self.depth), self.depth)
            for k in range(1, self.size):
                origin = lax.rem(mp + k, self.size)
                here = self.land.at[origin, :, cols]
                remote(here, here, self.send.at[0, 0], self.recv.at[origin, j], me, origin).wait_recv()
            return carry

        lax.fori_loop(0, self.blocks, step, 0)

    def total(self, rows):
        me, z, c, mp = place()
        sums = self.parts[mp, rows].astype(F32)
        for k in range(1, self.size):
            sums = sums + self.land[lax.rem(mp + k, self.size), rows].astype(F32)
        return sums

    def drain(self):
        def step(j, carry):
            for k in range(1, self.size):
                self.copy(k, j).wait_send()
            return carry

        lax.fori_loop(0, self.blocks, step, 0)


def grad_kernel(
    dp_size,
    mp_size,
    x_all,
    pre_grad,
    attended,
    hidden_all,
    cot_all,
    qkv_full,
    up_full,
    dense_full,
    down_full,
    query_grad,
    key_grad,
    value_grad,
    query_sum,
    key_sum,
    value_sum,
    up_sum,
    tokens,
    cot,
    gain,
    out_bias,
    dense_share,
    qkv_share,
    up_share,
    output,
    input_grad,
    totals,
    x_buf,
    pre,
    mixed_buf,
    attended_buf,
    hidden_buf,
    wide_buf,
    thin_buf,
    flip,
    give,
    first,
    second,
    load_sem,
    stream_sem,
    *scratch,
):
    me, z, c, mp = place()
    chips = dp_size // 2
    rows, model = tokens.shape
    width, inner = query_grad.shape[1], up_sum.shape[1]
    depth = model // dp_size
    qkv_scratch, up_scratch, dense_scratch, rest = scratch[:7], scratch[7:14], scratch[14:21], scratch[21:]
    grads = (query_grad, key_grad, value_grad)
    give_qkv = give.at[:, :, pl.ds(0, 3 * width)]
    give_up = give.at[:, :, pl.ds(0, inner)]
    give_dense = give.at[:, :, pl.ds(0, width)]
    dense = RowScatter(
        chips, mixed_buf, (attended_buf,), flip, give_dense, *dense_scratch[:2], dense_scratch[2:]
    )
    qkv = RowScatter(chips, x_buf, grads, flip, give_qkv, *qkv_scratch[:2], qkv_scratch[2:])
    up = RowScatter(chips, x_buf, (pre,), flip, give_up, *up_scratch[:2], up_scratch[2:])
    normed_group = GroupScatter(mp_size, dp_size, x_buf, *rest[:3])
    mixed_group = GroupScatter(mp_size, dp_size, mixed_buf, *rest[3:6])
    send_1, recv_1, send_2, recv_2 = rest[6:]

    loads = [
        pltpu.make_async_copy(source, target, load_sem.at[n])
        for n, (source, target) in enumerate(
            (
                (cot_all, mixed_buf),
                (attended, attended_buf),
                (x_all, x_buf),
                (pre_grad, pre),
                (hidden_all, hidden_buf),
                (tokens, rest[0].at[mp]),
                (cot, rest[3].at[mp]),
            )
        )
    ]
    for load in loads:
        load.start()

    def stream(wide, thin):
        def copies(j):
            slot = lax.rem(j, 2)
            r = pl.ds(pl.multiple_of(j * depth, depth), depth)
            return (
                pltpu.make_async_copy(wide.at[r], wide_buf.at[slot], stream_sem.at[0, slot]),
                pltpu.make_async_copy(
                    thin.at[r], thin_buf.at[slot, :, pl.ds(0, thin.shape[1])], stream_sem.at[1, slot]
                ),
            )

        return copies

    normed_stream = stream(up_full, qkv_full)
    mixed_stream = stream(down_full, dense_full)

    def partial_sums(copies, wide, thins, target, group_out):
        half = mp_size // 2

        def step(j, carry):
            slot = lax.rem(j, 2)
            for copy in copies(j):
                copy.wait()

            @pl.when(j + 1 < dp_size)
            def _():
                for copy in copies(j + 1):
                    copy.start()

            cols = pl.ds(pl.multiple_of(j * depth, depth), depth)
            for h in range(2):
                group = pl.ds(h * half, half)
                left = wide[group].reshape(half * rows, inner)
                sums = dot(left, wide_buf[slot], 1, 1)
                for n, thin in enumerate(thins):
                    left = thin[pl.ds(h * half * rows, half * rows), :]
                    sums = sums + dot(left, thin_buf[slot, :, n * width : (n + 1) * width], 1, 1)
                target[group, :, cols] = sums.astype(BF).reshape(half, rows, depth)
            group_out.start(j)
            return carry

        lax.fori_loop(0, dp_size, step, 0)

    for copy in mixed_stream(0):
        copy.start()
    greet_all(dp_size, mp_size)
    loads[0].wait()
    loads[1].wait()
    dense.swap()
    dense.collect()
    dense.drain_swap()
    loads[2].wait()
    qkv.swap()
    qkv.collect()
    if chips > 2:
        dense.relay(1)
    loads[4].wait()
    partial_sums(mixed_stream, hidden_buf, (attended_buf,), mixed_buf, mixed_group)
    for copy in normed_stream(0):
        copy.start()
    for s in range(2, chips - 1):
        dense.relay(s)
    if chips > 2:
        qkv.relay(1)
    loads[3].wait()
    qkv.drain_swap()
    up.swap()
    up.collect()
    dense.finish(dense_share)
    partial_sums(normed_stream, pre, grads, x_buf, normed_group)
    for s in range(2, chips - 1):
        qkv.relay(s)
    if chips > 2:
        up.relay(1)
    qkv.finish(qkv_share)

    normed_group.arrive()
    loads[5].wait()
    loads[6].wait()
    tile = 64
    second[me] = jnp.zeros((8, model), F32)

    def norm_back(i, carry):
        r = pl.ds(pl.multiple_of(i * tile, tile), tile)
        values = rest[0][mp, r].astype(F32)
        centre = values - jnp.mean(values, axis=-1, keepdims=True)
        spread = jnp.mean(centre * centre, axis=-1, keepdims=True)
        inverse = lax.rsqrt(spread + EPSILON)
        xhat = centre * inverse
        normed_grad = normed_group.total(r)
        e = normed_grad * gain[...]
        turned = e - jnp.mean(e, axis=-1, keepdims=True) - xhat * jnp.mean(e * xhat, axis=-1, keepdims=True)
        cot_rows = rest[3][mp, r].astype(F32)
        input_grad[r] = (cot_rows + turned * inverse).astype(BF)
        second[me, 0:1] += jnp.sum(normed_grad * xhat, axis=0, keepdims=True)
        second[me, 1:2] += jnp.sum(normed_grad, axis=0, keepdims=True)
        second[me, 2:3] += jnp.sum(cot_rows, axis=0, keepdims=True)
        return carry

    lax.fori_loop(0, rows // tile, norm_back, 0)
    second[me, 3:4, :inner] = up_sum[...]
    for n, vector in enumerate((query_sum, key_sum, value_sum)):
        second[me, 4:5, n * width : (n + 1) * width] = vector[...]
    first[mp] = second[me]

    def copy_1(k):
        return remote(
            first.at[mp], first.at[mp], send_1.at[k], recv_1.at[mp], me, lax.rem(mp + k, mp_size)
        )

    def copy_2(k):
        return remote(
            second.at[me], second.at[me], send_2.at[k], recv_2.at[me], lax.rem(me + k, dp_size), mp
        )

    for k in range(1, mp_size):
        copy_1(k).start()
    for s in range(2, chips - 1):
        up.relay(s)
    mixed_group.arrive()

    def add_up(i, carry):
        r = pl.ds(pl.multiple_of(i * tile, tile), tile)
        output[r] = (rest[0][mp, r].astype(F32) + mixed_group.total(r) + out_bias[...]).astype(BF)
        return carry

    lax.fori_loop(0, rows // tile, add_up, 0)
    for k in range(1, mp_size):
        origin = lax.rem(mp + k, mp_size)
        remote(first.at[origin], first.at[origin], send_1.at[0], recv_1.at[origin], me, origin).wait_recv()
    total = first[0]
    for k in range(1, mp_size):
        total = total + first[k]
    second[me, 0:3] = total[0:3]
    for k in range(1, dp_size):
        copy_2(k).start()
    up.finish(up_share)
    for k in range(1, dp_size):
        origin = lax.rem(me + k, dp_size)
        remote(second.at[origin], second.at[origin], send_2.at[0], recv_2.at[origin], origin, mp).wait_recv()
    total = second[0]
    for k in range(1, dp_size):
        total = total + second[k]
    totals[...] = total
    for k in range(1, mp_size):
        copy_1(k).wait_send()
    for k in range(1, dp_size):
        copy_2(k).wait_send()
    up.drain_swap()
    for stream_out in (dense, qkv, up, normed_group, mixed_group):
        stream_out.drain()


def greet_all(dp_size, mp_size):
    me, z, c, mp = place()
    bar = pltpu.get_barrier_semaphore()
    for k in range(1, mp_size):
        pl.semaphore_signal(bar, 1, device_id=(me, lax.rem(mp + k, mp_size)), device_id_type=MESH)
    for k in range(1, dp_size):
        pl.semaphore_signal(bar, 1, device_id=(lax.rem(me + k, dp_size), mp), device_id_type=MESH)
    pl.semaphore_wait(bar, mp_size + dp_size - 2)


def grad_stage(dp_size, mp_size, hbm_args, grads, sums, tokens, cot, gain, out_bias):
    pre_grad = hbm_args[1]
    rows, model = tokens.shape
    length = rows * mp_size
    depth, chips = model // dp_size, dp_size // 2
    width, inner = grads[0].shape[1], pre_grad.shape[2]
    wide = max(3 * width, inner)
    shape = jax.ShapeDtypeStruct
    semaphores = pltpu.SemaphoreType.DMA
    blocks = (mp_size, dp_size)
    group = [pltpu.VMEM((mp_size, rows, model), BF), semaphores(blocks), semaphores(blocks)]
    return pl.pallas_call(
        partial(grad_kernel, dp_size, mp_size),
        out_shape=(
            shape((depth, width), F32),
            shape((depth, 3 * width), F32),
            shape((depth, inner), F32),
            shape((rows, model), BF),
            shape((rows, model), BF),
            shape((8, model), F32),
        ),
        in_specs=[ANY] * len(hbm_args) + [VM] * 7 + [ANY] * 2 + [VM] * 2,
        out_specs=[VM] * 6,
        scratch_shapes=[
            pltpu.VMEM((mp_size, rows, model), BF),
            pltpu.VMEM((mp_size, rows, inner), BF),
            pltpu.VMEM((mp_size, rows, model), BF),
            pltpu.VMEM((length, width), BF),
            pltpu.VMEM((mp_size, rows, inner), BF),
            pltpu.VMEM((2, depth, inner), BF),
            pltpu.VMEM((2, depth, 3 * width), BF),
            pltpu.VMEM((depth, length), BF),
            pltpu.VMEM((chips, depth, wide), BF),
            pltpu.VMEM((mp_size, 8, model), F32),
            pltpu.VMEM((dp_size, 8, model), F32),
            semaphores((7,)),
            semaphores((2, 2)),
            *row_scatter_scratch(chips, depth, 3 * width),
            *row_scatter_scratch(chips, depth, inner),
            *row_scatter_scratch(chips, depth, width),
            *group,
            *group,
            *[semaphores((n,)) for n in (mp_size, mp_size, dp_size, dp_size)],
        ],
        compiler_params=pltpu.CompilerParams(
            collective_id=3, has_side_effects=True, vmem_limit_bytes=67043328
        ),
        name="grad_stage",
    )(*hbm_args, *grads, *sums, tokens, cot, gain.reshape(1, -1), out_bias.reshape(1, -1))


def body(
    tokens,
    ln_gain,
    ln_bias,
    qkv_weight,
    qkv_bias,
    dense_weight,
    dense_bias,
    fc1_weight,
    fc1_bias,
    fc2_weight,
    fc2_bias,
    starts,
    cotangent,
):
    dp_size, mp_size = lax.axis_size("dp"), lax.axis_size("mp")
    x_all, cot_all, up_all, hidden_all, slope_all, qkv_all, dense_all, projected = up_stage(
        dp_size,
        mp_size,
        tokens,
        ln_gain,
        ln_bias,
        cotangent,
        fc1_weight,
        fc1_bias,
        qkv_bias.reshape(1, -1),
        qkv_weight.astype(BF).reshape(qkv_weight.shape[0], -1),
        dense_weight.astype(BF),
    )
    gathered = x_all.reshape(-1, x_all.shape[-1])
    out_rows = cot_all.reshape(gathered.shape)
    up_full = up_all.reshape(-1, up_all.shape[-1])
    hidden_low = hidden_all.reshape(-1, up_all.shape[-1])
    slope = slope_all.reshape(hidden_low.shape)
    qkv_full = qkv_all.reshape(-1, qkv_all.shape[-1])
    dense_full = dense_all.reshape(-1, dense_all.shape[-1])
    local_width = dense_full.shape[1]
    projected = projected.reshape(gathered.shape[0], -1)
    attended_grad = jnp.dot(out_rows, dense_full, preferred_element_type=jnp.float32).astype(
        jnp.bfloat16
    )
    attended, query_grad, key_grad, value_grad, query_sum, key_sum, value_sum, down_share, down_all = (
        attention(
            dp_size, mp_size, projected, attended_grad, starts, out_rows, hidden_low, fc2_weight.astype(BF)
        )
    )
    down_full = down_all.reshape(-1, down_all.shape[-1])
    hidden_grad = jnp.dot(out_rows, down_full, preferred_element_type=jnp.float32)
    pre_grad = (hidden_grad * slope).astype(jnp.bfloat16)
    up_bias_grad = jnp.sum(pre_grad.astype(jnp.float32), axis=0)
    dense_share, qkv_share, up_share, output, input_grad, totals = grad_stage(
        dp_size,
        mp_size,
        (
            x_all,
            pre_grad.reshape(hidden_all.shape),
            attended,
            hidden_all,
            cot_all,
            qkv_full,
            up_full,
            dense_full,
            down_full,
        ),
        (query_grad, key_grad, value_grad),
        (query_sum, key_sum, value_sum, up_bias_grad.reshape(1, -1)),
        tokens,
        cotangent,
        ln_gain,
        dense_bias + fc2_bias,
    )
    qkv_share = qkv_share.reshape(-1, 3, local_width)
    gain_total, shift_total, bias_total = totals[0], totals[1], totals[2]
    up_bias_total = totals[3, : up_full.shape[1]]
    qkv_bias_total = totals[4, : 3 * local_width].reshape(3, local_width)
    return (
        output,
        input_grad,
        gain_total,
        shift_total,
        qkv_share,
        qkv_bias_total,
        dense_share,
        bias_total,
        up_share,
        up_bias_total,
        down_share,
        bias_total,
    )


def solution(mesh):
    in_specs = (
        P(("dp", "mp"), None),
        P(),
        P(),
        P("dp", None, "mp"),
        P(None, "mp"),
        P("dp", "mp"),
        P(),
        P("dp", "mp"),
        P("mp"),
        P("dp", "mp"),
        P(),
        P("dp"),
        P(("dp", "mp"), None),
    )
    out_specs = (
        P(("dp", "mp"), None),
        P(("dp", "mp"), None),
        P(),
        P(),
        P("dp", None, "mp"),
        P(None, "mp"),
        P("dp", "mp"),
        P(),
        P("dp", "mp"),
        P("mp"),
        P("dp", "mp"),
        P(),
    )
    return jax.shard_map(body, mesh=mesh, in_specs=in_specs, out_specs=out_specs, check_vma=False)
```

```python
from functools import partial

import jax
import jax.numpy as jnp
from jax import lax
from jax.experimental import pallas as pl
from jax.experimental.pallas import tpu as pltpu
from jax.sharding import PartitionSpec as P

HEAD_DIM = 64
ROT_DIM = 32
LENGTH = 1024
PIECE = 256
EPSILON = 1e-05
NEGATIVE = -1e30
MESH = pl.DeviceIdType.MESH
BF = jnp.bfloat16
F32 = jnp.float32
ANY = pl.BlockSpec(memory_space=pl.ANY)
VM = pl.BlockSpec(memory_space=pltpu.VMEM)


def dot(a, b, ca=1, cb=0):
    return lax.dot_general(a, b, (((ca,), (cb,)), ((), ())), preferred_element_type=F32)


def remote(src, dst, send, recv, dp_index, mp_index):
    return pltpu.make_async_remote_copy(
        src_ref=src,
        dst_ref=dst,
        send_sem=send,
        recv_sem=recv,
        device_id=(dp_index, mp_index),
        device_id_type=MESH,
    )


def place():
    me = lax.axis_index("dp")
    return me, me // 2, lax.rem(me, 2), lax.axis_index("mp")


def greet(chips, mp_size):
    me, z, c, mp = place()
    bar = pltpu.get_barrier_semaphore()
    pl.semaphore_signal(bar, 1, device_id=(2 * z + 1 - c, mp), device_id_type=MESH)

    @pl.when(z > 0)
    def _():
        pl.semaphore_signal(bar, 1, device_id=(me - 2, mp), device_id_type=MESH)

    @pl.when(z < chips - 1)
    def _():
        pl.semaphore_signal(bar, 1, device_id=(me + 2, mp), device_id_type=MESH)

    for k in range(1, mp_size):
        pl.semaphore_signal(
            bar, 1, device_id=(me, lax.rem(mp + k, mp_size)), device_id_type=MESH
        )
    count = mp_size + jnp.where(z > 0, 1, 0) + jnp.where(z < chips - 1, 1, 0)
    pl.semaphore_wait(bar, count)


class RowGather:
    def __init__(self, chips, own, full, sems):
        self.chips, self.own, self.full = chips, own, full
        self.recv, self.left, self.right, self.side = sems

    def copies(self, oz):
        me, z, c, mp = place()
        b = 2 * oz + c
        dst = self.full.at[b]

        def make(src, send, target):
            return remote(src, dst, send.at[oz], self.recv.at[b], target, mp)

        return (
            lambda src: make(src, self.left, me - 2),
            lambda src: make(src, self.right, me + 2),
            lambda src: make(src, self.side, 2 * z + 1 - c),
        )

    def start(self):
        me, z, c, mp = place()
        left, right, side = self.copies(z)

        @pl.when(z > 0)
        def _():
            left(self.own).start()

        @pl.when(z < self.chips - 1)
        def _():
            right(self.own).start()

        side(self.own).start()

    def wait_block(self, b):
        me, z, c, mp = place()
        remote(self.full.at[b], self.full.at[b], self.side.at[0], self.recv.at[b], me, mp).wait_recv()

    def stage(self, k):
        me, z, c, mp = place()

        @pl.when(z + k < self.chips)
        def _():
            oz = z + k
            self.wait_block(2 * oz + c)
            left, right, side = self.copies(oz)

            @pl.when(z > 0)
            def _():
                left(self.full.at[2 * oz + c]).start()

            side(self.full.at[2 * oz + c]).start()

        @pl.when(z - k >= 0)
        def _():
            oz = z - k
            self.wait_block(2 * oz + c)
            left, right, side = self.copies(oz)

            @pl.when(z < self.chips - 1)
            def _():
                right(self.full.at[2 * oz + c]).start()

            side(self.full.at[2 * oz + c]).start()

    def drain(self):
        me, z, c, mp = place()
        for oz in range(self.chips):
            left, right, side = self.copies(oz)

            @pl.when((z > 0) & (oz >= z))
            def _():
                left(self.full.at[2 * oz + c]).wait_send()

            @pl.when((z < self.chips - 1) & (oz <= z))
            def _():
                right(self.full.at[2 * oz + c]).wait_send()

            side(self.full.at[2 * oz + c]).wait_send()


class GroupGather:
    def __init__(self, size, own, full, sems):
        self.size, self.own, self.full = size, own, full
        self.send, self.recv = sems
        self.half = full.shape[1] // 2

    def to(self, src, origin, part, slot, target):
        me, z, c, mp = place()
        rows = self.full.at[origin] if part is None else self.full.at[origin, pl.ds(part * self.half, self.half)]
        sem = self.recv.at[origin, 0 if part is None else part]
        return remote(src, rows, self.send.at[slot], sem, me, target)

    def start(self):
        me, z, c, mp = place()
        for slot, peer in self.peers():
            self.to(self.own, mp, None, slot, peer).start()

    def peers(self):
        me, z, c, mp = place()
        if self.size == 4:
            x_peer = mp + 1 - 2 * lax.rem(mp, 2)
            return ((0, x_peer), (1, lax.rem(mp + 2, 4)))
        return tuple((k - 1, lax.rem(mp + k, self.size)) for k in range(1, self.size))

    def relays(self):
        (_, x_peer), (_, y_peer) = self.peers()
        return (
            self.to(self.full.at[x_peer, pl.ds(0, self.half)], x_peer, 0, 2, y_peer),
            self.to(self.full.at[y_peer, pl.ds(self.half, self.half)], y_peer, 1, 3, x_peer),
        )

    def relay(self):
        for slot, peer in self.peers():
            self.to(self.full.at[peer], peer, None, slot, peer).wait_recv()
        if self.size == 4:
            for copy in self.relays():
                copy.start()

    def finish(self):
        me, z, c, mp = place()
        if self.size == 4:
            far = 3 - mp
            for part in (0, 1):
                rows = self.full.at[far, pl.ds(part * self.half, self.half)]
                self.to(rows, far, part, 0, mp).wait_recv()

    def drain(self):
        me, z, c, mp = place()
        for slot, peer in self.peers():
            self.to(self.own, mp, None, slot, peer).wait_send()
        if self.size == 4:
            for copy in self.relays():
                copy.wait_send()


def row_gather_sems(dp_size):
    chips = dp_size // 2
    return [pltpu.SemaphoreType.DMA((n,)) for n in (dp_size, chips, chips, chips)]


def group_gather_sems(mp_size):
    return [pltpu.SemaphoreType.DMA((max(4, mp_size - 1),)), pltpu.SemaphoreType.DMA((mp_size, 2))]


def gelu_pair(v):
    k0, k1 = 0.7978845608028654, 0.044715
    square = v * v
    t = jnp.tanh(k0 * (v + k1 * v * square))
    half = 0.5 * (1.0 + t)
    slope = half + 0.5 * v * (1.0 - t * t) * (k0 + 3.0 * k0 * k1 * square)
    return v * half, slope


def up_kernel(
    dp_size,
    mp_size,
    tokens,
    gain,
    shift,
    cot,
    up_master,
    up_bias,
    qkv_bias,
    qkv_low,
    dense_low,
    x_out,
    cot_out,
    up_out,
    hidden_out,
    slope_out,
    qkv_out,
    dense_out,
    projected_out,
    x_all,
    up_all,
    acc,
    hidden,
    slope,
    *sems,
):
    chips = dp_size // 2
    row_sems, x_sems, cot_sems = sems[0:4], sems[4:6], sems[6:8]
    out_sem = sems[8]
    qkv_gather = RowGather(chips, qkv_low, qkv_out, sems[9:13])
    dense_gather = RowGather(chips, dense_low, dense_out, sems[13:17])
    me, z, c, mp = place()
    rows = tokens.shape[0]
    length = rows * mp_size
    depth, width = up_all.shape[1], up_all.shape[2]

    values = tokens[...].astype(F32)
    centre = values - jnp.mean(values, axis=-1, keepdims=True)
    spread = jnp.mean(centre * centre, axis=-1, keepdims=True)
    x_all[mp] = (centre * lax.rsqrt(spread + EPSILON) * gain[...] + shift[...]).astype(BF)
    up_all[me] = up_master[...].astype(BF)

    greet(chips, mp_size)
    weights = RowGather(chips, up_all.at[me], up_all, row_sems)
    x_gather = GroupGather(mp_size, x_all.at[mp], x_all, x_sems)
    cot_gather = GroupGather(mp_size, cot, cot_out, cot_sems)
    x_gather.start()
    weights.start()
    own_cot = pltpu.make_async_copy(cot, cot_out.at[mp], out_sem.at[0])
    own_cot.start()
    own_blocks = [
        pltpu.make_async_copy(qkv_low, qkv_out.at[me], out_sem.at[5]),
        pltpu.make_async_copy(dense_low, dense_out.at[me], out_sem.at[6]),
    ]
    for copy in own_blocks:
        copy.start()

    def product(oz, first=False):
        cols = pl.ds(pl.multiple_of(oz * (2 * depth), 2 * depth), 2 * depth)

        def tile(i, carry):
            r, n = i // (width // 512), lax.rem(i, width // 512)
            n0 = pl.ds(pl.multiple_of(n * 512, 512), 512)
            left = x_all[r, :, cols]
            right = up_all[pl.ds(2 * oz, 2), :, n0].reshape(2 * depth, 512)
            term = dot(left, right)
            if first:
                acc[r, :, n0] = term + up_bias[:, n0]
            else:
                acc[r, :, n0] += term
            return carry

        lax.fori_loop(0, mp_size * (width // 512), tile, 0)

    x_gather.relay()
    weights.stage(1)
    x_gather.finish()
    cot_gather.start()
    x_copy = pltpu.make_async_copy(x_all, x_out, out_sem.at[1])
    x_copy.start()
    weights.wait_block(2 * z + 1 - c)
    product(z, True)
    for k in range(1, chips):
        if k > 1:
            weights.stage(k)
        if k == min(2, chips - 1):
            qkv_gather.start()
        for oz, valid in ((z + k, z + k < chips), (z - k, z - k >= 0)):

            @pl.when(valid)
            def _():
                weights.wait_block(2 * oz + 1 - c)
                product(oz)

        if k == min(2, chips - 1):
            cot_gather.relay()
    up_copy = pltpu.make_async_copy(up_all, up_out, out_sem.at[2])
    up_copy.start()
    qkv_gather.stage(1)
    dense_gather.start()

    def finish(i, carry):
        r, n = i // (width // 512), lax.rem(i, width // 512)
        n0 = pl.ds(pl.multiple_of(n * 512, 512), 512)
        high, grad = gelu_pair(acc[r, :, n0])
        hidden[r, :, n0] = high.astype(BF)
        slope[r, :, n0] = grad.astype(BF)
        return carry

    lax.fori_loop(0, mp_size * (width // 512), finish, 0)
    hidden_copy = pltpu.make_async_copy(hidden, hidden_out, out_sem.at[3])
    slope_copy = pltpu.make_async_copy(slope, slope_out, out_sem.at[4])
    hidden_copy.start()
    slope_copy.start()
    weights.drain()
    up_copy.wait()
    own_blocks[0].wait()
    thirds = qkv_low.shape[1]
    part = 512 if thirds % 512 == 0 else 256

    def project(oz, begins=False):
        qkv_gather.wait_block(2 * oz + 1 - c)
        pair = pl.ds(2 * oz, 2)
        load = pltpu.make_async_copy(
            qkv_out.at[pair], up_all.at[pair, :, pl.ds(0, thirds)], out_sem.at[5]
        )
        load.start()
        load.wait()
        cols = pl.ds(pl.multiple_of(oz * (2 * depth), 2 * depth), 2 * depth)

        def tile(i, carry):
            r, n = i // (thirds // part), lax.rem(i, thirds // part)
            n0 = pl.ds(pl.multiple_of(n * part, part), part)
            term = dot(x_all[r, :, cols], up_all[pair, :, n0].reshape(2 * depth, part))
            if begins:
                acc[r, :, n0] = term + qkv_bias[:, n0]
            else:
                acc[r, :, n0] += term
            return carry

        lax.fori_loop(0, mp_size * (thirds // part), tile, 0)

    project(z, True)
    for k in range(1, chips):
        if k > 1:
            qkv_gather.stage(k)
            dense_gather.stage(k - 1)
        def side(i, carry):
            oz = jnp.where(i == 0, z + k, z - k)

            @pl.when((oz >= 0) & (oz < chips))
            def _():
                project(oz)

            return carry

        lax.fori_loop(0, 2, side, 0)

    projected_copy = pltpu.make_async_copy(acc.at[:, :, pl.ds(0, thirds)], projected_out, out_sem.at[2])
    projected_copy.start()
    dense_gather.stage(chips - 1)
    for oz in range(chips):
        dense_gather.wait_block(2 * oz + 1 - c)
    qkv_gather.drain()
    dense_gather.drain()
    cot_gather.finish()
    x_gather.drain()
    cot_gather.drain()
    for copy in (own_cot, x_copy, projected_copy, hidden_copy, slope_copy, own_blocks[1]):
        copy.wait()


def up_stage(dp_size, mp_size, tokens, gain, shift, cot, up_master, up_bias, qkv_bias, qkv_low, dense_low):
    rows, model = tokens.shape
    depth, width = up_master.shape
    shape = jax.ShapeDtypeStruct
    outs = (
        shape((mp_size, rows, model), BF),
        shape((mp_size, rows, model), BF),
        shape((dp_size, depth, width), BF),
        shape((mp_size, rows, width), BF),
        shape((mp_size, rows, width), BF),
        shape((dp_size, *qkv_low.shape), BF),
        shape((dp_size, *dense_low.shape), BF),
        shape((mp_size, rows, qkv_low.shape[1]), F32),
    )
    return pl.pallas_call(
        partial(up_kernel, dp_size, mp_size),
        out_shape=outs,
        in_specs=[VM] * 7 + [ANY] * 2,
        out_specs=[ANY] * 8,
        scratch_shapes=[
            pltpu.VMEM((mp_size, rows, model), BF),
            pltpu.VMEM((dp_size, depth, width), BF),
            pltpu.VMEM((mp_size, rows, width), F32),
            pltpu.VMEM((mp_size, rows, width), BF),
            pltpu.VMEM((mp_size, rows, width), BF),
            *row_gather_sems(dp_size),
            *group_gather_sems(mp_size),
            *group_gather_sems(mp_size),
            pltpu.SemaphoreType.DMA((7,)),
            *row_gather_sems(dp_size),
            *row_gather_sems(dp_size),
        ],
        compiler_params=pltpu.CompilerParams(
            collective_id=1, has_side_effects=True, vmem_limit_bytes=58 << 20
        ),
        name="up_stage",
    )(tokens, gain.reshape(1, -1), shift.reshape(1, -1), cot, up_master, up_bias.reshape(1, -1), qkv_bias, qkv_low, dense_low)


def attention_kernel(
    dp_size,
    mp_size,
    pairs,
    bias,
    q_in,
    k_in,
    v_in,
    out_grad,
    rot,
    cot_all,
    hidden,
    down_low,
    out,
    q_grad,
    k_grad,
    v_grad,
    q_sum,
    k_sum,
    v_sum,
    down_share,
    down_full,
    k_acc,
    v_acc,
    flip,
    give,
    own_sem,
    *scratch,
):
    length = q_in.shape[0]
    block = 256
    blocks = length // block

    chips = dp_size // 2
    me, z, c, mp = place()
    down = RowScatter(chips, cot_all, (hidden,), flip, give, *scratch[:2], scratch[2:7])
    gather = RowGather(chips, down_low, down_full, scratch[7:])
    own_block = pltpu.make_async_copy(down_low, down_full.at[me], own_sem)

    @pl.when(pl.program_id(0) == 0)
    def _():
        greet(chips, mp_size)
        gather.start()
        own_block.start()
        down.swap()
        down.collect()

    def turn(values, sign):
        return (
            values * rot[0]
            + sign * (pltpu.roll(values, 128 - ROT_DIM // 2, 1) * rot[1] + pltpu.roll(values, ROT_DIM // 2, 1) * rot[2])
        )

    scale = HEAD_DIM ** (-0.5)
    q_low = (turn(q_in[...], 1.0).astype(BF).astype(F32) * scale).astype(BF)
    k_low = turn(k_in[...], 1.0).astype(BF)
    v_low = v_in[...].astype(BF)
    grad = out_grad[...]
    k_flip, v_flip = k_low.T, v_low.T
    lane = lax.broadcasted_iota(jnp.int32, (length, 128), 1) < HEAD_DIM
    row = lax.broadcasted_iota(jnp.int32, (128, length), 0) < HEAD_DIM
    zero = jnp.zeros((), BF)
    k_acc[...] = jnp.zeros_like(k_acc)
    v_acc[...] = jnp.zeros_like(v_acc)
    heads = []
    for h in range(2):
        lanes, rows = (lane, row) if h == 0 else (~lane, ~row)
        heads.append(
            (
                jnp.where(lanes, q_low, zero),
                jnp.where(lanes, k_low, zero),
                jnp.where(lanes, v_low, zero),
                jnp.where(lanes, grad, zero),
                jnp.where(rows, k_flip, zero),
                jnp.where(rows, v_flip, zero),
            )
        )
    for i in range(blocks):
        here = slice(block * i, block * (i + 1))
        stop = min(length, block * (i + 2))
        parts = [(0, block * i)] if i else []
        parts.append((block * i, stop))
        out_flip = jnp.zeros((128, block), F32)
        q_flip = jnp.zeros((128, block), F32)
        for q_h, k_h, v_h, grad_h, kt_h, vt_h in heads:
            scores = [dot(k_h[a:b], q_low[here], 1, 1) for a, b in parts]
            scores[-1] = scores[-1] + bias[i, : stop - block * i]
            top = scores[-1].max(0, keepdims=True)
            for s in scores[:-1]:
                top = jnp.maximum(top, s.max(0, keepdims=True))
            expo = [jnp.exp(s - top) for s in scores]
            total = expo[0].sum(0, keepdims=True)
            for e in expo[1:]:
                total = total + e.sum(0, keepdims=True)
            share = 1.0 / total
            probs = [e * share for e in expo]
            grads = [dot(v_h[a:b], grad[here], 1, 1) for a, b in parts]
            inner = (probs[0] * grads[0]).sum(0, keepdims=True)
            for p, g in zip(probs[1:], grads[1:]):
                inner = inner + (p * g).sum(0, keepdims=True)
            for (a, b), p, g in zip(parts, probs, grads):
                p_low = p.astype(BF)
                s_grad = (p * (g - inner)).astype(BF)
                out_flip = out_flip + dot(vt_h[:, a:b], p_low)
                q_flip = q_flip + dot(kt_h[:, a:b], s_grad)
                v_acc[a:b] += dot(p_low, grad_h[here])
                k_acc[a:b] += dot(s_grad, q_h[here])
        out[here] = out_flip.T.astype(BF)
        q_rows = q_flip.T * scale
        q_back = (
            q_rows * rot[0, here]
            - pltpu.roll(q_rows, 128 - ROT_DIM // 2, 1) * rot[1, here]
            - pltpu.roll(q_rows, ROT_DIM // 2, 1) * rot[2, here]
        )
        q_grad[here] = q_back.astype(BF)
    k_grad[...] = turn(k_acc[...], -1.0).astype(BF)
    v_grad[...] = v_acc[...].astype(BF)
    for total_out, rows_out in ((q_sum, q_grad), (k_sum, k_grad), (v_sum, v_grad)):
        total_out[...] = jnp.sum(rows_out[...].astype(F32), axis=0, keepdims=True)
    for i in range(pairs):

        @pl.when(pl.program_id(0) == i)
        def _():
            for s in range(chips - 1):
                if min(s, pairs - 1) == i:
                    gather.stage(s + 1)
                    if s > 0:
                        down.relay(s)
            if i == pairs - 1:
                down.finish(down_share)
                for oz in range(chips):
                    gather.wait_block(2 * oz + 1 - c)
                own_block.wait()
                down.drain_swap()
                down.drain()
                gather.drain()


def mask_bias(start, length):
    block = 256
    parts = []
    for i in range(length // block):
        keys = block * i + lax.broadcasted_iota(jnp.int32, (2 * block, block), 0)
        places = block * i + lax.broadcasted_iota(jnp.int32, (2 * block, block), 1)
        inside = (keys >= start) & (keys < start + PIECE) & (places >= start) & (places < start + PIECE)
        parts.append(jnp.where((keys <= places) | inside, 0.0, NEGATIVE))
    return jnp.stack(parts)


def rotary_lanes(length):
    half_dim = ROT_DIM // 2
    lane = jnp.arange(128) % HEAD_DIM
    frequency = 10000.0 ** (-jnp.arange(half_dim).astype(F32) * 2.0 / ROT_DIM)
    angles = jnp.arange(length).astype(F32)[:, None] * frequency[None, :]
    cosine = jnp.tile(jnp.cos(angles), (1, 128 // half_dim))
    sine = jnp.tile(jnp.sin(angles), (1, 128 // half_dim))
    turned = lane[None, :] < ROT_DIM
    first = lane[None, :] < half_dim
    return jnp.stack(
        [
            jnp.where(turned, cosine, 1.0),
            jnp.where(first, -sine, 0.0),
            jnp.where(turned & ~first, sine, 0.0),
        ]
    )


def attention(dp_size, mp_size, projected, out_grad, start, cot_all, hidden, down_low):
    length, width = out_grad.shape
    pairs, chips = width // 128, dp_size // 2
    depth, inner = down_low.shape
    shape = jax.ShapeDtypeStruct

    def rows(shift):
        return pl.BlockSpec((length, 128), lambda i: (0, i + shift))

    def whole(*dims):
        return pl.BlockSpec(dims, lambda i: (0,) * len(dims), pipeline_mode=pl.Buffered(1))

    total = pl.BlockSpec((1, 128), lambda i: (0, i))
    return pl.pallas_call(
        partial(attention_kernel, dp_size, mp_size, pairs),
        grid=(pairs,),
        in_specs=[
            whole(length // 256, 512, 256),
            rows(0),
            rows(pairs),
            rows(2 * pairs),
            rows(0),
            whole(3, length, 128),
            whole(*cot_all.shape),
            whole(*hidden.shape),
            ANY,
        ],
        out_specs=[rows(0)] * 4 + [total] * 3 + [pl.BlockSpec((depth, inner), lambda i: (0, 0)), ANY],
        out_shape=[shape((length, width), BF)] * 4
        + [shape((1, width), F32)] * 3
        + [shape((depth, inner), F32), shape((dp_size, depth, inner), BF)],
        scratch_shapes=[
            pltpu.VMEM((length, 128), F32),
            pltpu.VMEM((length, 128), F32),
            pltpu.VMEM((depth, length), BF),
            pltpu.VMEM((chips, depth, inner), BF),
            pltpu.SemaphoreType.DMA,
            *row_scatter_scratch(chips, depth, inner),
            *row_gather_sems(dp_size),
        ],
        compiler_params=pltpu.CompilerParams(
            collective_id=4, has_side_effects=True, vmem_limit_bytes=62 << 20
        ),
        cost_estimate=pl.CostEstimate(
            flops=16 * length * length * width + 2 * length * cot_all.shape[1] * inner,
            bytes_accessed=16 * length * width,
            transcendentals=length * length * width // 64,
        ),
        name="attention",
    )(
        mask_bias(start[0], length),
        projected,
        projected,
        projected,
        out_grad,
        rotary_lanes(length),
        cot_all,
        hidden,
        down_low,
    )


def flat(ref, cols):
    values = ref[..., cols]
    return values.reshape(-1, values.shape[-1])


class RowScatter:
    pieces = 2

    def __init__(self, chips, left, rights, flip, give, part, land, sems):
        self.chips, self.left, self.rights, self.flip = chips, left, rights, flip
        self.give, self.part, self.land = give, part, land
        self.sib_send, self.sib_recv, self.send_l, self.send_r, self.recv = sems
        self.depth = part.shape[1]

    def target(self, p):
        me, z, c, mp = place()
        s, side = p // 2, lax.rem(p, 2)
        far = self.chips - 1
        t = jnp.where(side == 0, z + s - far, z - s + far)
        return t, (t >= 0) & (t < self.chips)

    def block(self, t, core, store):
        b = 2 * t + core
        cols = pl.ds(pl.multiple_of(b * self.depth, self.depth), self.depth)
        self.flip[...] = flat(self.left, cols).T
        place_at = 0
        for right in self.rights:
            width = right.shape[-1]
            tile = min(512, width)
            for n in range(0, width, tile):
                product = dot(self.flip[...], flat(right, slice(n, n + tile)))
                store(slice(place_at + n, place_at + n + tile), product)
            place_at += width

    def sibling(self, t):
        me, z, c, mp = place()
        return remote(
            self.give.at[t], self.part.at[t], self.sib_send.at[t], self.sib_recv.at[t], 2 * z + 1 - c, mp
        )

    def rows(self, q):
        return pl.ds(q * (self.depth // self.pieces), self.depth // self.pieces)

    def to_left(self, t, q):
        me, z, c, mp = place()
        r = self.rows(q)
        return remote(
            self.part.at[t, r], self.land.at[t, r], self.send_l.at[t, q], self.recv.at[t, q], me - 2, mp
        )

    def to_right(self, t, q):
        me, z, c, mp = place()
        r = self.rows(q)
        slot = jnp.where(t > z + 1, t, self.chips)
        return remote(
            self.part.at[t, r], self.land.at[slot, r], self.send_r.at[t, q], self.recv.at[slot, q], me + 2, mp
        )

    def landed(self, slot, q):
        me, z, c, mp = place()
        here = self.land.at[slot, self.rows(q)]
        remote(here, here, self.send_l.at[0, 0], self.recv.at[slot, q], me, mp).wait_recv()

    def swap(self):
        me, z, c, mp = place()

        def step(p, carry):
            t, valid = self.target(p)

            @pl.when(valid)
            def _():
                def store(cols, values):
                    self.give[t, :, cols] = values.astype(BF)

                self.block(t, 1 - c, store)
                self.sibling(t).start()

            return carry

        lax.fori_loop(0, 2 * self.chips - 1, step, 0)

    def collect(self):
        me, z, c, mp = place()
        last = self.chips - 1

        def step(p, carry):
            t, valid = self.target(p)

            @pl.when(valid)
            def _():
                self.sibling(t).wait_recv()

                def store(cols, values):
                    self.part[t, :, cols] = (values + self.part[t, :, cols].astype(F32)).astype(BF)

                self.block(t, c, store)

                @pl.when((t < z) & (z == last))
                def _():
                    for q in range(self.pieces):
                        self.to_left(t, q).start()

                @pl.when((t > z) & (z == 0))
                def _():
                    for q in range(self.pieces):
                        self.to_right(t, q).start()

            return carry

        lax.fori_loop(0, 2 * self.chips - 1, step, 0)

    def add(self, t, slot, q):
        r = self.rows(q)
        self.landed(slot, q)
        self.part[t, r] = (self.part[t, r].astype(F32) + self.land[slot, r].astype(F32)).astype(BF)

    def relay(self, s):
        me, z, c, mp = place()
        last = self.chips - 1
        for q in range(self.pieces):
            t = z + s - last

            @pl.when((t >= 0) & (z < last))
            def _():
                self.add(t, t, q)
                self.to_left(t, q).start()

            u = z - s + last

            @pl.when((u <= last) & (z > 0))
            def _():
                self.add(u, u, q)
                self.to_right(u, q).start()

    def finish(self, result):
        me, z, c, mp = place()
        for q in range(self.pieces):
            r = self.rows(q)
            result[r] = self.part[z, r].astype(F32)

            @pl.when(z < self.chips - 1)
            def _():
                self.landed(z, q)
                result[r] += self.land[z, r].astype(F32)

            @pl.when(z > 0)
            def _():
                self.landed(self.chips, q)
                result[r] += self.land[self.chips, r].astype(F32)

    def drain_swap(self):
        def step(t, carry):
            self.sibling(t).wait_send()
            return carry

        lax.fori_loop(0, self.chips, step, 0)

    def drain(self):
        me, z, c, mp = place()

        def step(t, carry):
            for q in range(self.pieces):

                @pl.when(t < z)
                def _():
                    self.to_left(t, q).wait_send()

                @pl.when(t > z)
                def _():
                    self.to_right(t, q).wait_send()

            return carry

        lax.fori_loop(0, self.chips, step, 0)


def row_scatter_scratch(chips, depth, width):
    return [
        pltpu.VMEM((chips, depth, width), BF),
        pltpu.VMEM((chips + 1, depth, width), BF),
        pltpu.SemaphoreType.DMA((chips,)),
        pltpu.SemaphoreType.DMA((chips,)),
        pltpu.SemaphoreType.DMA((chips, RowScatter.pieces)),
        pltpu.SemaphoreType.DMA((chips, RowScatter.pieces)),
        pltpu.SemaphoreType.DMA((chips + 1, RowScatter.pieces)),
    ]


class GroupScatter:
    def __init__(self, size, blocks, parts, land, send, recv):
        self.size, self.blocks, self.parts, self.land, self.send, self.recv = size, blocks, parts, land, send, recv
        self.depth = parts.shape[2] // blocks

    def copy(self, k, j):
        me, z, c, mp = place()
        peer = lax.rem(mp + k, self.size)
        cols = pl.ds(pl.multiple_of(j * self.depth, self.depth), self.depth)
        return remote(
            self.parts.at[peer, :, cols],
            self.land.at[mp, :, cols],
            self.send.at[k, j],
            self.recv.at[mp, j],
            me,
            peer,
        )

    def start(self, j):
        for k in range(1, self.size):
            self.copy(k, j).start()

    def arrive(self):
        me, z, c, mp = place()

        def step(j, carry):
            cols = pl.ds(pl.multiple_of(j * self.depth, self.depth), self.depth)
            for k in range(1, self.size):
                origin = lax.rem(mp + k, self.size)
                here = self.land.at[origin, :, cols]
                remote(here, here, self.send.at[0, 0], self.recv.at[origin, j], me, origin).wait_recv()
            return carry

        lax.fori_loop(0, self.blocks, step, 0)

    def total(self, rows):
        me, z, c, mp = place()
        sums = self.parts[mp, rows].astype(F32)
        for k in range(1, self.size):
            sums = sums + self.land[lax.rem(mp + k, self.size), rows].astype(F32)
        return sums

    def drain(self):
        def step(j, carry):
            for k in range(1, self.size):
                self.copy(k, j).wait_send()
            return carry

        lax.fori_loop(0, self.blocks, step, 0)


def grad_kernel(
    dp_size,
    mp_size,
    x_all,
    pre_grad,
    attended,
    hidden_all,
    cot_all,
    qkv_full,
    up_full,
    dense_full,
    down_full,
    query_grad,
    key_grad,
    value_grad,
    query_sum,
    key_sum,
    value_sum,
    up_sum,
    tokens,
    cot,
    gain,
    out_bias,
    dense_share,
    qkv_share,
    up_share,
    output,
    input_grad,
    totals,
    x_buf,
    pre,
    mixed_buf,
    attended_buf,
    hidden_buf,
    wide_buf,
    thin_buf,
    flip,
    give,
    first,
    second,
    load_sem,
    stream_sem,
    *scratch,
):
    me, z, c, mp = place()
    chips = dp_size // 2
    rows, model = tokens.shape
    width, inner = query_grad.shape[1], up_sum.shape[1]
    depth = model // dp_size
    qkv_scratch, up_scratch, dense_scratch, rest = scratch[:7], scratch[7:14], scratch[14:21], scratch[21:]
    grads = (query_grad, key_grad, value_grad)
    give_qkv = give.at[:, :, pl.ds(0, 3 * width)]
    give_up = give.at[:, :, pl.ds(0, inner)]
    give_dense = give.at[:, :, pl.ds(0, width)]
    dense = RowScatter(
        chips, mixed_buf, (attended_buf,), flip, give_dense, *dense_scratch[:2], dense_scratch[2:]
    )
    qkv = RowScatter(chips, x_buf, grads, flip, give_qkv, *qkv_scratch[:2], qkv_scratch[2:])
    up = RowScatter(chips, x_buf, (pre,), flip, give_up, *up_scratch[:2], up_scratch[2:])
    normed_group = GroupScatter(mp_size, dp_size, x_buf, *rest[:3])
    mixed_group = GroupScatter(mp_size, dp_size, mixed_buf, *rest[3:6])
    send_1, recv_1, send_2, recv_2 = rest[6:]

    loads = [
        pltpu.make_async_copy(source, target, load_sem.at[n])
        for n, (source, target) in enumerate(
            (
                (cot_all, mixed_buf),
                (attended, attended_buf),
                (x_all, x_buf),
                (pre_grad, pre),
                (hidden_all, hidden_buf),
                (tokens, rest[0].at[mp]),
                (cot, rest[3].at[mp]),
            )
        )
    ]
    for load in loads:
        load.start()

    def stream(wide, thin):
        def copies(j):
            slot = lax.rem(j, 2)
            r = pl.ds(pl.multiple_of(j * depth, depth), depth)
            return (
                pltpu.make_async_copy(wide.at[r], wide_buf.at[slot], stream_sem.at[0, slot]),
                pltpu.make_async_copy(
                    thin.at[r], thin_buf.at[slot, :, pl.ds(0, thin.shape[1])], stream_sem.at[1, slot]
                ),
            )

        return copies

    normed_stream = stream(up_full, qkv_full)
    mixed_stream = stream(down_full, dense_full)

    def partial_sums(copies, wide, thins, target, group_out):
        half = mp_size // 2

        def step(j, carry):
            slot = lax.rem(j, 2)
            for copy in copies(j):
                copy.wait()

            @pl.when(j + 1 < dp_size)
            def _():
                for copy in copies(j + 1):
                    copy.start()

            cols = pl.ds(pl.multiple_of(j * depth, depth), depth)
            for h in range(2):
                group = pl.ds(h * half, half)
                left = wide[group].reshape(half * rows, inner)
                sums = dot(left, wide_buf[slot], 1, 1)
                for n, thin in enumerate(thins):
                    left = thin[pl.ds(h * half * rows, half * rows), :]
                    sums = sums + dot(left, thin_buf[slot, :, n * width : (n + 1) * width], 1, 1)
                target[group, :, cols] = sums.astype(BF).reshape(half, rows, depth)
            group_out.start(j)
            return carry

        lax.fori_loop(0, dp_size, step, 0)

    for copy in mixed_stream(0):
        copy.start()
    greet_all(dp_size, mp_size)
    loads[0].wait()
    loads[1].wait()
    dense.swap()
    dense.collect()
    dense.drain_swap()
    loads[2].wait()
    qkv.swap()
    qkv.collect()
    if chips > 2:
        dense.relay(1)
    loads[4].wait()
    partial_sums(mixed_stream, hidden_buf, (attended_buf,), mixed_buf, mixed_group)
    for copy in normed_stream(0):
        copy.start()
    for s in range(2, chips - 1):
        dense.relay(s)
    if chips > 2:
        qkv.relay(1)
    loads[3].wait()
    qkv.drain_swap()
    up.swap()
    up.collect()
    dense.finish(dense_share)
    partial_sums(normed_stream, pre, grads, x_buf, normed_group)
    for s in range(2, chips - 1):
        qkv.relay(s)
    if chips > 2:
        up.relay(1)
    qkv.finish(qkv_share)

    normed_group.arrive()
    loads[5].wait()
    loads[6].wait()
    tile = 64
    second[me] = jnp.zeros((8, model), F32)

    def norm_back(i, carry):
        r = pl.ds(pl.multiple_of(i * tile, tile), tile)
        values = rest[0][mp, r].astype(F32)
        centre = values - jnp.mean(values, axis=-1, keepdims=True)
        spread = jnp.mean(centre * centre, axis=-1, keepdims=True)
        inverse = lax.rsqrt(spread + EPSILON)
        xhat = centre * inverse
        normed_grad = normed_group.total(r)
        e = normed_grad * gain[...]
        turned = e - jnp.mean(e, axis=-1, keepdims=True) - xhat * jnp.mean(e * xhat, axis=-1, keepdims=True)
        cot_rows = rest[3][mp, r].astype(F32)
        input_grad[r] = (cot_rows + turned * inverse).astype(BF)
        second[me, 0:1] += jnp.sum(normed_grad * xhat, axis=0, keepdims=True)
        second[me, 1:2] += jnp.sum(normed_grad, axis=0, keepdims=True)
        second[me, 2:3] += jnp.sum(cot_rows, axis=0, keepdims=True)
        return carry

    lax.fori_loop(0, rows // tile, norm_back, 0)
    second[me, 3:4, :inner] = up_sum[...]
    for n, vector in enumerate((query_sum, key_sum, value_sum)):
        second[me, 4:5, n * width : (n + 1) * width] = vector[...]
    first[mp] = second[me]

    def copy_1(k):
        return remote(
            first.at[mp], first.at[mp], send_1.at[k], recv_1.at[mp], me, lax.rem(mp + k, mp_size)
        )

    def copy_2(k):
        return remote(
            second.at[me], second.at[me], send_2.at[k], recv_2.at[me], lax.rem(me + k, dp_size), mp
        )

    for k in range(1, mp_size):
        copy_1(k).start()
    for s in range(2, chips - 1):
        up.relay(s)
    mixed_group.arrive()

    def add_up(i, carry):
        r = pl.ds(pl.multiple_of(i * tile, tile), tile)
        output[r] = (rest[0][mp, r].astype(F32) + mixed_group.total(r) + out_bias[...]).astype(BF)
        return carry

    lax.fori_loop(0, rows // tile, add_up, 0)
    for k in range(1, mp_size):
        origin = lax.rem(mp + k, mp_size)
        remote(first.at[origin], first.at[origin], send_1.at[0], recv_1.at[origin], me, origin).wait_recv()
    total = first[0]
    for k in range(1, mp_size):
        total = total + first[k]
    second[me, 0:3] = total[0:3]
    for k in range(1, dp_size):
        copy_2(k).start()
    up.finish(up_share)
    for k in range(1, dp_size):
        origin = lax.rem(me + k, dp_size)
        remote(second.at[origin], second.at[origin], send_2.at[0], recv_2.at[origin], origin, mp).wait_recv()
    total = second[0]
    for k in range(1, dp_size):
        total = total + second[k]
    totals[...] = total
    for k in range(1, mp_size):
        copy_1(k).wait_send()
    for k in range(1, dp_size):
        copy_2(k).wait_send()
    up.drain_swap()
    for stream_out in (dense, qkv, up, normed_group, mixed_group):
        stream_out.drain()


def greet_all(dp_size, mp_size):
    me, z, c, mp = place()
    bar = pltpu.get_barrier_semaphore()
    for k in range(1, mp_size):
        pl.semaphore_signal(bar, 1, device_id=(me, lax.rem(mp + k, mp_size)), device_id_type=MESH)
    for k in range(1, dp_size):
        pl.semaphore_signal(bar, 1, device_id=(lax.rem(me + k, dp_size), mp), device_id_type=MESH)
    pl.semaphore_wait(bar, mp_size + dp_size - 2)


def grad_stage(dp_size, mp_size, hbm_args, grads, sums, tokens, cot, gain, out_bias):
    pre_grad = hbm_args[1]
    rows, model = tokens.shape
    length = rows * mp_size
    depth, chips = model // dp_size, dp_size // 2
    width, inner = grads[0].shape[1], pre_grad.shape[2]
    wide = max(3 * width, inner)
    shape = jax.ShapeDtypeStruct
    semaphores = pltpu.SemaphoreType.DMA
    blocks = (mp_size, dp_size)
    group = [pltpu.VMEM((mp_size, rows, model), BF), semaphores(blocks), semaphores(blocks)]
    return pl.pallas_call(
        partial(grad_kernel, dp_size, mp_size),
        out_shape=(
            shape((depth, width), F32),
            shape((depth, 3 * width), F32),
            shape((depth, inner), F32),
            shape((rows, model), BF),
            shape((rows, model), BF),
            shape((8, model), F32),
        ),
        in_specs=[ANY] * len(hbm_args) + [VM] * 7 + [ANY] * 2 + [VM] * 2,
        out_specs=[VM] * 6,
        scratch_shapes=[
            pltpu.VMEM((mp_size, rows, model), BF),
            pltpu.VMEM((mp_size, rows, inner), BF),
            pltpu.VMEM((mp_size, rows, model), BF),
            pltpu.VMEM((length, width), BF),
            pltpu.VMEM((mp_size, rows, inner), BF),
            pltpu.VMEM((2, depth, inner), BF),
            pltpu.VMEM((2, depth, 3 * width), BF),
            pltpu.VMEM((depth, length), BF),
            pltpu.VMEM((chips, depth, wide), BF),
            pltpu.VMEM((mp_size, 8, model), F32),
            pltpu.VMEM((dp_size, 8, model), F32),
            semaphores((7,)),
            semaphores((2, 2)),
            *row_scatter_scratch(chips, depth, 3 * width),
            *row_scatter_scratch(chips, depth, inner),
            *row_scatter_scratch(chips, depth, width),
            *group,
            *group,
            *[semaphores((n,)) for n in (mp_size, mp_size, dp_size, dp_size)],
        ],
        compiler_params=pltpu.CompilerParams(
            collective_id=3, has_side_effects=True, vmem_limit_bytes=67043328
        ),
        name="grad_stage",
    )(*hbm_args, *grads, *sums, tokens, cot, gain.reshape(1, -1), out_bias.reshape(1, -1))


def body(
    tokens,
    ln_gain,
    ln_bias,
    qkv_weight,
    qkv_bias,
    dense_weight,
    dense_bias,
    fc1_weight,
    fc1_bias,
    fc2_weight,
    fc2_bias,
    starts,
    cotangent,
):
    dp_size, mp_size = lax.axis_size("dp"), lax.axis_size("mp")
    x_all, cot_all, up_all, hidden_all, slope_all, qkv_all, dense_all, projected = up_stage(
        dp_size,
        mp_size,
        tokens,
        ln_gain,
        ln_bias,
        cotangent,
        fc1_weight,
        fc1_bias,
        qkv_bias.reshape(1, -1),
        qkv_weight.astype(BF).reshape(qkv_weight.shape[0], -1),
        dense_weight.astype(BF),
    )
    gathered = x_all.reshape(-1, x_all.shape[-1])
    out_rows = cot_all.reshape(gathered.shape)
    up_full = up_all.reshape(-1, up_all.shape[-1])
    hidden_low = hidden_all.reshape(-1, up_all.shape[-1])
    slope = slope_all.reshape(hidden_low.shape)
    qkv_full = qkv_all.reshape(-1, qkv_all.shape[-1])
    dense_full = dense_all.reshape(-1, dense_all.shape[-1])
    local_width = dense_full.shape[1]
    projected = projected.reshape(gathered.shape[0], -1)
    attended_grad = jnp.dot(out_rows, dense_full, preferred_element_type=jnp.float32).astype(
        jnp.bfloat16
    )
    attended, query_grad, key_grad, value_grad, query_sum, key_sum, value_sum, down_share, down_all = (
        attention(
            dp_size, mp_size, projected, attended_grad, starts, out_rows, hidden_low, fc2_weight.astype(BF)
        )
    )
    down_full = down_all.reshape(-1, down_all.shape[-1])
    hidden_grad = jnp.dot(out_rows, down_full, preferred_element_type=jnp.float32)
    pre_grad = (hidden_grad * slope).astype(jnp.bfloat16)
    up_bias_grad = jnp.sum(pre_grad.astype(jnp.float32), axis=0)
    dense_share, qkv_share, up_share, output, input_grad, totals = grad_stage(
        dp_size,
        mp_size,
        (
            x_all,
            pre_grad.reshape(hidden_all.shape),
            attended,
            hidden_all,
            cot_all,
            qkv_full,
            up_full,
            dense_full,
            down_full,
        ),
        (query_grad, key_grad, value_grad),
        (query_sum, key_sum, value_sum, up_bias_grad.reshape(1, -1)),
        tokens,
        cotangent,
        ln_gain,
        dense_bias + fc2_bias,
    )
    qkv_share = qkv_share.reshape(-1, 3, local_width)
    gain_total, shift_total, bias_total = totals[0], totals[1], totals[2]
    up_bias_total = totals[3, : up_full.shape[1]]
    qkv_bias_total = totals[4, : 3 * local_width].reshape(3, local_width)
    return (
        output,
        input_grad,
        gain_total,
        shift_total,
        qkv_share,
        qkv_bias_total,
        dense_share,
        bias_total,
        up_share,
        up_bias_total,
        down_share,
        bias_total,
    )


def solution(mesh):
    in_specs = (
        P(("dp", "mp"), None),
        P(),
        P(),
        P("dp", None, "mp"),
        P(None, "mp"),
        P("dp", "mp"),
        P(),
        P("dp", "mp"),
        P("mp"),
        P("dp", "mp"),
        P(),
        P("dp"),
        P(("dp", "mp"), None),
    )
    out_specs = (
        P(("dp", "mp"), None),
        P(("dp", "mp"), None),
        P(),
        P(),
        P("dp", None, "mp"),
        P(None, "mp"),
        P("dp", "mp"),
        P(),
        P("dp", "mp"),
        P("mp"),
        P("dp", "mp"),
        P(),
    )
    return jax.shard_map(body, mesh=mesh, in_specs=in_specs, out_specs=out_specs, check_vma=False)
```
